512 devices in a mesh: sec: 2 (over z_hi), gx: 16 (over z_lo, core), gy: 16 (over x, y).
Axes of the slice: x: 4, y: 4, z: 16 (z_hi: 2, z_lo: 8; z = z_hi * 8 + z_lo), core: 2. Of those that a mesh axis runs over, the one named last changes fastest.
Arguments:
- terminal: float32 [4, 16, 256, 4096], P('sec', None, 'gx', 'gy'), may hold values from -6 to 6
- forward_temp: bfloat16 [2, 4, 16, 256, 4096], P(None, 'sec', None, 'gx', 'gy'), may hold values from -6 to 6
- conductivity: float32 [16, 256, 4096], P(None, 'gx', 'gy'), may hold values from 0.02 to 0.15
- velocity: float32 [2, 16, 256, 4096], P(None, None, 'gx', 'gy'), may hold values from -0.3 to 0.3
- fixed_mask: int32 [16, 256, 4096], P(None, 'gx', 'gy'), may hold values 0 or 1
- wells: int32 [4, 8, 3], P('sec'), may hold values from 0 to 4095, as said below
- misfit: float32 [2, 4, 8], P(None, 'sec'), may hold values from -12 to 12
- head_gradient: bfloat16 [2, 16, 256, 4096], P('sec', None, 'gx', 'gy'), may hold values from -6 to 6
- blocks: bfloat16 [32, 7, 128, 128], P('gy'), may hold values from -0.1875 to 0.1875
- block_cols: int32 [32, 7], P('gy'), may hold values from 0 to 31, as said below
Outputs:
- head_adjoint: float32 [2, 16, 256, 4096], P('sec', None, 'gx', 'gy')
- sensitivity: float32 [16, 256, 4096], P(None, 'gx', 'gy')
The draws below stay inside these ranges and needn't reach their ends.
Inputs may be any that keep to these rules, and one draw needn't show every extreme that they name: `wells`: each row is one cell (z, x, y) with z < 16, x < 256, y < 4096; the first test observes the cells (0, 0, 0) and (15, 255, 4095). `block_cols`: row r lists 7 different block columns, the first of which is r.
All inputs are finite; a program needn't handle non-finite values. No bound on the sum of `fixed_mask` on one device may be relied on, other than what follows from the above.
Results may differ from the reference program's by a relative error of at most 0.0029.
Values may be sent and summed in bfloat16 or wider, within the bound.
No kernel may reach another device: no remote copies, remote signals or barrier semaphores. Data moves between devices by JAX's collectives and lax.ppermute only.
A program may use at most 64 MiB of HBM per device.

```python
import math
import jax
import jax.numpy as jnp
from jax import lax

NZ = 16
BLOCK = 128
NNZB = 7
TESTS = 4
STEPS = 2
WELLS = 8
NX = 256
NY = 4096
NBY = 32


def draw_wells(key, part):
    key_z, key_x, key_y = jax.random.split(jax.random.fold_in(key, 11), 3)
    coord_z = jax.random.randint(key_z, (TESTS, WELLS, 1), 0, NZ, dtype=jnp.int32)
    coord_x = jax.random.randint(key_x, (TESTS, WELLS, 1), 0, NX, dtype=jnp.int32)
    coord_y = jax.random.randint(key_y, (TESTS, WELLS, 1), 0, NY, dtype=jnp.int32)
    cells = jnp.concatenate([coord_z, coord_x, coord_y], axis=2).astype(jnp.int32)
    cells = cells.at[0, 0, :].set(jnp.zeros((3,), jnp.int32))
    corner = jnp.array([NZ - 1, NX - 1, NY - 1], dtype=jnp.int32)
    cells = cells.at[0, 1, :].set(corner)
    return cells.astype(jnp.int32)


def draw_block_cols(key, part):
    scores = jax.random.randint(jax.random.fold_in(key, 23), (NBY, NBY), 0, 2 ** 20, dtype=jnp.int32)
    scores = scores * NBY + jnp.arange(NBY, dtype=jnp.int32)[None, :]
    scores = jnp.where(jnp.eye(NBY, dtype=bool), -1, scores)
    order = jnp.argsort(scores, axis=1)
    return order[:, :NNZB].astype(jnp.int32)


def plant(drawn, rng, smallest, top_value):
    shape = drawn.shape
    place = [jax.random.randint(jax.random.fold_in(rng, axis), (), 0, shape[axis]) for axis in range(len(shape))]
    drawn = drawn.at[tuple(place)].set(smallest)
    longest = shape.index(max(shape))
    place[longest] = (place[longest] + 1) % shape[longest]
    return drawn.at[tuple(place)].set(top_value)


def shard_levels(rng, extent, cuts, smallest, largest):
    level, own = 1.0, jax.random.fold_in(rng, 6)
    for axis_at, blocks in cuts:
        steps = jnp.exp(jax.random.uniform(jax.random.fold_in(own, axis_at), (blocks,), jnp.float32, smallest / len(cuts), largest / len(cuts)))
        level = level * jnp.repeat(steps, extent[axis_at] // blocks).reshape([-1 if axis == axis_at else 1 for axis in range(len(extent))])
    return level


def normal_values(key, extent, width, bound, cuts=(), held_as=jnp.bfloat16):
    entries = jax.random.normal(key, extent, jnp.float32) * width
    if len(cuts) > 0:
        entries = shard_levels(key, extent, cuts, -0.22, 0.18) * entries
    return jnp.clip(entries, min=-bound, max=bound).astype(held_as)


def setup_inputs(seed: int = 0) -> dict:
    splits = jax.random.split(jax.random.key(seed), 11)
    return {
        "terminal": normal_values(splits[0], (TESTS, NZ, NX, NY), 1.0, 6.0, ((0, 2), (2, 16), (3, 16)), jnp.float32),
        "forward_temp": normal_values(splits[1], (STEPS, TESTS, NZ, NX, NY), 1.0, 6.0, ((1, 2), (3, 16), (4, 16))),
        "conductivity": jnp.clip(jnp.exp(math.log(0.15) - 2.014903 * jax.random.uniform(splits[2], (NZ, NX, NY), jnp.float32) ** shard_levels(splits[2], (NZ, NX, NY), ((1, 16), (2, 16)), -0.2, 0.2)), 0.02, 0.15),
        "velocity": jnp.clip(jax.random.uniform(splits[3], (2, NZ, NX, NY), jnp.float32, -0.3, 0.3) * shard_levels(splits[3], (2, NZ, NX, NY), ((2, 16), (3, 16)), -0.4, 0.0), -0.3, 0.3),
        "fixed_mask": plant((jax.random.randint(splits[4], (NZ, NX, NY), 0, 8) < 1).astype(jnp.int32), jax.random.fold_in(splits[4], 1), 0, 1),
        "wells": draw_wells(jax.random.fold_in(splits[10], 71), 0),
        "misfit": normal_values(splits[6], (STEPS, TESTS, WELLS), 3.0, 12.0, ((1, 2),), jnp.float32),
        "head_gradient": normal_values(splits[7], (2, NZ, NX, NY), 1.0, 6.0, ((0, 2), (2, 16), (3, 16))),
        "blocks": normal_values(splits[8], (NBY, NNZB, BLOCK, BLOCK), (NNZB * BLOCK) ** -0.5, 0.1875, ((0, 16),)),
        "block_cols": draw_block_cols(jax.random.fold_in(splits[10], 71), 0),
    }


def shifted(padded):
    lead = [(0, 0)] * (padded.ndim - 3)
    deeper = jnp.pad(padded, lead + [(1, 1), (0, 0), (0, 0)])
    centre = deeper[..., 1:-1, 1:-1, 1:-1]
    beside_all = [deeper[..., 2:, 1:-1, 1:-1], deeper[..., :-2, 1:-1, 1:-1],
              deeper[..., 1:-1, 2:, 1:-1], deeper[..., 1:-1, :-2, 1:-1],
              deeper[..., 1:-1, 1:-1, 2:], deeper[..., 1:-1, 1:-1, :-2]]
    return centre, beside_all


def face_weights(kappa_pad):
    centre, beside_all = shifted(kappa_pad)
    return [2.0 * centre * other / jnp.where(centre + other > 0.0, centre + other, 1.0) for other in beside_all]


def advance(adjoint_pad, weights, keep, speed_x, speed_y, source):
    centre, beside_all = shifted(adjoint_pad)
    diffusion = weights[0] * (beside_all[0] - centre)
    for face in range(1, 6):
        diffusion = diffusion + weights[face] * (beside_all[face] - centre)
    slope_x = 0.5 * (beside_all[2] - beside_all[3])
    slope_y = 0.5 * (beside_all[4] - beside_all[5])
    updated = keep * (centre + diffusion + speed_x * slope_x + speed_y * slope_y + source)
    return updated, diffusion, slope_x, slope_y


def reference(terminal, forward_temp, conductivity, velocity, fixed_mask, wells, misfit, head_gradient, blocks, block_cols):
    keep = 1.0 - fixed_mask.astype(jnp.float32)
    weights = face_weights(jnp.pad(conductivity, ((0, 0), (1, 1), (1, 1))))
    heat_sens = jnp.zeros((NZ, NX, NY), jnp.float32)
    flow_x = jnp.zeros((NZ, NX, NY), jnp.float32)
    flow_y = jnp.zeros((NZ, NX, NY), jnp.float32)
    for test in range(TESTS):
        adjoint = terminal[test]
        for level in reversed(range(STEPS)):
            source = jnp.zeros((NZ, NX, NY), jnp.float32).at[wells[test, :, 0], wells[test, :, 1], wells[test, :, 2]].add(misfit[level, test])
            padded = jnp.pad(adjoint, ((0, 0), (1, 1), (1, 1)))
            adjoint, diffusion, slope_x, slope_y = advance(padded, weights, keep, velocity[0], velocity[1], source)
            temper = forward_temp[level, test].astype(jnp.float32)
            heat_sens = heat_sens + temper * diffusion
            flow_x = flow_x + temper * slope_x
            flow_y = flow_y + temper * slope_y
    rounded = jnp.stack([flow_x, flow_y]).astype(jnp.bfloat16)
    heads = []
    for comp in range(2):
        flat = rounded[comp].reshape(NZ * NX, NBY, BLOCK)

        def one_row(index):
            chosen = jnp.take(flat, block_cols[index], axis=1).astype(jnp.float32)
            return jnp.einsum('rkj,kij->ri', chosen, blocks[index].astype(jnp.float32), precision=lax.Precision.HIGHEST)

        per_row = lax.map(one_row, jnp.arange(NBY, dtype=jnp.int32))
        heads.append(jnp.transpose(per_row, (1, 0, 2)).reshape(NZ, NX, NY))
    head_adjoint = jnp.stack(heads)
    sensitivity = heat_sens + head_adjoint[0] * head_gradient[0].astype(jnp.float32) + head_adjoint[1] * head_gradient[1].astype(jnp.float32)
    return head_adjoint, sensitivity
```

```python
import jax
import jax.numpy as jnp
from jax import lax
from jax.sharding import PartitionSpec as P


def extended(cells, sides, width):
    for axis, dim in sides:
        count = lax.axis_size(axis)
        ends = count - 1
        head = lax.slice_in_dim(cells, 0, width, axis=dim)
        tail = lax.slice_in_dim(cells, cells.shape[dim] - width, cells.shape[dim], axis=dim)
        cells = jnp.concatenate(
            [
                lax.ppermute(tail, axis, [(i, (i + 1) % count) for i in range(ends)]),
                cells,
                lax.ppermute(head, axis, [((i + 1) % count, i) for i in range(ends)]),
            ],
            axis=dim,
        )
    return cells


def shifted(padded):
    lead = [(0, 0)] * (padded.ndim - 3)
    deeper = jnp.pad(padded, lead + [(1, 1), (0, 0), (0, 0)])
    centre = deeper[..., 1:-1, 1:-1, 1:-1]
    beside_all = [
        deeper[..., 2:, 1:-1, 1:-1],
        deeper[..., :-2, 1:-1, 1:-1],
        deeper[..., 1:-1, 2:, 1:-1],
        deeper[..., 1:-1, :-2, 1:-1],
        deeper[..., 1:-1, 1:-1, 2:],
        deeper[..., 1:-1, 1:-1, :-2],
    ]
    return (centre, beside_all)


def face_weights(kappa_pad):
    centre, beside_all = shifted(kappa_pad)
    return [
        2.0 * centre * other / jnp.where(centre + other > 0.0, centre + other, 1.0)
        for other in beside_all
    ]


def advance(adjoint_pad, weights, keep, speed_x, speed_y, source):
    centre, beside_all = shifted(adjoint_pad)
    diffusion = weights[0] * (beside_all[0] - centre)
    for face in range(1, 6):
        diffusion = diffusion + weights[face] * (beside_all[face] - centre)
    slope_x = 0.5 * (beside_all[2] - beside_all[3])
    slope_y = 0.5 * (beside_all[4] - beside_all[5])
    updated = keep * (centre + diffusion + speed_x * slope_x + speed_y * slope_y + source)
    return (updated, diffusion, slope_x, slope_y)


def well_sources(wells, misfit_level, layers, rows_x, cols_y, margin):
    start_x = lax.axis_index("gx") * rows_x - margin
    start_y = lax.axis_index("gy") * cols_y - margin
    coord_z = jnp.arange(layers, dtype=jnp.int32)[:, None, None]
    coord_x = (start_x + jnp.arange(rows_x + 2 * margin, dtype=jnp.int32))[None, :, None]
    coord_y = (start_y + jnp.arange(cols_y + 2 * margin, dtype=jnp.int32))[None, None, :]
    well_z = wells[:, :, 0][:, :, None, None, None]
    well_x = wells[:, :, 1][:, :, None, None, None]
    well_y = wells[:, :, 2][:, :, None, None, None]
    matches = (coord_z == well_z) & (coord_x == well_x) & (coord_y == well_y)
    return jnp.sum(jnp.where(matches, misfit_level[:, :, None, None, None], 0.0), axis=1)


def shards(
    terminal,
    forward_temp,
    conductivity,
    velocity,
    fixed_mask,
    wells,
    misfit,
    head_gradient,
    blocks,
    block_cols,
):
    layers, rows_x, cols_y = conductivity.shape
    steps = forward_temp.shape[0]
    keep = 1.0 - fixed_mask.astype(jnp.float32)
    heat_sens = jnp.zeros((layers, rows_x, cols_y), jnp.float32)
    flow_x = jnp.zeros((layers, rows_x, cols_y), jnp.float32)
    flow_y = jnp.zeros((layers, rows_x, cols_y), jnp.float32)
    kappa_pad = extended(conductivity, (("gx", 1), ("gy", 2)), 1)
    weights = face_weights(kappa_pad)
    adjoint = terminal
    for level in reversed(range(steps)):
        padded = extended(adjoint, (("gx", 2), ("gy", 3)), 1)
        source = well_sources(wells, misfit[level], layers, rows_x, cols_y, 0)
        adjoint, diffusion, slope_x, slope_y = advance(
            padded, weights, keep, velocity[0], velocity[1], source
        )
        temper = forward_temp[level].astype(jnp.float32)
        heat_sens = heat_sens + jnp.sum(temper * diffusion, axis=0)
        flow_x = flow_x + jnp.sum(temper * slope_x, axis=0)
        flow_y = flow_y + jnp.sum(temper * slope_y, axis=0)
    first = lax.axis_index("sec") == 0
    mine = jnp.where(first, flow_x, flow_y)
    other = jnp.where(first, flow_y, flow_x)
    partner = [(0, 1), (1, 0)]
    rounded = (mine + lax.ppermute(other, "sec", partner)).astype(jnp.bfloat16)
    row_blocks, per_row, block_size, _ = blocks.shape
    piece = lax.all_gather(rounded, "gy", axis=2, tiled=True)
    count = piece.shape[2] // block_size
    split_rows = piece.reshape(layers, rows_x, count, block_size)
    block_ids = jnp.arange(count, dtype=jnp.int32)
    chosen = (block_cols[:, :, None] == block_ids[None, None, :]).astype(jnp.bfloat16)
    portion = jnp.einsum("bkq,zxqj->bkzxj", chosen, split_rows, preferred_element_type=jnp.float32)
    picked = portion.astype(jnp.bfloat16)
    head = jnp.einsum(
        "bkzxj,bkij->zxbi", picked, blocks, preferred_element_type=jnp.float32
    ).reshape(layers, rows_x, cols_y)
    partial_sens = heat_sens + head * head_gradient[0].astype(jnp.float32)
    sensitivity = partial_sens + lax.ppermute(partial_sens, "sec", partner)
    return (head[None], sensitivity)


def solution(mesh):
    placed = (
        P("sec", None, "gx", "gy"),
        P(None, "sec", None, "gx", "gy"),
        P(None, "gx", "gy"),
        P(None, None, "gx", "gy"),
        P(None, "gx", "gy"),
        P("sec", None, None),
        P(None, "sec", None),
        P("sec", None, "gx", "gy"),
        P("gy", None, None, None),
        P("gy", None),
    )
    return jax.shard_map(
        shards,
        mesh=mesh,
        in_specs=placed,
        out_specs=(P("sec", None, "gx", "gy"), P(None, "gx", "gy")),
        check_vma=False,
    )
```

```python
import jax
import jax.numpy as jnp
from jax import lax
from jax.sharding import PartitionSpec as P


def extended(cells, sides, width):
    for axis, dim in sides:
        count = lax.axis_size(axis)
        ends = count - 1
        head = lax.slice_in_dim(cells, 0, width, axis=dim)
        tail = lax.slice_in_dim(cells, cells.shape[dim] - width, cells.shape[dim], axis=dim)
        cells = jnp.concatenate(
            [
                lax.ppermute(tail, axis, [(i, (i + 1) % count) for i in range(ends)]),
                cells,
                lax.ppermute(head, axis, [((i + 1) % count, i) for i in range(ends)]),
            ],
            axis=dim,
        )
    return cells


def shifted(padded):
    lead = [(0, 0)] * (padded.ndim - 3)
    deeper = jnp.pad(padded, lead + [(1, 1), (0, 0), (0, 0)])
    centre = deeper[..., 1:-1, 1:-1, 1:-1]
    beside_all = [
        deeper[..., 2:, 1:-1, 1:-1],
        deeper[..., :-2, 1:-1, 1:-1],
        deeper[..., 1:-1, 2:, 1:-1],
        deeper[..., 1:-1, :-2, 1:-1],
        deeper[..., 1:-1, 1:-1, 2:],
        deeper[..., 1:-1, 1:-1, :-2],
    ]
    return (centre, beside_all)


def face_weights(kappa_pad):
    centre, beside_all = shifted(kappa_pad)
    return [
        2.0 * centre * other / jnp.where(centre + other > 0.0, centre + other, 1.0)
        for other in beside_all
    ]


def advance(adjoint_pad, weights, keep, speed_x, speed_y, source):
    centre, beside_all = shifted(adjoint_pad)
    diffusion = weights[0] * (beside_all[0] - centre)
    for face in range(1, 6):
        diffusion = diffusion + weights[face] * (beside_all[face] - centre)
    slope_x = 0.5 * (beside_all[2] - beside_all[3])
    slope_y = 0.5 * (beside_all[4] - beside_all[5])
    updated = keep * (centre + diffusion + speed_x * slope_x + speed_y * slope_y + source)
    return (updated, diffusion, slope_x, slope_y)


def well_sources(wells, misfit_level, layers, rows_x, cols_y, margin):
    start_x = lax.axis_index("gx") * rows_x - margin
    start_y = lax.axis_index("gy") * cols_y - margin
    coord_z = jnp.arange(layers, dtype=jnp.int32)[:, None, None]
    coord_x = (start_x + jnp.arange(rows_x + 2 * margin, dtype=jnp.int32))[None, :, None]
    coord_y = (start_y + jnp.arange(cols_y + 2 * margin, dtype=jnp.int32))[None, None, :]
    well_z = wells[:, :, 0][:, :, None, None, None]
    well_x = wells[:, :, 1][:, :, None, None, None]
    well_y = wells[:, :, 2][:, :, None, None, None]
    matches = (coord_z == well_z) & (coord_x == well_x) & (coord_y == well_y)
    return jnp.sum(jnp.where(matches, misfit_level[:, :, None, None, None], 0.0), axis=1)


def shards(
    terminal,
    forward_temp,
    conductivity,
    velocity,
    fixed_mask,
    wells,
    misfit,
    head_gradient,
    blocks,
    block_cols,
):
    layers, rows_x, cols_y = conductivity.shape
    keep = 1.0 - fixed_mask.astype(jnp.float32)
    packed = jnp.concatenate([terminal, conductivity[None], velocity, keep[None]], axis=0)
    box = extended(packed, (("gx", 2), ("gy", 3)), 2)
    ring_velocity = box[3:5, :, 1:-1, 1:-1]
    ring_keep = box[5, :, 1:-1, 1:-1]
    ring_weights = face_weights(box[2])
    weights = [w[:, 1:-1, 1:-1] for w in ring_weights]
    ring_source = well_sources(wells, misfit[1], layers, rows_x, cols_y, 1)
    ring_adjoint, diffusion, slope_x, slope_y = advance(
        box[0:2], ring_weights, ring_keep, ring_velocity[0], ring_velocity[1], ring_source
    )
    temper = forward_temp[1].astype(jnp.float32)
    inner = (Ellipsis, slice(1, -1), slice(1, -1))
    heat_sens = jnp.sum(temper * diffusion[inner], axis=0)
    flow_x = jnp.sum(temper * slope_x[inner], axis=0)
    flow_y = jnp.sum(temper * slope_y[inner], axis=0)
    source = well_sources(wells, misfit[0], layers, rows_x, cols_y, 0)
    _, diffusion, slope_x, slope_y = advance(
        ring_adjoint, weights, keep, velocity[0], velocity[1], source
    )
    temper = forward_temp[0].astype(jnp.float32)
    heat_sens = heat_sens + jnp.sum(temper * diffusion, axis=0)
    flow_x = flow_x + jnp.sum(temper * slope_x, axis=0)
    flow_y = flow_y + jnp.sum(temper * slope_y, axis=0)
    first = lax.axis_index("sec") == 0
    mine = jnp.where(first, flow_x, flow_y)
    other = jnp.where(first, flow_y, flow_x)
    partner = [(0, 1), (1, 0)]
    rounded = (mine + lax.ppermute(other, "sec", partner)).astype(jnp.bfloat16)
    row_blocks, per_row, block_size, _ = blocks.shape
    piece = lax.all_gather(rounded, "gy", axis=2, tiled=True)
    count = piece.shape[2] // block_size
    split_rows = piece.reshape(layers, rows_x, count, block_size)
    block_ids = jnp.arange(count, dtype=jnp.int32)
    chosen = (block_cols[:, :, None] == block_ids[None, None, :]).astype(jnp.bfloat16)
    portion = jnp.einsum("bkq,zxqj->bkzxj", chosen, split_rows, preferred_element_type=jnp.float32)
    picked = portion.astype(jnp.bfloat16)
    head = jnp.einsum(
        "bkzxj,bkij->zxbi", picked, blocks, preferred_element_type=jnp.float32
    ).reshape(layers, rows_x, cols_y)
    partial_sens = heat_sens + head * head_gradient[0].astype(jnp.float32)
    sensitivity = partial_sens + lax.ppermute(partial_sens, "sec", partner)
    return (head[None], sensitivity)


def solution(mesh):
    placed = (
        P("sec", None, "gx", "gy"),
        P(None, "sec", None, "gx", "gy"),
        P(None, "gx", "gy"),
        P(None, None, "gx", "gy"),
        P(None, "gx", "gy"),
        P("sec", None, None),
        P(None, "sec", None),
        P("sec", None, "gx", "gy"),
        P("gy", None, None, None),
        P("gy", None),
    )
    return jax.shard_map(
        shards,
        mesh=mesh,
        in_specs=placed,
        out_specs=(P("sec", None, "gx", "gy"), P(None, "gx", "gy")),
        check_vma=False,
    )
```

```python
import jax
import jax.numpy as jnp
from jax import lax
from jax.sharding import PartitionSpec as P


def extended(cells, sides, width):
    for axis, dim in sides:
        count = lax.axis_size(axis)
        ends = count - 1
        head = lax.slice_in_dim(cells, 0, width, axis=dim)
        tail = lax.slice_in_dim(cells, cells.shape[dim] - width, cells.shape[dim], axis=dim)
        cells = jnp.concatenate(
            [
                lax.ppermute(tail, axis, [(i, (i + 1) % count) for i in range(ends)]),
                cells,
                lax.ppermute(head, axis, [((i + 1) % count, i) for i in range(ends)]),
            ],
            axis=dim,
        )
    return cells


def shifted(padded):
    lead = [(0, 0)] * (padded.ndim - 3)
    deeper = jnp.pad(padded, lead + [(1, 1), (0, 0), (0, 0)])
    centre = deeper[..., 1:-1, 1:-1, 1:-1]
    beside_all = [
        deeper[..., 2:, 1:-1, 1:-1],
        deeper[..., :-2, 1:-1, 1:-1],
        deeper[..., 1:-1, 2:, 1:-1],
        deeper[..., 1:-1, :-2, 1:-1],
        deeper[..., 1:-1, 1:-1, 2:],
        deeper[..., 1:-1, 1:-1, :-2],
    ]
    return (centre, beside_all)


def face_weights(kappa_pad):
    centre, beside_all = shifted(kappa_pad)
    return [
        2.0 * centre * other / jnp.where(centre + other > 0.0, centre + other, 1.0)
        for other in beside_all
    ]


def advance(adjoint_pad, weights, keep, speed_x, speed_y, source):
    centre, beside_all = shifted(adjoint_pad)
    diffusion = weights[0] * (beside_all[0] - centre)
    for face in range(1, 6):
        diffusion = diffusion + weights[face] * (beside_all[face] - centre)
    slope_x = 0.5 * (beside_all[2] - beside_all[3])
    slope_y = 0.5 * (beside_all[4] - beside_all[5])
    updated = keep * (centre + diffusion + speed_x * slope_x + speed_y * slope_y + source)
    return (updated, diffusion, slope_x, slope_y)


def well_sources(wells, misfit_level, layers, rows_x, cols_y, margin):
    start_x = lax.axis_index("gx") * rows_x - margin
    start_y = lax.axis_index("gy") * cols_y - margin
    coord_z = jnp.arange(layers, dtype=jnp.int32)[:, None, None]
    coord_x = (start_x + jnp.arange(rows_x + 2 * margin, dtype=jnp.int32))[None, :, None]
    coord_y = (start_y + jnp.arange(cols_y + 2 * margin, dtype=jnp.int32))[None, None, :]
    well_z = wells[:, :, 0][:, :, None, None, None]
    well_x = wells[:, :, 1][:, :, None, None, None]
    well_y = wells[:, :, 2][:, :, None, None, None]
    matches = (coord_z == well_z) & (coord_x == well_x) & (coord_y == well_y)
    return jnp.sum(jnp.where(matches, misfit_level[:, :, None, None, None], 0.0), axis=1)


def shards(
    terminal,
    forward_temp,
    conductivity,
    velocity,
    fixed_mask,
    wells,
    misfit,
    head_gradient,
    blocks,
    block_cols,
):
    layers, rows_x, cols_y = conductivity.shape
    keep = 1.0 - fixed_mask.astype(jnp.float32)
    packed = jnp.concatenate([terminal, conductivity[None], velocity, keep[None]], axis=0)
    box = extended(packed, (("gx", 2), ("gy", 3)), 2)
    ring_velocity = box[3:5, :, 1:-1, 1:-1]
    ring_keep = box[5, :, 1:-1, 1:-1]
    ring_weights = face_weights(box[2])
    weights = [w[:, 1:-1, 1:-1] for w in ring_weights]
    ring_source = well_sources(wells, misfit[1], layers, rows_x, cols_y, 1)
    ring_adjoint, diffusion, slope_x, slope_y = advance(
        box[0:2], ring_weights, ring_keep, ring_velocity[0], ring_velocity[1], ring_source
    )
    temper = forward_temp[1].astype(jnp.float32)
    inner = (Ellipsis, slice(1, -1), slice(1, -1))
    heat_sens = jnp.sum(temper * diffusion[inner], axis=0)
    flow_x = jnp.sum(temper * slope_x[inner], axis=0)
    flow_y = jnp.sum(temper * slope_y[inner], axis=0)
    source = well_sources(wells, misfit[0], layers, rows_x, cols_y, 0)
    _, diffusion, slope_x, slope_y = advance(
        ring_adjoint, weights, keep, velocity[0], velocity[1], source
    )
    temper = forward_temp[0].astype(jnp.float32)
    heat_sens = heat_sens + jnp.sum(temper * diffusion, axis=0)
    flow_x = flow_x + jnp.sum(temper * slope_x, axis=0)
    flow_y = flow_y + jnp.sum(temper * slope_y, axis=0)
    first = lax.axis_index("sec") == 0
    mine = jnp.where(first, flow_x, flow_y)
    other = jnp.where(first, flow_y, flow_x)
    partner = [(0, 1), (1, 0)]
    rounded = (mine + lax.ppermute(other, "sec", partner)).astype(jnp.bfloat16)
    row_blocks, per_row, block_size, _ = blocks.shape
    count = lax.axis_size("gy")
    side = int(round(count ** 0.5))
    me = lax.axis_index("gy")
    across = [rounded]
    for shift in range(1, side):
        pairs = [(i, (i // side) * side + (i % side + shift) % side) for i in range(count)]
        across.append(lax.ppermute(rounded, "gy", pairs))
    row = jnp.stack(across)
    along = [row]
    for shift in range(1, side):
        pairs = [(i, (i + side * shift) % count) for i in range(count)]
        along.append(lax.ppermute(row, "gy", pairs))
    halves = cols_y // block_size
    pieces = jnp.stack(along).reshape(count, layers, rows_x, halves, block_size)
    owner = block_cols // halves
    slot = ((me // side - owner // side) % side) * side + (me % side - owner % side) % side
    chosen = (
        (slot[:, :, None, None] == jnp.arange(count, dtype=jnp.int32)[None, None, :, None])
        & ((block_cols % halves)[:, :, None, None] == jnp.arange(halves, dtype=jnp.int32)[None, None, None, :])
    ).astype(jnp.bfloat16)
    portion = jnp.einsum("bkph,pzxhj->bkzxj", chosen, pieces, preferred_element_type=jnp.float32)
    picked = portion.astype(jnp.bfloat16)
    head = jnp.einsum(
        "bkzxj,bkij->zxbi", picked, blocks, preferred_element_type=jnp.float32
    ).reshape(layers, rows_x, cols_y)
    partial_sens = heat_sens + head * head_gradient[0].astype(jnp.float32)
    sensitivity = partial_sens + lax.ppermute(partial_sens, "sec", partner)
    return (head[None], sensitivity)


def solution(mesh):
    placed = (
        P("sec", None, "gx", "gy"),
        P(None, "sec", None, "gx", "gy"),
        P(None, "gx", "gy"),
        P(None, None, "gx", "gy"),
        P(None, "gx", "gy"),
        P("sec", None, None),
        P(None, "sec", None),
        P("sec", None, "gx", "gy"),
        P("gy", None, None, None),
        P("gy", None),
    )
    return jax.shard_map(
        shards,
        mesh=mesh,
        in_specs=placed,
        out_specs=(P("sec", None, "gx", "gy"), P(None, "gx", "gy")),
        check_vma=False,
    )
```

```python
import jax
import jax.numpy as jnp
from jax import lax
from jax.sharding import PartitionSpec as P


def extended(cells, sides, width):
    for axis, dim in sides:
        count = lax.axis_size(axis)
        ends = count - 1
        head = lax.slice_in_dim(cells, 0, width, axis=dim)
        tail = lax.slice_in_dim(cells, cells.shape[dim] - width, cells.shape[dim], axis=dim)
        cells = jnp.concatenate(
            [
                lax.ppermute(tail, axis, [(i, (i + 1) % count) for i in range(ends)]),
                cells,
                lax.ppermute(head, axis, [((i + 1) % count, i) for i in range(ends)]),
            ],
            axis=dim,
        )
    return cells


def shifted(padded):
    lead = [(0, 0)] * (padded.ndim - 3)
    deeper = jnp.pad(padded, lead + [(1, 1), (0, 0), (0, 0)])
    centre = deeper[..., 1:-1, 1:-1, 1:-1]
    beside_all = [
        deeper[..., 2:, 1:-1, 1:-1],
        deeper[..., :-2, 1:-1, 1:-1],
        deeper[..., 1:-1, 2:, 1:-1],
        deeper[..., 1:-1, :-2, 1:-1],
        deeper[..., 1:-1, 1:-1, 2:],
        deeper[..., 1:-1, 1:-1, :-2],
    ]
    return (centre, beside_all)


def face_weights(kappa_pad):
    centre, beside_all = shifted(kappa_pad)
    return [
        2.0 * centre * other / jnp.where(centre + other > 0.0, centre + other, 1.0)
        for other in beside_all
    ]


def advance(adjoint_pad, weights, keep, speed_x, speed_y, source):
    centre, beside_all = shifted(adjoint_pad)
    diffusion = weights[0] * (beside_all[0] - centre)
    for face in range(1, 6):
        diffusion = diffusion + weights[face] * (beside_all[face] - centre)
    slope_x = 0.5 * (beside_all[2] - beside_all[3])
    slope_y = 0.5 * (beside_all[4] - beside_all[5])
    updated = keep * (centre + diffusion + speed_x * slope_x + speed_y * slope_y + source)
    return (updated, diffusion, slope_x, slope_y)


def well_sources(wells, misfit_level, layers, rows_x, cols_y, margin):
    start_x = lax.axis_index("gx") * rows_x - margin
    start_y = lax.axis_index("gy") * cols_y - margin
    coord_z = jnp.arange(layers, dtype=jnp.int32)[:, None, None]
    coord_x = (start_x + jnp.arange(rows_x + 2 * margin, dtype=jnp.int32))[None, :, None]
    coord_y = (start_y + jnp.arange(cols_y + 2 * margin, dtype=jnp.int32))[None, None, :]
    well_z = wells[:, :, 0][:, :, None, None, None]
    well_x = wells[:, :, 1][:, :, None, None, None]
    well_y = wells[:, :, 2][:, :, None, None, None]
    matches = (coord_z == well_z) & (coord_x == well_x) & (coord_y == well_y)
    return jnp.sum(jnp.where(matches, misfit_level[:, :, None, None, None], 0.0), axis=1)


def head_chunk(mine, other, heat_sens, gradient, blocks, block_cols):
    partner = [(0, 1), (1, 0)]
    layers, rows_x, cols_y = mine.shape
    rounded = (mine + lax.ppermute(other, "sec", partner)).astype(jnp.bfloat16)
    row_blocks, per_row, block_size, _ = blocks.shape
    count = lax.axis_size("gy")
    side = int(round(count ** 0.5))
    me = lax.axis_index("gy")
    across = [rounded]
    for shift in range(1, side):
        pairs = [(i, (i // side) * side + (i % side + shift) % side) for i in range(count)]
        across.append(lax.ppermute(rounded, "gy", pairs))
    row = jnp.stack(across)
    along = [row]
    for shift in range(1, side):
        pairs = [(i, (i + side * shift) % count) for i in range(count)]
        along.append(lax.ppermute(row, "gy", pairs))
    halves = cols_y // block_size
    pieces = jnp.stack(along).reshape(count, layers, rows_x, halves, block_size)
    owner = block_cols // halves
    slot = ((me // side - owner // side) % side) * side + (me % side - owner % side) % side
    chosen = (
        (slot[:, :, None, None] == jnp.arange(count, dtype=jnp.int32)[None, None, :, None])
        & ((block_cols % halves)[:, :, None, None] == jnp.arange(halves, dtype=jnp.int32)[None, None, None, :])
    ).astype(jnp.bfloat16)
    portion = jnp.einsum("bkph,pzxhj->bkzxj", chosen, pieces, preferred_element_type=jnp.float32)
    picked = portion.astype(jnp.bfloat16)
    head = jnp.einsum(
        "bkzxj,bkij->zxbi", picked, blocks, preferred_element_type=jnp.float32
    ).reshape(layers, rows_x, cols_y)
    partial_sens = heat_sens + head * gradient
    return head, partial_sens + lax.ppermute(partial_sens, "sec", partner)


def shards(
    terminal,
    forward_temp,
    conductivity,
    velocity,
    fixed_mask,
    wells,
    misfit,
    head_gradient,
    blocks,
    block_cols,
):
    layers, rows_x, cols_y = conductivity.shape
    keep = 1.0 - fixed_mask.astype(jnp.float32)
    packed = jnp.concatenate([terminal, conductivity[None], velocity, keep[None]], axis=0)
    box = extended(packed, (("gx", 2), ("gy", 3)), 2)
    ring_velocity = box[3:5, :, 1:-1, 1:-1]
    ring_keep = box[5, :, 1:-1, 1:-1]
    ring_weights = face_weights(box[2])
    weights = [w[:, 1:-1, 1:-1] for w in ring_weights]
    ring_source = well_sources(wells, misfit[1], layers, rows_x, cols_y, 1)
    ring_adjoint, diffusion, slope_x, slope_y = advance(
        box[0:2], ring_weights, ring_keep, ring_velocity[0], ring_velocity[1], ring_source
    )
    temper = forward_temp[1].astype(jnp.float32)
    inner = (Ellipsis, slice(1, -1), slice(1, -1))
    heat_sens = jnp.sum(temper * diffusion[inner], axis=0)
    flow_x = jnp.sum(temper * slope_x[inner], axis=0)
    flow_y = jnp.sum(temper * slope_y[inner], axis=0)
    source = well_sources(wells, misfit[0], layers, rows_x, cols_y, 0)
    _, diffusion, slope_x, slope_y = advance(
        ring_adjoint, weights, keep, velocity[0], velocity[1], source
    )
    temper = forward_temp[0].astype(jnp.float32)
    heat_sens = heat_sens + jnp.sum(temper * diffusion, axis=0)
    flow_x = flow_x + jnp.sum(temper * slope_x, axis=0)
    flow_y = flow_y + jnp.sum(temper * slope_y, axis=0)
    first = lax.axis_index("sec") == 0
    mine = jnp.where(first, flow_x, flow_y)
    other = jnp.where(first, flow_y, flow_x)
    gradient = head_gradient[0].astype(jnp.float32)
    chunks = 2
    depth = layers // chunks
    heads, sens = [], []
    for part in range(chunks):
        cut = slice(part * depth, (part + 1) * depth)
        head, total = head_chunk(
            mine[cut], other[cut], heat_sens[cut], gradient[cut], blocks, block_cols
        )
        heads.append(head)
        sens.append(total)
    head = jnp.concatenate(heads, axis=0)
    sensitivity = jnp.concatenate(sens, axis=0)
    return (head[None], sensitivity)


def solution(mesh):
    placed = (
        P("sec", None, "gx", "gy"),
        P(None, "sec", None, "gx", "gy"),
        P(None, "gx", "gy"),
        P(None, None, "gx", "gy"),
        P(None, "gx", "gy"),
        P("sec", None, None),
        P(None, "sec", None),
        P("sec", None, "gx", "gy"),
        P("gy", None, None, None),
        P("gy", None),
    )
    return jax.shard_map(
        shards,
        mesh=mesh,
        in_specs=placed,
        out_specs=(P("sec", None, "gx", "gy"), P(None, "gx", "gy")),
        check_vma=False,
    )
```

```python
import jax
import jax.numpy as jnp
from jax import lax
from jax.sharding import PartitionSpec as P


def extended(cells, sides, width):
    for axis, dim in sides:
        count = lax.axis_size(axis)
        ends = count - 1
        head = lax.slice_in_dim(cells, 0, width, axis=dim)
        tail = lax.slice_in_dim(cells, cells.shape[dim] - width, cells.shape[dim], axis=dim)
        cells = jnp.concatenate(
            [
                lax.ppermute(tail, axis, [(i, (i + 1) % count) for i in range(ends)]),
                cells,
                lax.ppermute(head, axis, [((i + 1) % count, i) for i in range(ends)]),
            ],
            axis=dim,
        )
    return cells


def shifted(padded):
    lead = [(0, 0)] * (padded.ndim - 3)
    deeper = jnp.pad(padded, lead + [(1, 1), (0, 0), (0, 0)])
    centre = deeper[..., 1:-1, 1:-1, 1:-1]
    beside_all = [
        deeper[..., 2:, 1:-1, 1:-1],
        deeper[..., :-2, 1:-1, 1:-1],
        deeper[..., 1:-1, 2:, 1:-1],
        deeper[..., 1:-1, :-2, 1:-1],
        deeper[..., 1:-1, 1:-1, 2:],
        deeper[..., 1:-1, 1:-1, :-2],
    ]
    return (centre, beside_all)


def face_weights(kappa_pad):
    centre, beside_all = shifted(kappa_pad)
    return [
        2.0 * centre * other / jnp.where(centre + other > 0.0, centre + other, 1.0)
        for other in beside_all
    ]


def advance(adjoint_pad, weights, keep, speed_x, speed_y, source):
    centre, beside_all = shifted(adjoint_pad)
    diffusion = weights[0] * (beside_all[0] - centre)
    for face in range(1, 6):
        diffusion = diffusion + weights[face] * (beside_all[face] - centre)
    slope_x = 0.5 * (beside_all[2] - beside_all[3])
    slope_y = 0.5 * (beside_all[4] - beside_all[5])
    updated = keep * (centre + diffusion + speed_x * slope_x + speed_y * slope_y + source)
    return (updated, diffusion, slope_x, slope_y)


def well_sources(wells, misfit_level, layers, rows_x, cols_y, margin):
    start_x = lax.axis_index("gx") * rows_x - margin
    start_y = lax.axis_index("gy") * cols_y - margin
    coord_z = jnp.arange(layers, dtype=jnp.int32)[:, None, None]
    coord_x = (start_x + jnp.arange(rows_x + 2 * margin, dtype=jnp.int32))[None, :, None]
    coord_y = (start_y + jnp.arange(cols_y + 2 * margin, dtype=jnp.int32))[None, None, :]
    well_z = wells[:, :, 0][:, :, None, None, None]
    well_x = wells[:, :, 1][:, :, None, None, None]
    well_y = wells[:, :, 2][:, :, None, None, None]
    matches = (coord_z == well_z) & (coord_x == well_x) & (coord_y == well_y)
    return jnp.sum(jnp.where(matches, misfit_level[:, :, None, None, None], 0.0), axis=1)


def shards(
    terminal,
    forward_temp,
    conductivity,
    velocity,
    fixed_mask,
    wells,
    misfit,
    head_gradient,
    blocks,
    block_cols,
):
    layers, rows_x, cols_y = conductivity.shape
    keep = 1.0 - fixed_mask.astype(jnp.float32)
    packed = jnp.concatenate([terminal, conductivity[None], velocity, keep[None]], axis=0)
    box = extended(packed, (("gx", 2), ("gy", 3)), 2)
    ring_velocity = box[3:5, :, 1:-1, 1:-1]
    ring_keep = box[5, :, 1:-1, 1:-1]
    ring_weights = face_weights(box[2])
    weights = [w[:, 1:-1, 1:-1] for w in ring_weights]
    ring_source = well_sources(wells, misfit[1], layers, rows_x, cols_y, 1)
    ring_adjoint, diffusion, slope_x, slope_y = advance(
        box[0:2], ring_weights, ring_keep, ring_velocity[0], ring_velocity[1], ring_source
    )
    temper = forward_temp[1].astype(jnp.float32)
    inner = (Ellipsis, slice(1, -1), slice(1, -1))
    heat_sens = jnp.sum(temper * diffusion[inner], axis=0)
    flow_x = jnp.sum(temper * slope_x[inner], axis=0)
    flow_y = jnp.sum(temper * slope_y[inner], axis=0)
    source = well_sources(wells, misfit[0], layers, rows_x, cols_y, 0)
    _, diffusion, slope_x, slope_y = advance(
        ring_adjoint, weights, keep, velocity[0], velocity[1], source
    )
    temper = forward_temp[0].astype(jnp.float32)
    heat_sens = heat_sens + jnp.sum(temper * diffusion, axis=0)
    flow_x = flow_x + jnp.sum(temper * slope_x, axis=0)
    flow_y = flow_y + jnp.sum(temper * slope_y, axis=0)
    first = lax.axis_index("sec") == 0
    mine = jnp.where(first, flow_x, flow_y)
    other = jnp.where(first, flow_y, flow_x)
    partner = [(0, 1), (1, 0)]
    rounded = (mine + lax.ppermute(other, "sec", partner)).astype(jnp.bfloat16)
    row_blocks, per_row, block_size, _ = blocks.shape
    count = lax.axis_size("gy")
    side = int(round(count ** 0.5))
    me = lax.axis_index("gy")
    def inner(shift):
        return [(i, (i // side) * side + (i % side + shift) % side) for i in range(count)]

    def outer(shift):
        return [(i, (i + side * shift) % count) for i in range(count)]

    def gather(value, first, second):
        row = jnp.stack([value] + [lax.ppermute(value, "gy", first(t)) for t in range(1, side)])
        return jnp.stack([row] + [lax.ppermute(row, "gy", second(t)) for t in range(1, side)])

    halves = cols_y // block_size
    front = gather(rounded[..., :block_size], inner, outer)
    back = gather(rounded[..., block_size:], outer, inner)
    pieces = jnp.stack(
        [front.reshape(count, layers, rows_x, block_size), back.reshape(count, layers, rows_x, block_size)],
        axis=3,
    )
    owner = block_cols // halves
    step_x = (me // side - owner // side) % side
    step_y = (me % side - owner % side) % side
    slot = jnp.where(block_cols % halves == 0, step_x * side + step_y, step_y * side + step_x)
    chosen = (
        (slot[:, :, None, None] == jnp.arange(count, dtype=jnp.int32)[None, None, :, None])
        & ((block_cols % halves)[:, :, None, None] == jnp.arange(halves, dtype=jnp.int32)[None, None, None, :])
    ).astype(jnp.bfloat16)
    portion = jnp.einsum("bkph,pzxhj->bkzxj", chosen, pieces, preferred_element_type=jnp.float32)
    picked = portion.astype(jnp.bfloat16)
    head = jnp.einsum(
        "bkzxj,bkij->zxbi", picked, blocks, preferred_element_type=jnp.float32
    ).reshape(layers, rows_x, cols_y)
    partial_sens = heat_sens + head * head_gradient[0].astype(jnp.float32)
    sensitivity = partial_sens + lax.ppermute(partial_sens, "sec", partner)
    return (head[None], sensitivity)


def solution(mesh):
    placed = (
        P("sec", None, "gx", "gy"),
        P(None, "sec", None, "gx", "gy"),
        P(None, "gx", "gy"),
        P(None, None, "gx", "gy"),
        P(None, "gx", "gy"),
        P("sec", None, None),
        P(None, "sec", None),
        P("sec", None, "gx", "gy"),
        P("gy", None, None, None),
        P("gy", None),
    )
    return jax.shard_map(
        shards,
        mesh=mesh,
        in_specs=placed,
        out_specs=(P("sec", None, "gx", "gy"), P(None, "gx", "gy")),
        check_vma=False,
    )
```

```python
import jax
import jax.numpy as jnp
from jax import lax
from jax.sharding import PartitionSpec as P


def extended(cells, sides, width):
    for axis, dim in sides:
        count = lax.axis_size(axis)
        ends = count - 1
        head = lax.slice_in_dim(cells, 0, width, axis=dim)
        tail = lax.slice_in_dim(cells, cells.shape[dim] - width, cells.shape[dim], axis=dim)
        cells = jnp.concatenate(
            [
                lax.ppermute(tail, axis, [(i, (i + 1) % count) for i in range(ends)]),
                cells,
                lax.ppermute(head, axis, [((i + 1) % count, i) for i in range(ends)]),
            ],
            axis=dim,
        )
    return cells


def shifted(padded):
    lead = [(0, 0)] * (padded.ndim - 3)
    deeper = jnp.pad(padded, lead + [(1, 1), (0, 0), (0, 0)])
    centre = deeper[..., 1:-1, 1:-1, 1:-1]
    beside_all = [
        deeper[..., 2:, 1:-1, 1:-1],
        deeper[..., :-2, 1:-1, 1:-1],
        deeper[..., 1:-1, 2:, 1:-1],
        deeper[..., 1:-1, :-2, 1:-1],
        deeper[..., 1:-1, 1:-1, 2:],
        deeper[..., 1:-1, 1:-1, :-2],
    ]
    return (centre, beside_all)


def face_weights(kappa_pad):
    centre, beside_all = shifted(kappa_pad)
    return [
        2.0 * centre * other / jnp.where(centre + other > 0.0, centre + other, 1.0)
        for other in beside_all
    ]


def advance(adjoint_pad, weights, keep, speed_x, speed_y, source):
    centre, beside_all = shifted(adjoint_pad)
    diffusion = weights[0] * (beside_all[0] - centre)
    for face in range(1, 6):
        diffusion = diffusion + weights[face] * (beside_all[face] - centre)
    slope_x = 0.5 * (beside_all[2] - beside_all[3])
    slope_y = 0.5 * (beside_all[4] - beside_all[5])
    updated = keep * (centre + diffusion + speed_x * slope_x + speed_y * slope_y + source)
    return (updated, diffusion, slope_x, slope_y)


def well_sources(wells, misfit_level, layers, rows_x, cols_y, margin):
    start_x = lax.axis_index("gx") * rows_x - margin
    start_y = lax.axis_index("gy") * cols_y - margin
    coord_z = jnp.arange(layers, dtype=jnp.int32)[:, None, None]
    coord_x = (start_x + jnp.arange(rows_x + 2 * margin, dtype=jnp.int32))[None, :, None]
    coord_y = (start_y + jnp.arange(cols_y + 2 * margin, dtype=jnp.int32))[None, None, :]
    well_z = wells[:, :, 0][:, :, None, None, None]
    well_x = wells[:, :, 1][:, :, None, None, None]
    well_y = wells[:, :, 2][:, :, None, None, None]
    matches = (coord_z == well_z) & (coord_x == well_x) & (coord_y == well_y)
    return jnp.sum(jnp.where(matches, misfit_level[:, :, None, None, None], 0.0), axis=1)


def shards(
    terminal,
    forward_temp,
    conductivity,
    velocity,
    fixed_mask,
    wells,
    misfit,
    head_gradient,
    blocks,
    block_cols,
):
    layers, rows_x, cols_y = conductivity.shape
    keep = 1.0 - fixed_mask.astype(jnp.float32)
    packed = jnp.concatenate([terminal, conductivity[None], velocity, keep[None]], axis=0)
    box = extended(packed, (("gx", 2), ("gy", 3)), 2)
    ring_velocity = box[3:5, :, 1:-1, 1:-1]
    ring_keep = box[5, :, 1:-1, 1:-1]
    ring_weights = face_weights(box[2])
    weights = [w[:, 1:-1, 1:-1] for w in ring_weights]
    ring_source = well_sources(wells, misfit[1], layers, rows_x, cols_y, 1)
    ring_adjoint, diffusion, slope_x, slope_y = advance(
        box[0:2], ring_weights, ring_keep, ring_velocity[0], ring_velocity[1], ring_source
    )
    temper = forward_temp[1].astype(jnp.float32)
    inner = (Ellipsis, slice(1, -1), slice(1, -1))
    heat_sens = jnp.sum(temper * diffusion[inner], axis=0)
    flow_x = jnp.sum(temper * slope_x[inner], axis=0)
    flow_y = jnp.sum(temper * slope_y[inner], axis=0)
    source = well_sources(wells, misfit[0], layers, rows_x, cols_y, 0)
    _, diffusion, slope_x, slope_y = advance(
        ring_adjoint, weights, keep, velocity[0], velocity[1], source
    )
    temper = forward_temp[0].astype(jnp.float32)
    heat_sens = heat_sens + jnp.sum(temper * diffusion, axis=0)
    flow_x = flow_x + jnp.sum(temper * slope_x, axis=0)
    flow_y = flow_y + jnp.sum(temper * slope_y, axis=0)
    first = lax.axis_index("sec") == 0
    mine = jnp.where(first, flow_x, flow_y)
    other = jnp.where(first, flow_y, flow_x)
    partner = [(0, 1), (1, 0)]
    rounded = (mine + lax.ppermute(other, "sec", partner)).astype(jnp.bfloat16)
    row_blocks, per_row, block_size, _ = blocks.shape
    count = lax.axis_size("gy")
    halves = cols_y // block_size
    copies = jnp.broadcast_to(rounded[None], (count,) + rounded.shape)
    gathered = lax.all_to_all(copies, "gy", 0, 0, tiled=False)
    pieces = gathered.reshape(count, layers, rows_x, halves, block_size)
    chosen = (
        ((block_cols // halves)[:, :, None, None] == jnp.arange(count, dtype=jnp.int32)[None, None, :, None])
        & ((block_cols % halves)[:, :, None, None] == jnp.arange(halves, dtype=jnp.int32)[None, None, None, :])
    ).astype(jnp.bfloat16)
    portion = jnp.einsum("bkph,pzxhj->bkzxj", chosen, pieces, preferred_element_type=jnp.float32)
    picked = portion.astype(jnp.bfloat16)
    head = jnp.einsum(
        "bkzxj,bkij->zxbi", picked, blocks, preferred_element_type=jnp.float32
    ).reshape(layers, rows_x, cols_y)
    partial_sens = heat_sens + head * head_gradient[0].astype(jnp.float32)
    sensitivity = partial_sens + lax.ppermute(partial_sens, "sec", partner)
    return (head[None], sensitivity)


def solution(mesh):
    placed = (
        P("sec", None, "gx", "gy"),
        P(None, "sec", None, "gx", "gy"),
        P(None, "gx", "gy"),
        P(None, None, "gx", "gy"),
        P(None, "gx", "gy"),
        P("sec", None, None),
        P(None, "sec", None),
        P("sec", None, "gx", "gy"),
        P("gy", None, None, None),
        P("gy", None),
    )
    return jax.shard_map(
        shards,
        mesh=mesh,
        in_specs=placed,
        out_specs=(P("sec", None, "gx", "gy"), P(None, "gx", "gy")),
        check_vma=False,
    )
```

```python
import jax
import jax.numpy as jnp
from jax import lax
from jax.sharding import PartitionSpec as P
from jax.experimental import pallas as pl
from jax.experimental.pallas import tpu as pltpu


def extended(cells, sides, width):
    for axis, dim in sides:
        count = lax.axis_size(axis)
        ends = count - 1
        head = lax.slice_in_dim(cells, 0, width, axis=dim)
        tail = lax.slice_in_dim(cells, cells.shape[dim] - width, cells.shape[dim], axis=dim)
        cells = jnp.concatenate(
            [
                lax.ppermute(tail, axis, [(i, (i + 1) % count) for i in range(ends)]),
                cells,
                lax.ppermute(head, axis, [((i + 1) % count, i) for i in range(ends)]),
            ],
            axis=dim,
        )
    return cells


def shifted(padded):
    lead = [(0, 0)] * (padded.ndim - 3)
    deeper = jnp.pad(padded, lead + [(1, 1), (0, 0), (0, 0)])
    centre = deeper[..., 1:-1, 1:-1, 1:-1]
    beside_all = [
        deeper[..., 2:, 1:-1, 1:-1],
        deeper[..., :-2, 1:-1, 1:-1],
        deeper[..., 1:-1, 2:, 1:-1],
        deeper[..., 1:-1, :-2, 1:-1],
        deeper[..., 1:-1, 1:-1, 2:],
        deeper[..., 1:-1, 1:-1, :-2],
    ]
    return (centre, beside_all)


def face_weights(kappa_pad):
    centre, beside_all = shifted(kappa_pad)
    return [
        2.0 * centre * other / jnp.where(centre + other > 0.0, centre + other, 1.0)
        for other in beside_all
    ]


def advance(adjoint_pad, weights, keep, speed_x, speed_y, source):
    centre, beside_all = shifted(adjoint_pad)
    diffusion = weights[0] * (beside_all[0] - centre)
    for face in range(1, 6):
        diffusion = diffusion + weights[face] * (beside_all[face] - centre)
    slope_x = 0.5 * (beside_all[2] - beside_all[3])
    slope_y = 0.5 * (beside_all[4] - beside_all[5])
    updated = keep * (centre + diffusion + speed_x * slope_x + speed_y * slope_y + source)
    return (updated, diffusion, slope_x, slope_y)


def well_sources(wells, misfit_level, layers, rows_x, cols_y, margin):
    start_x = lax.axis_index("gx") * rows_x - margin
    start_y = lax.axis_index("gy") * cols_y - margin
    coord_z = jnp.arange(layers, dtype=jnp.int32)[:, None, None]
    coord_x = (start_x + jnp.arange(rows_x + 2 * margin, dtype=jnp.int32))[None, :, None]
    coord_y = (start_y + jnp.arange(cols_y + 2 * margin, dtype=jnp.int32))[None, None, :]
    well_z = wells[:, :, 0][:, :, None, None, None]
    well_x = wells[:, :, 1][:, :, None, None, None]
    well_y = wells[:, :, 2][:, :, None, None, None]
    matches = (coord_z == well_z) & (coord_x == well_x) & (coord_y == well_y)
    return jnp.sum(jnp.where(matches, misfit_level[:, :, None, None, None], 0.0), axis=1)


def head_kernel(cols_ref, gathered_ref, blocks_ref, heat_ref, grad_ref, head_ref, part_ref):
    row_blocks, per_row, size, _ = blocks_ref.shape
    halves = gathered_ref.shape[2] // size
    for row in range(row_blocks):
        total = jnp.zeros((gathered_ref.shape[1], size), jnp.float32)
        for k in range(per_row):
            col = cols_ref[row, k]
            start = pl.multiple_of((col % halves) * size, size)
            slab = gathered_ref[col // halves, :, pl.ds(start, size)]
            total = total + lax.dot_general(
                slab, blocks_ref[row, k], (((1,), (1,)), ((), ())), preferred_element_type=jnp.float32
            )
        out = slice(row * size, (row + 1) * size)
        head_ref[:, out] = total
        part_ref[:, out] = heat_ref[:, out] + total * grad_ref[:, out].astype(jnp.float32)


def apply_head(block_cols, gathered, blocks, heat, grad):
    cells, width = heat.shape
    vmem = pltpu.VMEM
    return pl.pallas_call(
        head_kernel,
        out_shape=(
            jax.ShapeDtypeStruct((cells, width), jnp.float32),
            jax.ShapeDtypeStruct((cells, width), jnp.float32),
        ),
        in_specs=[pl.BlockSpec(memory_space=pltpu.SMEM)] + [pl.BlockSpec(memory_space=vmem)] * 4,
        out_specs=(pl.BlockSpec(memory_space=vmem), pl.BlockSpec(memory_space=vmem)),
        cost_estimate=pl.CostEstimate(
            flops=2 * cells * width * blocks.shape[1] * blocks.shape[2],
            bytes_accessed=gathered.size * 2 + blocks.size * 2 + cells * width * 14,
            transcendentals=0,
        ),
    )(block_cols, gathered, blocks, heat, grad)


def shards(
    terminal,
    forward_temp,
    conductivity,
    velocity,
    fixed_mask,
    wells,
    misfit,
    head_gradient,
    blocks,
    block_cols,
):
    layers, rows_x, cols_y = conductivity.shape
    keep = 1.0 - fixed_mask.astype(jnp.float32)
    packed = jnp.concatenate([terminal, conductivity[None], velocity, keep[None]], axis=0)
    box = extended(packed, (("gx", 2), ("gy", 3)), 2)
    ring_velocity = box[3:5, :, 1:-1, 1:-1]
    ring_keep = box[5, :, 1:-1, 1:-1]
    ring_weights = face_weights(box[2])
    weights = [w[:, 1:-1, 1:-1] for w in ring_weights]
    ring_source = well_sources(wells, misfit[1], layers, rows_x, cols_y, 1)
    ring_adjoint, diffusion, slope_x, slope_y = advance(
        box[0:2], ring_weights, ring_keep, ring_velocity[0], ring_velocity[1], ring_source
    )
    temper = forward_temp[1].astype(jnp.float32)
    inner = (Ellipsis, slice(1, -1), slice(1, -1))
    heat_sens = jnp.sum(temper * diffusion[inner], axis=0)
    flow_x = jnp.sum(temper * slope_x[inner], axis=0)
    flow_y = jnp.sum(temper * slope_y[inner], axis=0)
    source = well_sources(wells, misfit[0], layers, rows_x, cols_y, 0)
    _, diffusion, slope_x, slope_y = advance(
        ring_adjoint, weights, keep, velocity[0], velocity[1], source
    )
    temper = forward_temp[0].astype(jnp.float32)
    heat_sens = heat_sens + jnp.sum(temper * diffusion, axis=0)
    flow_x = flow_x + jnp.sum(temper * slope_x, axis=0)
    flow_y = flow_y + jnp.sum(temper * slope_y, axis=0)
    first = lax.axis_index("sec") == 0
    mine = jnp.where(first, flow_x, flow_y)
    other = jnp.where(first, flow_y, flow_x)
    partner = [(0, 1), (1, 0)]
    rounded = (mine + lax.ppermute(other, "sec", partner)).astype(jnp.bfloat16)
    row_blocks, per_row, block_size, _ = blocks.shape
    count = lax.axis_size("gy")
    copies = jnp.broadcast_to(rounded[None], (count,) + rounded.shape)
    gathered = lax.all_to_all(copies, "gy", 0, 0, tiled=False)
    cells = layers * rows_x
    head, partial_sens = apply_head(
        block_cols,
        gathered.reshape(count, cells, cols_y),
        blocks,
        heat_sens.reshape(cells, cols_y),
        head_gradient[0].reshape(cells, cols_y),
    )
    head = head.reshape(layers, rows_x, cols_y)
    partial_sens = partial_sens.reshape(layers, rows_x, cols_y)
    sensitivity = partial_sens + lax.ppermute(partial_sens, "sec", partner)
    return (head[None], sensitivity)


def solution(mesh):
    placed = (
        P("sec", None, "gx", "gy"),
        P(None, "sec", None, "gx", "gy"),
        P(None, "gx", "gy"),
        P(None, None, "gx", "gy"),
        P(None, "gx", "gy"),
        P("sec", None, None),
        P(None, "sec", None),
        P("sec", None, "gx", "gy"),
        P("gy", None, None, None),
        P("gy", None),
    )
    return jax.shard_map(
        shards,
        mesh=mesh,
        in_specs=placed,
        out_specs=(P("sec", None, "gx", "gy"), P(None, "gx", "gy")),
        check_vma=False,
    )
```

```python
import jax
import jax.numpy as jnp
from jax import lax
from jax.sharding import PartitionSpec as P
from jax.experimental import pallas as pl
from jax.experimental.pallas import tpu as pltpu


def extended(cells, sides, width):
    for axis, dim in sides:
        count = lax.axis_size(axis)
        ends = count - 1
        head = lax.slice_in_dim(cells, 0, width, axis=dim)
        tail = lax.slice_in_dim(cells, cells.shape[dim] - width, cells.shape[dim], axis=dim)
        cells = jnp.concatenate(
            [
                lax.ppermute(tail, axis, [(i, (i + 1) % count) for i in range(ends)]),
                cells,
                lax.ppermute(head, axis, [((i + 1) % count, i) for i in range(ends)]),
            ],
            axis=dim,
        )
    return cells


def shifted(padded):
    lead = [(0, 0)] * (padded.ndim - 3)
    deeper = jnp.pad(padded, lead + [(1, 1), (0, 0), (0, 0)])
    centre = deeper[..., 1:-1, 1:-1, 1:-1]
    beside_all = [
        deeper[..., 2:, 1:-1, 1:-1],
        deeper[..., :-2, 1:-1, 1:-1],
        deeper[..., 1:-1, 2:, 1:-1],
        deeper[..., 1:-1, :-2, 1:-1],
        deeper[..., 1:-1, 1:-1, 2:],
        deeper[..., 1:-1, 1:-1, :-2],
    ]
    return (centre, beside_all)


def face_weights(kappa_pad):
    centre, beside_all = shifted(kappa_pad)
    return [
        2.0 * centre * other / jnp.where(centre + other > 0.0, centre + other, 1.0)
        for other in beside_all
    ]


def advance(adjoint_pad, weights, keep, speed_x, speed_y, source):
    centre, beside_all = shifted(adjoint_pad)
    diffusion = weights[0] * (beside_all[0] - centre)
    for face in range(1, 6):
        diffusion = diffusion + weights[face] * (beside_all[face] - centre)
    slope_x = 0.5 * (beside_all[2] - beside_all[3])
    slope_y = 0.5 * (beside_all[4] - beside_all[5])
    updated = keep * (centre + diffusion + speed_x * slope_x + speed_y * slope_y + source)
    return (updated, diffusion, slope_x, slope_y)


def well_sources(wells, misfit_level, layers, rows_x, cols_y, margin):
    start_x = lax.axis_index("gx") * rows_x - margin
    start_y = lax.axis_index("gy") * cols_y - margin
    coord_z = jnp.arange(layers, dtype=jnp.int32)[:, None, None]
    coord_x = (start_x + jnp.arange(rows_x + 2 * margin, dtype=jnp.int32))[None, :, None]
    coord_y = (start_y + jnp.arange(cols_y + 2 * margin, dtype=jnp.int32))[None, None, :]
    well_z = wells[:, :, 0][:, :, None, None, None]
    well_x = wells[:, :, 1][:, :, None, None, None]
    well_y = wells[:, :, 2][:, :, None, None, None]
    matches = (coord_z == well_z) & (coord_x == well_x) & (coord_y == well_y)
    return jnp.sum(jnp.where(matches, misfit_level[:, :, None, None, None], 0.0), axis=1)


def conductance(centre, other):
    return 2.0 * centre * other / jnp.where(centre + other > 0.0, centre + other, 1.0)


def heat_kernel(offs_ref, wells_ref, misfit_ref, box_ref, temp_ref, heat_ref, fx_ref, fy_ref, adj_ref, w_ref):
    tests, layers, rows, cols = adj_ref.shape
    tile_x, tile_y = heat_ref.shape[1], heat_ref.shape[2]
    zero = jnp.zeros((rows, cols), jnp.float32)

    def plane(ref, lead, z):
        above = jnp.where(z + 1 < layers, ref[lead, jnp.minimum(z + 1, layers - 1)], zero)
        below = jnp.where(z > 0, ref[lead, jnp.maximum(z - 1, 0)], zero)
        return ref[lead, z], above, below

    def faces(value, above, below):
        return [
            above,
            below,
            pltpu.roll(value, rows - 1, 0),
            pltpu.roll(value, 1, 0),
            pltpu.roll(value, cols - 1, 1),
            pltpu.roll(value, 1, 1),
        ]

    def weigh(z, carry):
        centre, above, below = plane(box_ref, 2, z)
        for face, other in enumerate(faces(centre, above, below)):
            w_ref[face, z] = conductance(centre, other)
        return carry

    lax.fori_loop(0, layers, weigh, 0)

    def advance(source_ref, level, store):
        def body(z, carry):
            speed_x = box_ref[3, z]
            speed_y = box_ref[4, z]
            keep = box_ref[5, z]
            heat = fx = fy = None
            for test in range(tests):
                centre, above, below = plane(source_ref, test, z)
                beside = faces(centre, above, below)
                diffusion = w_ref[0, z] * (beside[0] - centre)
                for face in range(1, 6):
                    diffusion = diffusion + w_ref[face, z] * (beside[face] - centre)
                slope_x = 0.5 * (beside[2] - beside[3])
                slope_y = 0.5 * (beside[4] - beside[5])
                updated = keep * (centre + diffusion + speed_x * slope_x + speed_y * slope_y)
                if store:
                    adj_ref[test, z] = updated
                temper = temp_ref[level, test, z].astype(jnp.float32)
                terms = [temper * v[:tile_x, :tile_y] for v in (diffusion, slope_x, slope_y)]
                if heat is None:
                    heat, fx, fy = terms
                else:
                    heat, fx, fy = heat + terms[0], fx + terms[1], fy + terms[2]
            if store:
                heat_ref[z], fx_ref[z], fy_ref[z] = heat, fx, fy
            else:
                heat_ref[z] = heat_ref[z] + heat
                fx_ref[z] = fx_ref[z] + fx
                fy_ref[z] = fy_ref[z] + fy
            return carry

        lax.fori_loop(0, layers, body, 0)

    advance(box_ref, 1, True)
    row_ids = lax.broadcasted_iota(jnp.int32, (rows, cols), 0)
    col_ids = lax.broadcasted_iota(jnp.int32, (rows, cols), 1)
    for test in range(tests):
        for well in range(wells_ref.shape[1]):
            depth = wells_ref[test, well, 0]
            at_x = wells_ref[test, well, 1] - offs_ref[0]
            at_y = wells_ref[test, well, 2] - offs_ref[1]
            inside = (at_x >= -2) & (at_x < tile_x + 2) & (at_y >= -2) & (at_y < tile_y + 2)
            amount = jnp.where(inside, misfit_ref[1, test, well], 0.0)
            hit = (row_ids == jnp.where(at_x < 0, at_x + rows, at_x)) & (
                col_ids == jnp.where(at_y < 0, at_y + cols, at_y)
            )
            adj_ref[test, depth] = adj_ref[test, depth] + jnp.where(hit, box_ref[5, depth] * amount, 0.0)
    advance(adj_ref, 0, False)


def heat_phase(offs, wells, misfit, box, temp):
    channels, layers, rows, cols = box.shape
    tests = temp.shape[1]
    tile = temp.shape[3:]
    smem = pl.BlockSpec(memory_space=pltpu.SMEM)
    vmem = pl.BlockSpec(memory_space=pltpu.VMEM)
    out = jax.ShapeDtypeStruct((layers,) + tile, jnp.float32)
    return pl.pallas_call(
        heat_kernel,
        out_shape=(out, out, out),
        in_specs=[smem, smem, smem, vmem, vmem],
        out_specs=(vmem, vmem, vmem),
        scratch_shapes=[
            pltpu.VMEM((tests, layers, rows, cols), jnp.float32),
            pltpu.VMEM((6, layers, rows, cols), jnp.float32),
        ],
    )(offs, wells, misfit, box, temp)


def circular(cells, sides, width, sizes):
    for (axis, dim), size in zip(sides, sizes):
        ends = lax.axis_size(axis) - 1
        length = cells.shape[dim]
        head = lax.slice_in_dim(cells, 0, width, axis=dim)
        tail = lax.slice_in_dim(cells, length - width, length, axis=dim)
        gap = list(cells.shape)
        gap[dim] = size - length - 2 * width
        cells = jnp.concatenate(
            [
                cells,
                lax.ppermute(head, axis, [(i + 1, i) for i in range(ends)]),
                jnp.zeros(gap, cells.dtype),
                lax.ppermute(tail, axis, [(i, i + 1) for i in range(ends)]),
            ],
            axis=dim,
        )
    return cells


def head_kernel(cols_ref, gathered_ref, blocks_ref, heat_ref, grad_ref, head_ref, part_ref):
    row_blocks, per_row, size, _ = blocks_ref.shape
    halves = gathered_ref.shape[2] // size
    for row in range(row_blocks):
        total = jnp.zeros((gathered_ref.shape[1], size), jnp.float32)
        for k in range(per_row):
            col = cols_ref[row, k]
            start = pl.multiple_of((col % halves) * size, size)
            slab = gathered_ref[col // halves, :, pl.ds(start, size)]
            total = total + lax.dot_general(
                slab, blocks_ref[row, k], (((1,), (1,)), ((), ())), preferred_element_type=jnp.float32
            )
        out = slice(row * size, (row + 1) * size)
        head_ref[:, out] = total
        part_ref[:, out] = heat_ref[:, out] + total * grad_ref[:, out].astype(jnp.float32)


def apply_head(block_cols, gathered, blocks, heat, grad):
    cells, width = heat.shape
    vmem = pltpu.VMEM
    return pl.pallas_call(
        head_kernel,
        out_shape=(
            jax.ShapeDtypeStruct((cells, width), jnp.float32),
            jax.ShapeDtypeStruct((cells, width), jnp.float32),
        ),
        in_specs=[pl.BlockSpec(memory_space=pltpu.SMEM)] + [pl.BlockSpec(memory_space=vmem)] * 4,
        out_specs=(pl.BlockSpec(memory_space=vmem), pl.BlockSpec(memory_space=vmem)),
        cost_estimate=pl.CostEstimate(
            flops=2 * cells * width * blocks.shape[1] * blocks.shape[2],
            bytes_accessed=gathered.size * 2 + blocks.size * 2 + cells * width * 14,
            transcendentals=0,
        ),
    )(block_cols, gathered, blocks, heat, grad)


def shards(
    terminal,
    forward_temp,
    conductivity,
    velocity,
    fixed_mask,
    wells,
    misfit,
    head_gradient,
    blocks,
    block_cols,
):
    layers, rows_x, cols_y = conductivity.shape
    keep = 1.0 - fixed_mask.astype(jnp.float32)
    packed = jnp.concatenate([terminal, conductivity[None], velocity, keep[None]], axis=0)
    width = 2
    sizes = (-(-(rows_x + 2 * width) // 8) * 8, -(-(cols_y + 2 * width) // 128) * 128)
    box = circular(packed, (("gx", 2), ("gy", 3)), width, sizes)
    offs = jnp.stack([lax.axis_index("gx") * rows_x, lax.axis_index("gy") * cols_y]).astype(jnp.int32)
    heat_sens, flow_x, flow_y = heat_phase(offs, wells, misfit, box, forward_temp)
    first = lax.axis_index("sec") == 0
    mine = jnp.where(first, flow_x, flow_y)
    other = jnp.where(first, flow_y, flow_x)
    partner = [(0, 1), (1, 0)]
    rounded = (mine + lax.ppermute(other, "sec", partner)).astype(jnp.bfloat16)
    row_blocks, per_row, block_size, _ = blocks.shape
    count = lax.axis_size("gy")
    copies = jnp.broadcast_to(rounded[None], (count,) + rounded.shape)
    gathered = lax.all_to_all(copies, "gy", 0, 0, tiled=False)
    cells = layers * rows_x
    head, partial_sens = apply_head(
        block_cols,
        gathered.reshape(count, cells, cols_y),
        blocks,
        heat_sens.reshape(cells, cols_y),
        head_gradient[0].reshape(cells, cols_y),
    )
    head = head.reshape(layers, rows_x, cols_y)
    partial_sens = partial_sens.reshape(layers, rows_x, cols_y)
    sensitivity = partial_sens + lax.ppermute(partial_sens, "sec", partner)
    return (head[None], sensitivity)


def solution(mesh):
    placed = (
        P("sec", None, "gx", "gy"),
        P(None, "sec", None, "gx", "gy"),
        P(None, "gx", "gy"),
        P(None, None, "gx", "gy"),
        P(None, "gx", "gy"),
        P("sec", None, None),
        P(None, "sec", None),
        P("sec", None, "gx", "gy"),
        P("gy", None, None, None),
        P("gy", None),
    )
    return jax.shard_map(
        shards,
        mesh=mesh,
        in_specs=placed,
        out_specs=(P("sec", None, "gx", "gy"), P(None, "gx", "gy")),
        check_vma=False,
    )
```

```python
import jax
import jax.numpy as jnp
from jax import lax
from jax.sharding import PartitionSpec as P
from jax.experimental import pallas as pl
from jax.experimental.pallas import tpu as pltpu


def extended(cells, sides, width):
    for axis, dim in sides:
        count = lax.axis_size(axis)
        ends = count - 1
        head = lax.slice_in_dim(cells, 0, width, axis=dim)
        tail = lax.slice_in_dim(cells, cells.shape[dim] - width, cells.shape[dim], axis=dim)
        cells = jnp.concatenate(
            [
                lax.ppermute(tail, axis, [(i, (i + 1) % count) for i in range(ends)]),
                cells,
                lax.ppermute(head, axis, [((i + 1) % count, i) for i in range(ends)]),
            ],
            axis=dim,
        )
    return cells


def shifted(padded):
    lead = [(0, 0)] * (padded.ndim - 3)
    deeper = jnp.pad(padded, lead + [(1, 1), (0, 0), (0, 0)])
    centre = deeper[..., 1:-1, 1:-1, 1:-1]
    beside_all = [
        deeper[..., 2:, 1:-1, 1:-1],
        deeper[..., :-2, 1:-1, 1:-1],
        deeper[..., 1:-1, 2:, 1:-1],
        deeper[..., 1:-1, :-2, 1:-1],
        deeper[..., 1:-1, 1:-1, 2:],
        deeper[..., 1:-1, 1:-1, :-2],
    ]
    return (centre, beside_all)


def face_weights(kappa_pad):
    centre, beside_all = shifted(kappa_pad)
    return [
        2.0 * centre * other / jnp.where(centre + other > 0.0, centre + other, 1.0)
        for other in beside_all
    ]


def advance(adjoint_pad, weights, keep, speed_x, speed_y, source):
    centre, beside_all = shifted(adjoint_pad)
    diffusion = weights[0] * (beside_all[0] - centre)
    for face in range(1, 6):
        diffusion = diffusion + weights[face] * (beside_all[face] - centre)
    slope_x = 0.5 * (beside_all[2] - beside_all[3])
    slope_y = 0.5 * (beside_all[4] - beside_all[5])
    updated = keep * (centre + diffusion + speed_x * slope_x + speed_y * slope_y + source)
    return (updated, diffusion, slope_x, slope_y)


def well_sources(wells, misfit_level, layers, rows_x, cols_y, margin):
    start_x = lax.axis_index("gx") * rows_x - margin
    start_y = lax.axis_index("gy") * cols_y - margin
    coord_z = jnp.arange(layers, dtype=jnp.int32)[:, None, None]
    coord_x = (start_x + jnp.arange(rows_x + 2 * margin, dtype=jnp.int32))[None, :, None]
    coord_y = (start_y + jnp.arange(cols_y + 2 * margin, dtype=jnp.int32))[None, None, :]
    well_z = wells[:, :, 0][:, :, None, None, None]
    well_x = wells[:, :, 1][:, :, None, None, None]
    well_y = wells[:, :, 2][:, :, None, None, None]
    matches = (coord_z == well_z) & (coord_x == well_x) & (coord_y == well_y)
    return jnp.sum(jnp.where(matches, misfit_level[:, :, None, None, None], 0.0), axis=1)


def conductance(centre, other):
    return 2.0 * centre * other / jnp.where(centre + other > 0.0, centre + other, 1.0)


def heat_kernel(offs_ref, wells_ref, misfit_ref, box_ref, temp_ref, heat_ref, fx_ref, fy_ref, adj_ref, w_ref):
    tests, layers, rows, cols = adj_ref.shape
    tile_x, tile_y = heat_ref.shape[1], heat_ref.shape[2]
    zero = jnp.zeros((rows, cols), jnp.float32)

    def plane(ref, lead, z):
        above = jnp.where(z + 1 < layers, ref[lead, jnp.minimum(z + 1, layers - 1)], zero)
        below = jnp.where(z > 0, ref[lead, jnp.maximum(z - 1, 0)], zero)
        return ref[lead, z], above, below

    def faces(value, above, below):
        return [
            above,
            below,
            pltpu.roll(value, rows - 1, 0),
            pltpu.roll(value, 1, 0),
            pltpu.roll(value, cols - 1, 1),
            pltpu.roll(value, 1, 1),
        ]

    def weigh(z, carry):
        centre, above, below = plane(box_ref, 2, z)
        for face, other in enumerate(faces(centre, above, below)):
            w_ref[face, z] = conductance(centre, other)
        return carry

    lax.fori_loop(0, layers, weigh, 0)

    def advance(source_ref, level, store):
        def body(z, carry):
            speed_x = box_ref[3, z]
            speed_y = box_ref[4, z]
            keep = box_ref[5, z]
            heat = fx = fy = None
            for test in range(tests):
                centre, above, below = plane(source_ref, test, z)
                beside = faces(centre, above, below)
                diffusion = w_ref[0, z] * (beside[0] - centre)
                for face in range(1, 6):
                    diffusion = diffusion + w_ref[face, z] * (beside[face] - centre)
                slope_x = 0.5 * (beside[2] - beside[3])
                slope_y = 0.5 * (beside[4] - beside[5])
                updated = keep * (centre + diffusion + speed_x * slope_x + speed_y * slope_y)
                if store:
                    adj_ref[test, z] = updated
                temper = temp_ref[level, test, z].astype(jnp.float32)
                terms = [temper * v[:tile_x, :tile_y] for v in (diffusion, slope_x, slope_y)]
                if heat is None:
                    heat, fx, fy = terms
                else:
                    heat, fx, fy = heat + terms[0], fx + terms[1], fy + terms[2]
            if store:
                heat_ref[z], fx_ref[z], fy_ref[z] = heat, fx, fy
            else:
                heat_ref[z] = heat_ref[z] + heat
                fx_ref[z] = fx_ref[z] + fx
                fy_ref[z] = fy_ref[z] + fy
            return carry

        lax.fori_loop(0, layers, body, 0)

    advance(box_ref, 1, True)
    row_ids = lax.broadcasted_iota(jnp.int32, (rows, cols), 0)
    col_ids = lax.broadcasted_iota(jnp.int32, (rows, cols), 1)
    for test in range(tests):
        for well in range(wells_ref.shape[1]):
            depth = wells_ref[test, well, 0]
            at_x = wells_ref[test, well, 1] - offs_ref[0]
            at_y = wells_ref[test, well, 2] - offs_ref[1]
            inside = (at_x >= -2) & (at_x < tile_x + 2) & (at_y >= -2) & (at_y < tile_y + 2)
            amount = jnp.where(inside, misfit_ref[1, test, well], 0.0)
            hit = (row_ids == jnp.where(at_x < 0, at_x + rows, at_x)) & (
                col_ids == jnp.where(at_y < 0, at_y + cols, at_y)
            )
            adj_ref[test, depth] = adj_ref[test, depth] + jnp.where(hit, box_ref[5, depth] * amount, 0.0)
    advance(adj_ref, 0, False)


def heat_phase(offs, wells, misfit, box, temp):
    channels, layers, rows, cols = box.shape
    tests = temp.shape[1]
    tile = temp.shape[3:]
    smem = pl.BlockSpec(memory_space=pltpu.SMEM)
    vmem = pl.BlockSpec(memory_space=pltpu.VMEM)
    out = jax.ShapeDtypeStruct((layers,) + tile, jnp.float32)
    return pl.pallas_call(
        heat_kernel,
        out_shape=(out, out, out),
        in_specs=[smem, smem, smem, vmem, vmem],
        out_specs=(vmem, vmem, vmem),
        scratch_shapes=[
            pltpu.VMEM((tests, layers, rows, cols), jnp.float32),
            pltpu.VMEM((6, layers, rows, cols), jnp.float32),
        ],
    )(offs, wells, misfit, box, temp)


def circular(cells, sides, width, sizes):
    for (axis, dim), size in zip(sides, sizes):
        ends = lax.axis_size(axis) - 1
        length = cells.shape[dim]
        head = lax.slice_in_dim(cells, 0, width, axis=dim)
        tail = lax.slice_in_dim(cells, length - width, length, axis=dim)
        gap = list(cells.shape)
        gap[dim] = size - length - 2 * width
        cells = jnp.concatenate(
            [
                cells,
                lax.ppermute(head, axis, [(i + 1, i) for i in range(ends)]),
                jnp.zeros(gap, cells.dtype),
                lax.ppermute(tail, axis, [(i, i + 1) for i in range(ends)]),
            ],
            axis=dim,
        )
    return cells


def head_kernel(cols_ref, gathered_ref, blocks_ref, heat_ref, grad_ref, head_ref, part_ref):
    row_blocks, per_row, size, _ = blocks_ref.shape
    halves = gathered_ref.shape[2] // size
    for row in range(row_blocks):
        total = jnp.zeros((gathered_ref.shape[1], size), jnp.float32)
        for k in range(per_row):
            col = cols_ref[row, k]
            start = pl.multiple_of((col % halves) * size, size)
            slab = gathered_ref[col // halves, :, pl.ds(start, size)]
            total = total + lax.dot_general(
                slab, blocks_ref[row, k], (((1,), (1,)), ((), ())), preferred_element_type=jnp.float32
            )
        out = slice(row * size, (row + 1) * size)
        head_ref[:, out] = total
        part_ref[:, out] = heat_ref[:, out] + total * grad_ref[:, out].astype(jnp.float32)


def apply_head(block_cols, gathered, blocks, heat, grad):
    cells, width = heat.shape
    vmem = pltpu.VMEM
    return pl.pallas_call(
        head_kernel,
        out_shape=(
            jax.ShapeDtypeStruct((cells, width), jnp.float32),
            jax.ShapeDtypeStruct((cells, width), jnp.float32),
        ),
        in_specs=[pl.BlockSpec(memory_space=pltpu.SMEM)] + [pl.BlockSpec(memory_space=vmem)] * 4,
        out_specs=(pl.BlockSpec(memory_space=vmem), pl.BlockSpec(memory_space=vmem)),
        cost_estimate=pl.CostEstimate(
            flops=2 * cells * width * blocks.shape[1] * blocks.shape[2],
            bytes_accessed=gathered.size * 2 + blocks.size * 2 + cells * width * 14,
            transcendentals=0,
        ),
    )(block_cols, gathered, blocks, heat, grad)


def head_chunk(mine, other, heat_sens, gradient, blocks, block_cols):
    partner = [(0, 1), (1, 0)]
    layers, rows_x, cols_y = mine.shape
    rounded = (mine + lax.ppermute(other, "sec", partner)).astype(jnp.bfloat16)
    count = lax.axis_size("gy")
    copies = jnp.broadcast_to(rounded[None], (count,) + rounded.shape)
    gathered = lax.all_to_all(copies, "gy", 0, 0, tiled=False)
    cells = layers * rows_x
    head, partial_sens = apply_head(
        block_cols,
        gathered.reshape(count, cells, cols_y),
        blocks,
        heat_sens.reshape(cells, cols_y),
        gradient.reshape(cells, cols_y),
    )
    head = head.reshape(layers, rows_x, cols_y)
    partial_sens = partial_sens.reshape(layers, rows_x, cols_y)
    return head, partial_sens + lax.ppermute(partial_sens, "sec", partner)


def shards(
    terminal,
    forward_temp,
    conductivity,
    velocity,
    fixed_mask,
    wells,
    misfit,
    head_gradient,
    blocks,
    block_cols,
):
    layers, rows_x, cols_y = conductivity.shape
    keep = 1.0 - fixed_mask.astype(jnp.float32)
    packed = jnp.concatenate([terminal, conductivity[None], velocity, keep[None]], axis=0)
    width = 2
    sizes = (-(-(rows_x + 2 * width) // 8) * 8, -(-(cols_y + 2 * width) // 128) * 128)
    box = circular(packed, (("gx", 2), ("gy", 3)), width, sizes)
    offs = jnp.stack([lax.axis_index("gx") * rows_x, lax.axis_index("gy") * cols_y]).astype(jnp.int32)
    heat_sens, flow_x, flow_y = heat_phase(offs, wells, misfit, box, forward_temp)
    first = lax.axis_index("sec") == 0
    mine = jnp.where(first, flow_x, flow_y)
    other = jnp.where(first, flow_y, flow_x)
    chunks = 2
    depth = layers // chunks
    heads, sens = [], []
    for part in range(chunks):
        cut = slice(part * depth, (part + 1) * depth)
        head, total = head_chunk(
            mine[cut], other[cut], heat_sens[cut], head_gradient[0, cut], blocks, block_cols
        )
        heads.append(head)
        sens.append(total)
    head = jnp.concatenate(heads, axis=0)
    sensitivity = jnp.concatenate(sens, axis=0)
    return (head[None], sensitivity)


def solution(mesh):
    placed = (
        P("sec", None, "gx", "gy"),
        P(None, "sec", None, "gx", "gy"),
        P(None, "gx", "gy"),
        P(None, None, "gx", "gy"),
        P(None, "gx", "gy"),
        P("sec", None, None),
        P(None, "sec", None),
        P("sec", None, "gx", "gy"),
        P("gy", None, None, None),
        P("gy", None),
    )
    return jax.shard_map(
        shards,
        mesh=mesh,
        in_specs=placed,
        out_specs=(P("sec", None, "gx", "gy"), P(None, "gx", "gy")),
        check_vma=False,
    )
```

```python
import jax
import jax.numpy as jnp
from jax import lax
from jax.sharding import PartitionSpec as P
from jax.experimental import pallas as pl
from jax.experimental.pallas import tpu as pltpu


def extended(cells, sides, width):
    for axis, dim in sides:
        count = lax.axis_size(axis)
        ends = count - 1
        head = lax.slice_in_dim(cells, 0, width, axis=dim)
        tail = lax.slice_in_dim(cells, cells.shape[dim] - width, cells.shape[dim], axis=dim)
        cells = jnp.concatenate(
            [
                lax.ppermute(tail, axis, [(i, (i + 1) % count) for i in range(ends)]),
                cells,
                lax.ppermute(head, axis, [((i + 1) % count, i) for i in range(ends)]),
            ],
            axis=dim,
        )
    return cells


def shifted(padded):
    lead = [(0, 0)] * (padded.ndim - 3)
    deeper = jnp.pad(padded, lead + [(1, 1), (0, 0), (0, 0)])
    centre = deeper[..., 1:-1, 1:-1, 1:-1]
    beside_all = [
        deeper[..., 2:, 1:-1, 1:-1],
        deeper[..., :-2, 1:-1, 1:-1],
        deeper[..., 1:-1, 2:, 1:-1],
        deeper[..., 1:-1, :-2, 1:-1],
        deeper[..., 1:-1, 1:-1, 2:],
        deeper[..., 1:-1, 1:-1, :-2],
    ]
    return (centre, beside_all)


def face_weights(kappa_pad):
    centre, beside_all = shifted(kappa_pad)
    return [
        2.0 * centre * other / jnp.where(centre + other > 0.0, centre + other, 1.0)
        for other in beside_all
    ]


def advance(adjoint_pad, weights, keep, speed_x, speed_y, source):
    centre, beside_all = shifted(adjoint_pad)
    diffusion = weights[0] * (beside_all[0] - centre)
    for face in range(1, 6):
        diffusion = diffusion + weights[face] * (beside_all[face] - centre)
    slope_x = 0.5 * (beside_all[2] - beside_all[3])
    slope_y = 0.5 * (beside_all[4] - beside_all[5])
    updated = keep * (centre + diffusion + speed_x * slope_x + speed_y * slope_y + source)
    return (updated, diffusion, slope_x, slope_y)


def well_sources(wells, misfit_level, layers, rows_x, cols_y, margin):
    start_x = lax.axis_index("gx") * rows_x - margin
    start_y = lax.axis_index("gy") * cols_y - margin
    coord_z = jnp.arange(layers, dtype=jnp.int32)[:, None, None]
    coord_x = (start_x + jnp.arange(rows_x + 2 * margin, dtype=jnp.int32))[None, :, None]
    coord_y = (start_y + jnp.arange(cols_y + 2 * margin, dtype=jnp.int32))[None, None, :]
    well_z = wells[:, :, 0][:, :, None, None, None]
    well_x = wells[:, :, 1][:, :, None, None, None]
    well_y = wells[:, :, 2][:, :, None, None, None]
    matches = (coord_z == well_z) & (coord_x == well_x) & (coord_y == well_y)
    return jnp.sum(jnp.where(matches, misfit_level[:, :, None, None, None], 0.0), axis=1)


def conductance(centre, other):
    return 2.0 * centre * other / jnp.where(centre + other > 0.0, centre + other, 1.0)


def heat_kernel(offs_ref, wells_ref, misfit_ref, box_ref, temp_ref, heat_ref, fx_ref, fy_ref, adj_ref, w_ref):
    tests, layers, rows, cols = adj_ref.shape
    tile_x, tile_y = heat_ref.shape[1], heat_ref.shape[2]
    zero = jnp.zeros((rows, cols), jnp.float32)

    def plane(ref, lead, z):
        above = jnp.where(z + 1 < layers, ref[lead, jnp.minimum(z + 1, layers - 1)], zero)
        below = jnp.where(z > 0, ref[lead, jnp.maximum(z - 1, 0)], zero)
        return ref[lead, z], above, below

    def faces(value, above, below):
        return [
            above,
            below,
            pltpu.roll(value, rows - 1, 0),
            pltpu.roll(value, 1, 0),
            pltpu.roll(value, cols - 1, 1),
            pltpu.roll(value, 1, 1),
        ]

    def weigh(z, carry):
        centre, above, below = plane(box_ref, 2, z)
        for face, other in enumerate(faces(centre, above, below)):
            w_ref[face, z] = conductance(centre, other)
        return carry

    lax.fori_loop(0, layers, weigh, 0)

    def advance(source_ref, level, store):
        def body(z, carry):
            speed_x = box_ref[3, z]
            speed_y = box_ref[4, z]
            keep = box_ref[5, z]
            heat = fx = fy = None
            for test in range(tests):
                centre, above, below = plane(source_ref, test, z)
                beside = faces(centre, above, below)
                diffusion = w_ref[0, z] * (beside[0] - centre)
                for face in range(1, 6):
                    diffusion = diffusion + w_ref[face, z] * (beside[face] - centre)
                slope_x = 0.5 * (beside[2] - beside[3])
                slope_y = 0.5 * (beside[4] - beside[5])
                updated = keep * (centre + diffusion + speed_x * slope_x + speed_y * slope_y)
                if store:
                    adj_ref[test, z] = updated
                temper = temp_ref[level, test, z].astype(jnp.float32)
                terms = [temper * v[:tile_x, :tile_y] for v in (diffusion, slope_x, slope_y)]
                if heat is None:
                    heat, fx, fy = terms
                else:
                    heat, fx, fy = heat + terms[0], fx + terms[1], fy + terms[2]
            if store:
                heat_ref[z], fx_ref[z], fy_ref[z] = heat, fx, fy
            else:
                heat_ref[z] = heat_ref[z] + heat
                fx_ref[z] = fx_ref[z] + fx
                fy_ref[z] = fy_ref[z] + fy
            return carry

        lax.fori_loop(0, layers, body, 0)

    advance(box_ref, 1, True)
    row_ids = lax.broadcasted_iota(jnp.int32, (rows, cols), 0)
    col_ids = lax.broadcasted_iota(jnp.int32, (rows, cols), 1)
    for test in range(tests):
        for well in range(wells_ref.shape[1]):
            depth = wells_ref[test, well, 0]
            at_x = wells_ref[test, well, 1] - offs_ref[0]
            at_y = wells_ref[test, well, 2] - offs_ref[1]
            inside = (at_x >= -2) & (at_x < tile_x + 2) & (at_y >= -2) & (at_y < tile_y + 2)
            amount = jnp.where(inside, misfit_ref[1, test, well], 0.0)
            hit = (row_ids == jnp.where(at_x < 0, at_x + rows, at_x)) & (
                col_ids == jnp.where(at_y < 0, at_y + cols, at_y)
            )
            adj_ref[test, depth] = adj_ref[test, depth] + jnp.where(hit, box_ref[5, depth] * amount, 0.0)
    advance(adj_ref, 0, False)


def heat_phase(offs, wells, misfit, box, temp):
    channels, layers, rows, cols = box.shape
    tests = temp.shape[1]
    tile = temp.shape[3:]
    smem = pl.BlockSpec(memory_space=pltpu.SMEM)
    vmem = pl.BlockSpec(memory_space=pltpu.VMEM)
    out = jax.ShapeDtypeStruct((layers,) + tile, jnp.float32)
    return pl.pallas_call(
        heat_kernel,
        out_shape=(out, out, out),
        in_specs=[smem, smem, smem, vmem, vmem],
        out_specs=(vmem, vmem, vmem),
        scratch_shapes=[
            pltpu.VMEM((tests, layers, rows, cols), jnp.float32),
            pltpu.VMEM((6, layers, rows, cols), jnp.float32),
        ],
    )(offs, wells, misfit, box, temp)


def circular(cells, sides, width, sizes):
    for (axis, dim), size in zip(sides, sizes):
        ends = lax.axis_size(axis) - 1
        length = cells.shape[dim]
        head = lax.slice_in_dim(cells, 0, width, axis=dim)
        tail = lax.slice_in_dim(cells, length - width, length, axis=dim)
        gap = list(cells.shape)
        gap[dim] = size - length - 2 * width
        cells = jnp.concatenate(
            [
                cells,
                lax.ppermute(head, axis, [(i + 1, i) for i in range(ends)]),
                jnp.zeros(gap, cells.dtype),
                lax.ppermute(tail, axis, [(i, i + 1) for i in range(ends)]),
            ],
            axis=dim,
        )
    return cells


def halo_box(cells, width, sizes):
    rows, cols = cells.shape[-2:]
    count_x, count_y = lax.axis_size("gx"), lax.axis_size("gy")

    def fetch(piece, step_x, step_y):
        pairs = [
            ((i + step_x) * count_y + j + step_y, i * count_y + j)
            for i in range(count_x)
            for j in range(count_y)
            if 0 <= i + step_x < count_x and 0 <= j + step_y < count_y
        ]
        return lax.ppermute(piece, ("gx", "gy"), pairs)

    top, bottom = slice(0, width), slice(rows - width, rows)
    left, right = slice(0, width), slice(cols - width, cols)
    lead = cells.shape[:-2]

    def gap(height, length):
        return jnp.zeros(lead + (height, length), cells.dtype)

    def strip(middle, after, before):
        height = middle.shape[-2]
        return jnp.concatenate([middle, after, gap(height, sizes[1] - cols - 2 * width), before], axis=-1)

    body = strip(cells, fetch(cells[..., :, left], 0, 1), fetch(cells[..., :, right], 0, -1))
    below = strip(
        fetch(cells[..., top, :], 1, 0),
        fetch(cells[..., top, left], 1, 1),
        fetch(cells[..., top, right], 1, -1),
    )
    above = strip(
        fetch(cells[..., bottom, :], -1, 0),
        fetch(cells[..., bottom, left], -1, 1),
        fetch(cells[..., bottom, right], -1, -1),
    )
    return jnp.concatenate([body, below, gap(sizes[0] - rows - 2 * width, sizes[1]), above], axis=-2)


def head_kernel(cols_ref, gathered_ref, blocks_ref, heat_ref, grad_ref, head_ref, part_ref):
    row_blocks, per_row, size, _ = blocks_ref.shape
    halves = gathered_ref.shape[2] // size
    for row in range(row_blocks):
        total = jnp.zeros((gathered_ref.shape[1], size), jnp.float32)
        for k in range(per_row):
            col = cols_ref[row, k]
            start = pl.multiple_of((col % halves) * size, size)
            slab = gathered_ref[col // halves, :, pl.ds(start, size)]
            total = total + lax.dot_general(
                slab, blocks_ref[row, k], (((1,), (1,)), ((), ())), preferred_element_type=jnp.float32
            )
        out = slice(row * size, (row + 1) * size)
        head_ref[:, out] = total
        part_ref[:, out] = heat_ref[:, out] + total * grad_ref[:, out].astype(jnp.float32)


def apply_head(block_cols, gathered, blocks, heat, grad):
    cells, width = heat.shape
    vmem = pltpu.VMEM
    return pl.pallas_call(
        head_kernel,
        out_shape=(
            jax.ShapeDtypeStruct((cells, width), jnp.float32),
            jax.ShapeDtypeStruct((cells, width), jnp.float32),
        ),
        in_specs=[pl.BlockSpec(memory_space=pltpu.SMEM)] + [pl.BlockSpec(memory_space=vmem)] * 4,
        out_specs=(pl.BlockSpec(memory_space=vmem), pl.BlockSpec(memory_space=vmem)),
        cost_estimate=pl.CostEstimate(
            flops=2 * cells * width * blocks.shape[1] * blocks.shape[2],
            bytes_accessed=gathered.size * 2 + blocks.size * 2 + cells * width * 14,
            transcendentals=0,
        ),
    )(block_cols, gathered, blocks, heat, grad)


def shards(
    terminal,
    forward_temp,
    conductivity,
    velocity,
    fixed_mask,
    wells,
    misfit,
    head_gradient,
    blocks,
    block_cols,
):
    layers, rows_x, cols_y = conductivity.shape
    keep = 1.0 - fixed_mask.astype(jnp.float32)
    packed = jnp.concatenate([terminal, conductivity[None], velocity, keep[None]], axis=0)
    width = 2
    sizes = (-(-(rows_x + 2 * width) // 8) * 8, -(-(cols_y + 2 * width) // 128) * 128)
    box = halo_box(packed, width, sizes)
    offs = jnp.stack([lax.axis_index("gx") * rows_x, lax.axis_index("gy") * cols_y]).astype(jnp.int32)
    heat_sens, flow_x, flow_y = heat_phase(offs, wells, misfit, box, forward_temp)
    first = lax.axis_index("sec") == 0
    mine = jnp.where(first, flow_x, flow_y)
    other = jnp.where(first, flow_y, flow_x)
    partner = [(0, 1), (1, 0)]
    rounded = (mine + lax.ppermute(other, "sec", partner)).astype(jnp.bfloat16)
    row_blocks, per_row, block_size, _ = blocks.shape
    count = lax.axis_size("gy")
    copies = jnp.broadcast_to(rounded[None], (count,) + rounded.shape)
    gathered = lax.all_to_all(copies, "gy", 0, 0, tiled=False)
    cells = layers * rows_x
    head, partial_sens = apply_head(
        block_cols,
        gathered.reshape(count, cells, cols_y),
        blocks,
        heat_sens.reshape(cells, cols_y),
        head_gradient[0].reshape(cells, cols_y),
    )
    head = head.reshape(layers, rows_x, cols_y)
    partial_sens = partial_sens.reshape(layers, rows_x, cols_y)
    sensitivity = partial_sens + lax.ppermute(partial_sens, "sec", partner)
    return (head[None], sensitivity)


def solution(mesh):
    placed = (
        P("sec", None, "gx", "gy"),
        P(None, "sec", None, "gx", "gy"),
        P(None, "gx", "gy"),
        P(None, None, "gx", "gy"),
        P(None, "gx", "gy"),
        P("sec", None, None),
        P(None, "sec", None),
        P("sec", None, "gx", "gy"),
        P("gy", None, None, None),
        P("gy", None),
    )
    return jax.shard_map(
        shards,
        mesh=mesh,
        in_specs=placed,
        out_specs=(P("sec", None, "gx", "gy"), P(None, "gx", "gy")),
        check_vma=False,
    )
```

```python
import jax
import jax.numpy as jnp
from jax import lax
from jax.sharding import PartitionSpec as P
from jax.experimental import pallas as pl
from jax.experimental.pallas import tpu as pltpu


def extended(cells, sides, width):
    for axis, dim in sides:
        count = lax.axis_size(axis)
        ends = count - 1
        head = lax.slice_in_dim(cells, 0, width, axis=dim)
        tail = lax.slice_in_dim(cells, cells.shape[dim] - width, cells.shape[dim], axis=dim)
        cells = jnp.concatenate(
            [
                lax.ppermute(tail, axis, [(i, (i + 1) % count) for i in range(ends)]),
                cells,
                lax.ppermute(head, axis, [((i + 1) % count, i) for i in range(ends)]),
            ],
            axis=dim,
        )
    return cells


def shifted(padded):
    lead = [(0, 0)] * (padded.ndim - 3)
    deeper = jnp.pad(padded, lead + [(1, 1), (0, 0), (0, 0)])
    centre = deeper[..., 1:-1, 1:-1, 1:-1]
    beside_all = [
        deeper[..., 2:, 1:-1, 1:-1],
        deeper[..., :-2, 1:-1, 1:-1],
        deeper[..., 1:-1, 2:, 1:-1],
        deeper[..., 1:-1, :-2, 1:-1],
        deeper[..., 1:-1, 1:-1, 2:],
        deeper[..., 1:-1, 1:-1, :-2],
    ]
    return (centre, beside_all)


def face_weights(kappa_pad):
    centre, beside_all = shifted(kappa_pad)
    return [
        2.0 * centre * other / jnp.where(centre + other > 0.0, centre + other, 1.0)
        for other in beside_all
    ]


def advance(adjoint_pad, weights, keep, speed_x, speed_y, source):
    centre, beside_all = shifted(adjoint_pad)
    diffusion = weights[0] * (beside_all[0] - centre)
    for face in range(1, 6):
        diffusion = diffusion + weights[face] * (beside_all[face] - centre)
    slope_x = 0.5 * (beside_all[2] - beside_all[3])
    slope_y = 0.5 * (beside_all[4] - beside_all[5])
    updated = keep * (centre + diffusion + speed_x * slope_x + speed_y * slope_y + source)
    return (updated, diffusion, slope_x, slope_y)


def well_sources(wells, misfit_level, layers, rows_x, cols_y, margin):
    start_x = lax.axis_index("gx") * rows_x - margin
    start_y = lax.axis_index("gy") * cols_y - margin
    coord_z = jnp.arange(layers, dtype=jnp.int32)[:, None, None]
    coord_x = (start_x + jnp.arange(rows_x + 2 * margin, dtype=jnp.int32))[None, :, None]
    coord_y = (start_y + jnp.arange(cols_y + 2 * margin, dtype=jnp.int32))[None, None, :]
    well_z = wells[:, :, 0][:, :, None, None, None]
    well_x = wells[:, :, 1][:, :, None, None, None]
    well_y = wells[:, :, 2][:, :, None, None, None]
    matches = (coord_z == well_z) & (coord_x == well_x) & (coord_y == well_y)
    return jnp.sum(jnp.where(matches, misfit_level[:, :, None, None, None], 0.0), axis=1)


def conductance(centre, other):
    return 2.0 * centre * other / jnp.where(centre + other > 0.0, centre + other, 1.0)


def heat_kernel(offs_ref, wells_ref, misfit_ref, box_ref, temp_ref, heat_ref, fx_ref, fy_ref, adj_ref, w_ref):
    tests, layers, rows, cols = adj_ref.shape
    tile_x, tile_y = heat_ref.shape[1], heat_ref.shape[2]
    zero = jnp.zeros((rows, cols), jnp.float32)

    def plane(ref, lead, z):
        above = jnp.where(z + 1 < layers, ref[lead, jnp.minimum(z + 1, layers - 1)], zero)
        below = jnp.where(z > 0, ref[lead, jnp.maximum(z - 1, 0)], zero)
        return ref[lead, z], above, below

    def faces(value, above, below):
        return [
            above,
            below,
            pltpu.roll(value, rows - 1, 0),
            pltpu.roll(value, 1, 0),
            pltpu.roll(value, cols - 1, 1),
            pltpu.roll(value, 1, 1),
        ]

    def weigh(z, carry):
        centre, above, below = plane(box_ref, 2, z)
        for face, other in enumerate(faces(centre, above, below)):
            w_ref[face, z] = conductance(centre, other)
        return carry

    lax.fori_loop(0, layers, weigh, 0)

    def advance(source_ref, level, store):
        def body(z, carry):
            speed_x = box_ref[3, z]
            speed_y = box_ref[4, z]
            keep = box_ref[5, z]
            heat = fx = fy = None
            for test in range(tests):
                centre, above, below = plane(source_ref, test, z)
                beside = faces(centre, above, below)
                diffusion = w_ref[0, z] * (beside[0] - centre)
                for face in range(1, 6):
                    diffusion = diffusion + w_ref[face, z] * (beside[face] - centre)
                slope_x = 0.5 * (beside[2] - beside[3])
                slope_y = 0.5 * (beside[4] - beside[5])
                updated = keep * (centre + diffusion + speed_x * slope_x + speed_y * slope_y)
                if store:
                    adj_ref[test, z] = updated
                temper = temp_ref[level, test, z].astype(jnp.float32)
                terms = [temper * v[:tile_x, :tile_y] for v in (diffusion, slope_x, slope_y)]
                if heat is None:
                    heat, fx, fy = terms
                else:
                    heat, fx, fy = heat + terms[0], fx + terms[1], fy + terms[2]
            if store:
                heat_ref[z], fx_ref[z], fy_ref[z] = heat, fx, fy
            else:
                heat_ref[z] = heat_ref[z] + heat
                fx_ref[z] = fx_ref[z] + fx
                fy_ref[z] = fy_ref[z] + fy
            return carry

        lax.fori_loop(0, layers, body, 0)

    advance(box_ref, 1, True)
    row_ids = lax.broadcasted_iota(jnp.int32, (rows, cols), 0)
    col_ids = lax.broadcasted_iota(jnp.int32, (rows, cols), 1)
    for test in range(tests):
        for well in range(wells_ref.shape[1]):
            depth = wells_ref[test, well, 0]
            at_x = wells_ref[test, well, 1] - offs_ref[0]
            at_y = wells_ref[test, well, 2] - offs_ref[1]
            inside = (at_x >= -2) & (at_x < tile_x + 2) & (at_y >= -2) & (at_y < tile_y + 2)
            amount = jnp.where(inside, misfit_ref[1, test, well], 0.0)
            hit = (row_ids == jnp.where(at_x < 0, at_x + rows, at_x)) & (
                col_ids == jnp.where(at_y < 0, at_y + cols, at_y)
            )
            adj_ref[test, depth] = adj_ref[test, depth] + jnp.where(hit, box_ref[5, depth] * amount, 0.0)
    advance(adj_ref, 0, False)


def heat_phase(offs, wells, misfit, box, temp):
    channels, layers, rows, cols = box.shape
    tests = temp.shape[1]
    tile = temp.shape[3:]
    smem = pl.BlockSpec(memory_space=pltpu.SMEM)
    vmem = pl.BlockSpec(memory_space=pltpu.VMEM)
    out = jax.ShapeDtypeStruct((layers,) + tile, jnp.float32)
    return pl.pallas_call(
        heat_kernel,
        out_shape=(out, out, out),
        in_specs=[smem, smem, smem, vmem, vmem],
        out_specs=(vmem, vmem, vmem),
        scratch_shapes=[
            pltpu.VMEM((tests, layers, rows, cols), jnp.float32),
            pltpu.VMEM((6, layers, rows, cols), jnp.float32),
        ],
    )(offs, wells, misfit, box, temp)


def circular(cells, sides, width, sizes):
    for (axis, dim), size in zip(sides, sizes):
        ends = lax.axis_size(axis) - 1
        length = cells.shape[dim]
        head = lax.slice_in_dim(cells, 0, width, axis=dim)
        tail = lax.slice_in_dim(cells, length - width, length, axis=dim)
        gap = list(cells.shape)
        gap[dim] = size - length - 2 * width
        cells = jnp.concatenate(
            [
                cells,
                lax.ppermute(head, axis, [(i + 1, i) for i in range(ends)]),
                jnp.zeros(gap, cells.dtype),
                lax.ppermute(tail, axis, [(i, i + 1) for i in range(ends)]),
            ],
            axis=dim,
        )
    return cells


def head_kernel(cols_ref, gathered_ref, blocks_ref, heat_ref, grad_ref, head_ref, part_ref):
    row_blocks, per_row, size, _ = blocks_ref.shape
    halves = gathered_ref.shape[2] // size
    for row in range(row_blocks):
        total = jnp.zeros((gathered_ref.shape[1], size), jnp.float32)
        for k in range(per_row):
            col = cols_ref[row, k]
            start = pl.multiple_of((col % halves) * size, size)
            slab = gathered_ref[col // halves, :, pl.ds(start, size)]
            total = total + lax.dot_general(
                slab, blocks_ref[row, k], (((1,), (1,)), ((), ())), preferred_element_type=jnp.float32
            )
        out = slice(row * size, (row + 1) * size)
        head_ref[:, out] = total
        part_ref[:, out] = heat_ref[:, out] + total * grad_ref[:, out].astype(jnp.float32)


def apply_head(block_cols, gathered, blocks, heat, grad):
    cells, width = heat.shape
    vmem = pltpu.VMEM
    return pl.pallas_call(
        head_kernel,
        out_shape=(
            jax.ShapeDtypeStruct((cells, width), jnp.float32),
            jax.ShapeDtypeStruct((cells, width), jnp.float32),
        ),
        in_specs=[pl.BlockSpec(memory_space=pltpu.SMEM)] + [pl.BlockSpec(memory_space=vmem)] * 4,
        out_specs=(pl.BlockSpec(memory_space=vmem), pl.BlockSpec(memory_space=vmem)),
        cost_estimate=pl.CostEstimate(
            flops=2 * cells * width * blocks.shape[1] * blocks.shape[2],
            bytes_accessed=gathered.size * 2 + blocks.size * 2 + cells * width * 14,
            transcendentals=0,
        ),
    )(block_cols, gathered, blocks, heat, grad)


def shards(
    terminal,
    forward_temp,
    conductivity,
    velocity,
    fixed_mask,
    wells,
    misfit,
    head_gradient,
    blocks,
    block_cols,
):
    layers, rows_x, cols_y = conductivity.shape
    keep = 1.0 - fixed_mask.astype(jnp.float32)
    packed = jnp.concatenate([terminal, conductivity[None], velocity, keep[None]], axis=0)
    width = 2
    sizes = (-(-(rows_x + 2 * width) // 8) * 8, -(-(cols_y + 2 * width) // 128) * 128)
    def rows(lo, hi):
        cut = (Ellipsis, slice(lo, hi), slice(None))
        edge_keep = 1.0 - fixed_mask[cut].astype(jnp.float32)
        return jnp.concatenate(
            [terminal[cut], conductivity[None][cut], velocity[cut], edge_keep[None]], axis=0
        )

    ends = lax.axis_size("gx") - 1
    gap = jnp.zeros(packed.shape[:2] + (sizes[0] - rows_x - 2 * width, cols_y), packed.dtype)
    stacked = jnp.concatenate(
        [
            packed,
            lax.ppermute(rows(0, width), "gx", [(i + 1, i) for i in range(ends)]),
            gap,
            lax.ppermute(rows(rows_x - width, rows_x), "gx", [(i, i + 1) for i in range(ends)]),
        ],
        axis=2,
    )
    box = circular(stacked, (("gy", 3),), width, sizes[1:])
    offs = jnp.stack([lax.axis_index("gx") * rows_x, lax.axis_index("gy") * cols_y]).astype(jnp.int32)
    heat_sens, flow_x, flow_y = heat_phase(offs, wells, misfit, box, forward_temp)
    first = lax.axis_index("sec") == 0
    mine = jnp.where(first, flow_x, flow_y)
    other = jnp.where(first, flow_y, flow_x)
    partner = [(0, 1), (1, 0)]
    rounded = (mine + lax.ppermute(other, "sec", partner)).astype(jnp.bfloat16)
    row_blocks, per_row, block_size, _ = blocks.shape
    count = lax.axis_size("gy")
    copies = jnp.broadcast_to(rounded[None], (count,) + rounded.shape)
    gathered = lax.all_to_all(copies, "gy", 0, 0, tiled=False)
    cells = layers * rows_x
    head, partial_sens = apply_head(
        block_cols,
        gathered.reshape(count, cells, cols_y),
        blocks,
        heat_sens.reshape(cells, cols_y),
        head_gradient[0].reshape(cells, cols_y),
    )
    head = head.reshape(layers, rows_x, cols_y)
    partial_sens = partial_sens.reshape(layers, rows_x, cols_y)
    sensitivity = partial_sens + lax.ppermute(partial_sens, "sec", partner)
    return (head[None], sensitivity)


def solution(mesh):
    placed = (
        P("sec", None, "gx", "gy"),
        P(None, "sec", None, "gx", "gy"),
        P(None, "gx", "gy"),
        P(None, None, "gx", "gy"),
        P(None, "gx", "gy"),
        P("sec", None, None),
        P(None, "sec", None),
        P("sec", None, "gx", "gy"),
        P("gy", None, None, None),
        P("gy", None),
    )
    return jax.shard_map(
        shards,
        mesh=mesh,
        in_specs=placed,
        out_specs=(P("sec", None, "gx", "gy"), P(None, "gx", "gy")),
        check_vma=False,
    )
```

```python
import jax
import jax.numpy as jnp
from jax import lax
from jax.sharding import PartitionSpec as P
from jax.experimental import pallas as pl
from jax.experimental.pallas import tpu as pltpu


def extended(cells, sides, width):
    for axis, dim in sides:
        count = lax.axis_size(axis)
        ends = count - 1
        head = lax.slice_in_dim(cells, 0, width, axis=dim)
        tail = lax.slice_in_dim(cells, cells.shape[dim] - width, cells.shape[dim], axis=dim)
        cells = jnp.concatenate(
            [
                lax.ppermute(tail, axis, [(i, (i + 1) % count) for i in range(ends)]),
                cells,
                lax.ppermute(head, axis, [((i + 1) % count, i) for i in range(ends)]),
            ],
            axis=dim,
        )
    return cells


def shifted(padded):
    lead = [(0, 0)] * (padded.ndim - 3)
    deeper = jnp.pad(padded, lead + [(1, 1), (0, 0), (0, 0)])
    centre = deeper[..., 1:-1, 1:-1, 1:-1]
    beside_all = [
        deeper[..., 2:, 1:-1, 1:-1],
        deeper[..., :-2, 1:-1, 1:-1],
        deeper[..., 1:-1, 2:, 1:-1],
        deeper[..., 1:-1, :-2, 1:-1],
        deeper[..., 1:-1, 1:-1, 2:],
        deeper[..., 1:-1, 1:-1, :-2],
    ]
    return (centre, beside_all)


def face_weights(kappa_pad):
    centre, beside_all = shifted(kappa_pad)
    return [
        2.0 * centre * other / jnp.where(centre + other > 0.0, centre + other, 1.0)
        for other in beside_all
    ]


def advance(adjoint_pad, weights, keep, speed_x, speed_y, source):
    centre, beside_all = shifted(adjoint_pad)
    diffusion = weights[0] * (beside_all[0] - centre)
    for face in range(1, 6):
        diffusion = diffusion + weights[face] * (beside_all[face] - centre)
    slope_x = 0.5 * (beside_all[2] - beside_all[3])
    slope_y = 0.5 * (beside_all[4] - beside_all[5])
    updated = keep * (centre + diffusion + speed_x * slope_x + speed_y * slope_y + source)
    return (updated, diffusion, slope_x, slope_y)


def well_sources(wells, misfit_level, layers, rows_x, cols_y, margin):
    start_x = lax.axis_index("gx") * rows_x - margin
    start_y = lax.axis_index("gy") * cols_y - margin
    coord_z = jnp.arange(layers, dtype=jnp.int32)[:, None, None]
    coord_x = (start_x + jnp.arange(rows_x + 2 * margin, dtype=jnp.int32))[None, :, None]
    coord_y = (start_y + jnp.arange(cols_y + 2 * margin, dtype=jnp.int32))[None, None, :]
    well_z = wells[:, :, 0][:, :, None, None, None]
    well_x = wells[:, :, 1][:, :, None, None, None]
    well_y = wells[:, :, 2][:, :, None, None, None]
    matches = (coord_z == well_z) & (coord_x == well_x) & (coord_y == well_y)
    return jnp.sum(jnp.where(matches, misfit_level[:, :, None, None, None], 0.0), axis=1)


def conductance(centre, other):
    return 2.0 * centre * other / jnp.where(centre + other > 0.0, centre + other, 1.0)


def heat_kernel(
    offs_ref, wells_ref, misfit_ref, tile_ref, after_ref, before_ref, side_ref, temp_ref,
    heat_ref, fx_ref, fy_ref, adj_ref, w_ref, box_ref,
):
    channels, layers, tile_x, tile_y = tile_ref.shape
    width = after_ref.shape[2]
    rows = box_ref.shape[2]
    box_ref[:, :, 0:tile_x, 0:tile_y] = tile_ref[...]
    box_ref[:, :, tile_x:tile_x + width, 0:tile_y] = after_ref[...]
    box_ref[:, :, tile_x + width:rows - width, 0:tile_y] = jnp.zeros(
        (channels, layers, rows - tile_x - 2 * width, tile_y), jnp.float32
    )
    box_ref[:, :, rows - width:rows, 0:tile_y] = before_ref[...]
    box_ref[:, :, :, tile_y:] = side_ref[...]
    tests, layers, rows, cols = adj_ref.shape
    tile_x, tile_y = heat_ref.shape[1], heat_ref.shape[2]
    zero = jnp.zeros((rows, cols), jnp.float32)

    def plane(ref, lead, z):
        above = jnp.where(z + 1 < layers, ref[lead, jnp.minimum(z + 1, layers - 1)], zero)
        below = jnp.where(z > 0, ref[lead, jnp.maximum(z - 1, 0)], zero)
        return ref[lead, z], above, below

    def faces(value, above, below):
        return [
            above,
            below,
            pltpu.roll(value, rows - 1, 0),
            pltpu.roll(value, 1, 0),
            pltpu.roll(value, cols - 1, 1),
            pltpu.roll(value, 1, 1),
        ]

    def weigh(z, carry):
        centre, above, below = plane(box_ref, 2, z)
        for face, other in enumerate(faces(centre, above, below)):
            w_ref[face, z] = conductance(centre, other)
        return carry

    lax.fori_loop(0, layers, weigh, 0)

    def advance(source_ref, level, store):
        def body(z, carry):
            speed_x = box_ref[3, z]
            speed_y = box_ref[4, z]
            keep = box_ref[5, z]
            heat = fx = fy = None
            for test in range(tests):
                centre, above, below = plane(source_ref, test, z)
                beside = faces(centre, above, below)
                diffusion = w_ref[0, z] * (beside[0] - centre)
                for face in range(1, 6):
                    diffusion = diffusion + w_ref[face, z] * (beside[face] - centre)
                slope_x = 0.5 * (beside[2] - beside[3])
                slope_y = 0.5 * (beside[4] - beside[5])
                updated = keep * (centre + diffusion + speed_x * slope_x + speed_y * slope_y)
                if store:
                    adj_ref[test, z] = updated
                temper = temp_ref[level, test, z].astype(jnp.float32)
                terms = [temper * v[:tile_x, :tile_y] for v in (diffusion, slope_x, slope_y)]
                if heat is None:
                    heat, fx, fy = terms
                else:
                    heat, fx, fy = heat + terms[0], fx + terms[1], fy + terms[2]
            if store:
                heat_ref[z], fx_ref[z], fy_ref[z] = heat, fx, fy
            else:
                heat_ref[z] = heat_ref[z] + heat
                fx_ref[z] = fx_ref[z] + fx
                fy_ref[z] = fy_ref[z] + fy
            return carry

        lax.fori_loop(0, layers, body, 0)

    advance(box_ref, 1, True)
    row_ids = lax.broadcasted_iota(jnp.int32, (rows, cols), 0)
    col_ids = lax.broadcasted_iota(jnp.int32, (rows, cols), 1)
    for test in range(tests):
        for well in range(wells_ref.shape[1]):
            depth = wells_ref[test, well, 0]
            at_x = wells_ref[test, well, 1] - offs_ref[0]
            at_y = wells_ref[test, well, 2] - offs_ref[1]
            inside = (at_x >= -2) & (at_x < tile_x + 2) & (at_y >= -2) & (at_y < tile_y + 2)
            amount = jnp.where(inside, misfit_ref[1, test, well], 0.0)
            hit = (row_ids == jnp.where(at_x < 0, at_x + rows, at_x)) & (
                col_ids == jnp.where(at_y < 0, at_y + cols, at_y)
            )
            adj_ref[test, depth] = adj_ref[test, depth] + jnp.where(hit, box_ref[5, depth] * amount, 0.0)
    advance(adj_ref, 0, False)


def heat_phase(offs, wells, misfit, tile, after, before, side, temp, rows):
    channels, layers = tile.shape[:2]
    cols = tile.shape[3] + side.shape[3]
    tests = temp.shape[1]
    plane_shape = temp.shape[3:]
    smem = pl.BlockSpec(memory_space=pltpu.SMEM)
    vmem = pl.BlockSpec(memory_space=pltpu.VMEM)
    out = jax.ShapeDtypeStruct((layers,) + plane_shape, jnp.float32)
    return pl.pallas_call(
        heat_kernel,
        out_shape=(out, out, out),
        in_specs=[smem, smem, smem, vmem, vmem, vmem, vmem, vmem],
        out_specs=(vmem, vmem, vmem),
        scratch_shapes=[
            pltpu.VMEM((tests, layers, rows, cols), jnp.float32),
            pltpu.VMEM((6, layers, rows, cols), jnp.float32),
            pltpu.VMEM((channels, layers, rows, cols), jnp.float32),
        ],
    )(offs, wells, misfit, tile, after, before, side, temp)


def circular(cells, sides, width, sizes):
    for (axis, dim), size in zip(sides, sizes):
        ends = lax.axis_size(axis) - 1
        length = cells.shape[dim]
        head = lax.slice_in_dim(cells, 0, width, axis=dim)
        tail = lax.slice_in_dim(cells, length - width, length, axis=dim)
        gap = list(cells.shape)
        gap[dim] = size - length - 2 * width
        cells = jnp.concatenate(
            [
                cells,
                lax.ppermute(head, axis, [(i + 1, i) for i in range(ends)]),
                jnp.zeros(gap, cells.dtype),
                lax.ppermute(tail, axis, [(i, i + 1) for i in range(ends)]),
            ],
            axis=dim,
        )
    return cells


def head_kernel(cols_ref, gathered_ref, blocks_ref, heat_ref, grad_ref, head_ref, part_ref):
    row_blocks, per_row, size, _ = blocks_ref.shape
    halves = gathered_ref.shape[2] // size
    for row in range(row_blocks):
        total = jnp.zeros((gathered_ref.shape[1], size), jnp.float32)
        for k in range(per_row):
            col = cols_ref[row, k]
            start = pl.multiple_of((col % halves) * size, size)
            slab = gathered_ref[col // halves, :, pl.ds(start, size)]
            total = total + lax.dot_general(
                slab, blocks_ref[row, k], (((1,), (1,)), ((), ())), preferred_element_type=jnp.float32
            )
        out = slice(row * size, (row + 1) * size)
        head_ref[:, out] = total
        part_ref[:, out] = heat_ref[:, out] + total * grad_ref[:, out].astype(jnp.float32)


def apply_head(block_cols, gathered, blocks, heat, grad):
    cells, width = heat.shape
    vmem = pltpu.VMEM
    return pl.pallas_call(
        head_kernel,
        out_shape=(
            jax.ShapeDtypeStruct((cells, width), jnp.float32),
            jax.ShapeDtypeStruct((cells, width), jnp.float32),
        ),
        in_specs=[pl.BlockSpec(memory_space=pltpu.SMEM)] + [pl.BlockSpec(memory_space=vmem)] * 4,
        out_specs=(pl.BlockSpec(memory_space=vmem), pl.BlockSpec(memory_space=vmem)),
        cost_estimate=pl.CostEstimate(
            flops=2 * cells * width * blocks.shape[1] * blocks.shape[2],
            bytes_accessed=gathered.size * 2 + blocks.size * 2 + cells * width * 14,
            transcendentals=0,
        ),
    )(block_cols, gathered, blocks, heat, grad)


def shards(
    terminal,
    forward_temp,
    conductivity,
    velocity,
    fixed_mask,
    wells,
    misfit,
    head_gradient,
    blocks,
    block_cols,
):
    layers, rows_x, cols_y = conductivity.shape
    keep = 1.0 - fixed_mask.astype(jnp.float32)
    packed = jnp.concatenate([terminal, conductivity[None], velocity, keep[None]], axis=0)
    width = 2
    sizes = (-(-(rows_x + 2 * width) // 8) * 8, -(-(cols_y + 2 * width) // 128) * 128)
    ends_x = lax.axis_size("gx") - 1
    ends_y = lax.axis_size("gy") - 1
    after = lax.ppermute(packed[:, :, :width], "gx", [(i + 1, i) for i in range(ends_x)])
    before = lax.ppermute(packed[:, :, rows_x - width:], "gx", [(i, i + 1) for i in range(ends_x)])

    def column(cut):
        gap = jnp.zeros(packed.shape[:2] + (sizes[0] - rows_x - 2 * width, width), packed.dtype)
        return jnp.concatenate([packed[..., cut], after[..., cut], gap, before[..., cut]], axis=2)

    side = jnp.concatenate(
        [
            lax.ppermute(column(slice(0, width)), "gy", [(i + 1, i) for i in range(ends_y)]),
            jnp.zeros(packed.shape[:2] + (sizes[0], sizes[1] - cols_y - 2 * width), packed.dtype),
            lax.ppermute(column(slice(cols_y - width, cols_y)), "gy", [(i, i + 1) for i in range(ends_y)]),
        ],
        axis=3,
    )
    offs = jnp.stack([lax.axis_index("gx") * rows_x, lax.axis_index("gy") * cols_y]).astype(jnp.int32)
    heat_sens, flow_x, flow_y = heat_phase(
        offs, wells, misfit, packed, after, before, side, forward_temp, sizes[0]
    )
    first = lax.axis_index("sec") == 0
    mine = jnp.where(first, flow_x, flow_y)
    other = jnp.where(first, flow_y, flow_x)
    partner = [(0, 1), (1, 0)]
    rounded = (mine + lax.ppermute(other, "sec", partner)).astype(jnp.bfloat16)
    row_blocks, per_row, block_size, _ = blocks.shape
    count = lax.axis_size("gy")
    copies = jnp.broadcast_to(rounded[None], (count,) + rounded.shape)
    gathered = lax.all_to_all(copies, "gy", 0, 0, tiled=False)
    cells = layers * rows_x
    head, partial_sens = apply_head(
        block_cols,
        gathered.reshape(count, cells, cols_y),
        blocks,
        heat_sens.reshape(cells, cols_y),
        head_gradient[0].reshape(cells, cols_y),
    )
    head = head.reshape(layers, rows_x, cols_y)
    partial_sens = partial_sens.reshape(layers, rows_x, cols_y)
    sensitivity = partial_sens + lax.ppermute(partial_sens, "sec", partner)
    return (head[None], sensitivity)


def solution(mesh):
    placed = (
        P("sec", None, "gx", "gy"),
        P(None, "sec", None, "gx", "gy"),
        P(None, "gx", "gy"),
        P(None, None, "gx", "gy"),
        P(None, "gx", "gy"),
        P("sec", None, None),
        P(None, "sec", None),
        P("sec", None, "gx", "gy"),
        P("gy", None, None, None),
        P("gy", None),
    )
    return jax.shard_map(
        shards,
        mesh=mesh,
        in_specs=placed,
        out_specs=(P("sec", None, "gx", "gy"), P(None, "gx", "gy")),
        check_vma=False,
    )
```

```python
import jax
import jax.numpy as jnp
from jax import lax
from jax.sharding import PartitionSpec as P
from jax.experimental import pallas as pl
from jax.experimental.pallas import tpu as pltpu


def extended(cells, sides, width):
    for axis, dim in sides:
        count = lax.axis_size(axis)
        ends = count - 1
        head = lax.slice_in_dim(cells, 0, width, axis=dim)
        tail = lax.slice_in_dim(cells, cells.shape[dim] - width, cells.shape[dim], axis=dim)
        cells = jnp.concatenate(
            [
                lax.ppermute(tail, axis, [(i, (i + 1) % count) for i in range(ends)]),
                cells,
                lax.ppermute(head, axis, [((i + 1) % count, i) for i in range(ends)]),
            ],
            axis=dim,
        )
    return cells


def shifted(padded):
    lead = [(0, 0)] * (padded.ndim - 3)
    deeper = jnp.pad(padded, lead + [(1, 1), (0, 0), (0, 0)])
    centre = deeper[..., 1:-1, 1:-1, 1:-1]
    beside_all = [
        deeper[..., 2:, 1:-1, 1:-1],
        deeper[..., :-2, 1:-1, 1:-1],
        deeper[..., 1:-1, 2:, 1:-1],
        deeper[..., 1:-1, :-2, 1:-1],
        deeper[..., 1:-1, 1:-1, 2:],
        deeper[..., 1:-1, 1:-1, :-2],
    ]
    return (centre, beside_all)


def face_weights(kappa_pad):
    centre, beside_all = shifted(kappa_pad)
    return [
        2.0 * centre * other / jnp.where(centre + other > 0.0, centre + other, 1.0)
        for other in beside_all
    ]


def advance(adjoint_pad, weights, keep, speed_x, speed_y, source):
    centre, beside_all = shifted(adjoint_pad)
    diffusion = weights[0] * (beside_all[0] - centre)
    for face in range(1, 6):
        diffusion = diffusion + weights[face] * (beside_all[face] - centre)
    slope_x = 0.5 * (beside_all[2] - beside_all[3])
    slope_y = 0.5 * (beside_all[4] - beside_all[5])
    updated = keep * (centre + diffusion + speed_x * slope_x + speed_y * slope_y + source)
    return (updated, diffusion, slope_x, slope_y)


def well_sources(wells, misfit_level, layers, rows_x, cols_y, margin):
    start_x = lax.axis_index("gx") * rows_x - margin
    start_y = lax.axis_index("gy") * cols_y - margin
    coord_z = jnp.arange(layers, dtype=jnp.int32)[:, None, None]
    coord_x = (start_x + jnp.arange(rows_x + 2 * margin, dtype=jnp.int32))[None, :, None]
    coord_y = (start_y + jnp.arange(cols_y + 2 * margin, dtype=jnp.int32))[None, None, :]
    well_z = wells[:, :, 0][:, :, None, None, None]
    well_x = wells[:, :, 1][:, :, None, None, None]
    well_y = wells[:, :, 2][:, :, None, None, None]
    matches = (coord_z == well_z) & (coord_x == well_x) & (coord_y == well_y)
    return jnp.sum(jnp.where(matches, misfit_level[:, :, None, None, None], 0.0), axis=1)


def conductance(centre, other):
    return 2.0 * centre * other / jnp.where(centre + other > 0.0, centre + other, 1.0)


def heat_kernel(
    offs_ref, wells_ref, misfit_ref, ext_ref, side_ref, temp_ref,
    heat_ref, fx_ref, fy_ref, adj_ref, w_ref, box_ref,
):
    tile_y = ext_ref.shape[3]
    box_ref[:, :, :, 0:tile_y] = ext_ref[...]
    box_ref[:, :, :, tile_y:] = side_ref[...]
    tests, layers, rows, cols = adj_ref.shape
    tile_x, tile_y = heat_ref.shape[1], heat_ref.shape[2]
    zero = jnp.zeros((rows, cols), jnp.float32)

    def plane(ref, lead, z):
        above = jnp.where(z + 1 < layers, ref[lead, jnp.minimum(z + 1, layers - 1)], zero)
        below = jnp.where(z > 0, ref[lead, jnp.maximum(z - 1, 0)], zero)
        return ref[lead, z], above, below

    def faces(value, above, below):
        return [
            above,
            below,
            pltpu.roll(value, rows - 1, 0),
            pltpu.roll(value, 1, 0),
            pltpu.roll(value, cols - 1, 1),
            pltpu.roll(value, 1, 1),
        ]

    def weigh(z, carry):
        centre, above, below = plane(box_ref, 2, z)
        for face, other in enumerate(faces(centre, above, below)):
            w_ref[face, z] = conductance(centre, other)
        return carry

    lax.fori_loop(0, layers, weigh, 0)

    def advance(source_ref, level, store):
        def body(z, carry):
            speed_x = box_ref[3, z]
            speed_y = box_ref[4, z]
            keep = box_ref[5, z]
            heat = fx = fy = None
            for test in range(tests):
                centre, above, below = plane(source_ref, test, z)
                beside = faces(centre, above, below)
                diffusion = w_ref[0, z] * (beside[0] - centre)
                for face in range(1, 6):
                    diffusion = diffusion + w_ref[face, z] * (beside[face] - centre)
                slope_x = 0.5 * (beside[2] - beside[3])
                slope_y = 0.5 * (beside[4] - beside[5])
                updated = keep * (centre + diffusion + speed_x * slope_x + speed_y * slope_y)
                if store:
                    adj_ref[test, z] = updated
                temper = temp_ref[level, test, z].astype(jnp.float32)
                terms = [temper * v[:tile_x, :tile_y] for v in (diffusion, slope_x, slope_y)]
                if heat is None:
                    heat, fx, fy = terms
                else:
                    heat, fx, fy = heat + terms[0], fx + terms[1], fy + terms[2]
            if store:
                heat_ref[z], fx_ref[z], fy_ref[z] = heat, fx, fy
            else:
                heat_ref[z] = heat_ref[z] + heat
                fx_ref[z] = fx_ref[z] + fx
                fy_ref[z] = fy_ref[z] + fy
            return carry

        lax.fori_loop(0, layers, body, 0)

    advance(box_ref, 1, True)
    row_ids = lax.broadcasted_iota(jnp.int32, (rows, cols), 0)
    col_ids = lax.broadcasted_iota(jnp.int32, (rows, cols), 1)
    for test in range(tests):
        for well in range(wells_ref.shape[1]):
            depth = wells_ref[test, well, 0]
            at_x = wells_ref[test, well, 1] - offs_ref[0]
            at_y = wells_ref[test, well, 2] - offs_ref[1]
            inside = (at_x >= -2) & (at_x < tile_x + 2) & (at_y >= -2) & (at_y < tile_y + 2)
            amount = jnp.where(inside, misfit_ref[1, test, well], 0.0)
            hit = (row_ids == jnp.where(at_x < 0, at_x + rows, at_x)) & (
                col_ids == jnp.where(at_y < 0, at_y + cols, at_y)
            )
            adj_ref[test, depth] = adj_ref[test, depth] + jnp.where(hit, box_ref[5, depth] * amount, 0.0)
    advance(adj_ref, 0, False)


def heat_phase(offs, wells, misfit, ext, side, temp):
    channels, layers, rows = ext.shape[:3]
    cols = ext.shape[3] + side.shape[3]
    tests = temp.shape[1]
    plane_shape = temp.shape[3:]
    smem = pl.BlockSpec(memory_space=pltpu.SMEM)
    vmem = pl.BlockSpec(memory_space=pltpu.VMEM)
    out = jax.ShapeDtypeStruct((layers,) + plane_shape, jnp.float32)
    return pl.pallas_call(
        heat_kernel,
        out_shape=(out, out, out),
        in_specs=[smem, smem, smem, vmem, vmem, vmem],
        out_specs=(vmem, vmem, vmem),
        scratch_shapes=[
            pltpu.VMEM((tests, layers, rows, cols), jnp.float32),
            pltpu.VMEM((6, layers, rows, cols), jnp.float32),
            pltpu.VMEM((channels, layers, rows, cols), jnp.float32),
        ],
    )(offs, wells, misfit, ext, side, temp)


def circular(cells, sides, width, sizes):
    for (axis, dim), size in zip(sides, sizes):
        ends = lax.axis_size(axis) - 1
        length = cells.shape[dim]
        head = lax.slice_in_dim(cells, 0, width, axis=dim)
        tail = lax.slice_in_dim(cells, length - width, length, axis=dim)
        gap = list(cells.shape)
        gap[dim] = size - length - 2 * width
        cells = jnp.concatenate(
            [
                cells,
                lax.ppermute(head, axis, [(i + 1, i) for i in range(ends)]),
                jnp.zeros(gap, cells.dtype),
                lax.ppermute(tail, axis, [(i, i + 1) for i in range(ends)]),
            ],
            axis=dim,
        )
    return cells


def head_kernel(cols_ref, gathered_ref, blocks_ref, heat_ref, grad_ref, head_ref, part_ref):
    row_blocks, per_row, size, _ = blocks_ref.shape
    halves = gathered_ref.shape[2] // size
    for row in range(row_blocks):
        total = jnp.zeros((gathered_ref.shape[1], size), jnp.float32)
        for k in range(per_row):
            col = cols_ref[row, k]
            start = pl.multiple_of((col % halves) * size, size)
            slab = gathered_ref[col // halves, :, pl.ds(start, size)]
            total = total + lax.dot_general(
                slab, blocks_ref[row, k], (((1,), (1,)), ((), ())), preferred_element_type=jnp.float32
            )
        out = slice(row * size, (row + 1) * size)
        head_ref[:, out] = total
        part_ref[:, out] = heat_ref[:, out] + total * grad_ref[:, out].astype(jnp.float32)


def apply_head(block_cols, gathered, blocks, heat, grad):
    cells, width = heat.shape
    vmem = pltpu.VMEM
    return pl.pallas_call(
        head_kernel,
        out_shape=(
            jax.ShapeDtypeStruct((cells, width), jnp.float32),
            jax.ShapeDtypeStruct((cells, width), jnp.float32),
        ),
        in_specs=[pl.BlockSpec(memory_space=pltpu.SMEM)] + [pl.BlockSpec(memory_space=vmem)] * 4,
        out_specs=(pl.BlockSpec(memory_space=vmem), pl.BlockSpec(memory_space=vmem)),
        cost_estimate=pl.CostEstimate(
            flops=2 * cells * width * blocks.shape[1] * blocks.shape[2],
            bytes_accessed=gathered.size * 2 + blocks.size * 2 + cells * width * 14,
            transcendentals=0,
        ),
    )(block_cols, gathered, blocks, heat, grad)


def shards(
    terminal,
    forward_temp,
    conductivity,
    velocity,
    fixed_mask,
    wells,
    misfit,
    head_gradient,
    blocks,
    block_cols,
):
    layers, rows_x, cols_y = conductivity.shape
    keep = 1.0 - fixed_mask.astype(jnp.float32)
    packed = jnp.concatenate([terminal, conductivity[None], velocity, keep[None]], axis=0)
    width = 2
    sizes = (-(-(rows_x + 2 * width) // 8) * 8, -(-(cols_y + 2 * width) // 128) * 128)
    ends_x = lax.axis_size("gx") - 1
    ends_y = lax.axis_size("gy") - 1
    after = lax.ppermute(packed[:, :, :width], "gx", [(i + 1, i) for i in range(ends_x)])
    before = lax.ppermute(packed[:, :, rows_x - width:], "gx", [(i, i + 1) for i in range(ends_x)])

    gap = jnp.zeros(packed.shape[:2] + (sizes[0] - rows_x - 2 * width, cols_y), packed.dtype)
    ext = jnp.concatenate([packed, after, gap, before], axis=2)
    side = jnp.concatenate(
        [
            lax.ppermute(ext[..., :width], "gy", [(i + 1, i) for i in range(ends_y)]),
            jnp.zeros(packed.shape[:2] + (sizes[0], sizes[1] - cols_y - 2 * width), packed.dtype),
            lax.ppermute(ext[..., cols_y - width:], "gy", [(i, i + 1) for i in range(ends_y)]),
        ],
        axis=3,
    )
    offs = jnp.stack([lax.axis_index("gx") * rows_x, lax.axis_index("gy") * cols_y]).astype(jnp.int32)
    heat_sens, flow_x, flow_y = heat_phase(offs, wells, misfit, ext, side, forward_temp)
    first = lax.axis_index("sec") == 0
    mine = jnp.where(first, flow_x, flow_y)
    other = jnp.where(first, flow_y, flow_x)
    partner = [(0, 1), (1, 0)]
    rounded = (mine + lax.ppermute(other, "sec", partner)).astype(jnp.bfloat16)
    row_blocks, per_row, block_size, _ = blocks.shape
    count = lax.axis_size("gy")
    copies = jnp.broadcast_to(rounded[None], (count,) + rounded.shape)
    gathered = lax.all_to_all(copies, "gy", 0, 0, tiled=False)
    cells = layers * rows_x
    head, partial_sens = apply_head(
        block_cols,
        gathered.reshape(count, cells, cols_y),
        blocks,
        heat_sens.reshape(cells, cols_y),
        head_gradient[0].reshape(cells, cols_y),
    )
    head = head.reshape(layers, rows_x, cols_y)
    partial_sens = partial_sens.reshape(layers, rows_x, cols_y)
    sensitivity = partial_sens + lax.ppermute(partial_sens, "sec", partner)
    return (head[None], sensitivity)


def solution(mesh):
    placed = (
        P("sec", None, "gx", "gy"),
        P(None, "sec", None, "gx", "gy"),
        P(None, "gx", "gy"),
        P(None, None, "gx", "gy"),
        P(None, "gx", "gy"),
        P("sec", None, None),
        P(None, "sec", None),
        P("sec", None, "gx", "gy"),
        P("gy", None, None, None),
        P("gy", None),
    )
    return jax.shard_map(
        shards,
        mesh=mesh,
        in_specs=placed,
        out_specs=(P("sec", None, "gx", "gy"), P(None, "gx", "gy")),
        check_vma=False,
    )
```

```python
import jax
import jax.numpy as jnp
from jax import lax
from jax.sharding import PartitionSpec as P
from jax.experimental import pallas as pl
from jax.experimental.pallas import tpu as pltpu


def extended(cells, sides, width):
    for axis, dim in sides:
        count = lax.axis_size(axis)
        ends = count - 1
        head = lax.slice_in_dim(cells, 0, width, axis=dim)
        tail = lax.slice_in_dim(cells, cells.shape[dim] - width, cells.shape[dim], axis=dim)
        cells = jnp.concatenate(
            [
                lax.ppermute(tail, axis, [(i, (i + 1) % count) for i in range(ends)]),
                cells,
                lax.ppermute(head, axis, [((i + 1) % count, i) for i in range(ends)]),
            ],
            axis=dim,
        )
    return cells


def shifted(padded):
    lead = [(0, 0)] * (padded.ndim - 3)
    deeper = jnp.pad(padded, lead + [(1, 1), (0, 0), (0, 0)])
    centre = deeper[..., 1:-1, 1:-1, 1:-1]
    beside_all = [
        deeper[..., 2:, 1:-1, 1:-1],
        deeper[..., :-2, 1:-1, 1:-1],
        deeper[..., 1:-1, 2:, 1:-1],
        deeper[..., 1:-1, :-2, 1:-1],
        deeper[..., 1:-1, 1:-1, 2:],
        deeper[..., 1:-1, 1:-1, :-2],
    ]
    return (centre, beside_all)


def face_weights(kappa_pad):
    centre, beside_all = shifted(kappa_pad)
    return [
        2.0 * centre * other / jnp.where(centre + other > 0.0, centre + other, 1.0)
        for other in beside_all
    ]


def advance(adjoint_pad, weights, keep, speed_x, speed_y, source):
    centre, beside_all = shifted(adjoint_pad)
    diffusion = weights[0] * (beside_all[0] - centre)
    for face in range(1, 6):
        diffusion = diffusion + weights[face] * (beside_all[face] - centre)
    slope_x = 0.5 * (beside_all[2] - beside_all[3])
    slope_y = 0.5 * (beside_all[4] - beside_all[5])
    updated = keep * (centre + diffusion + speed_x * slope_x + speed_y * slope_y + source)
    return (updated, diffusion, slope_x, slope_y)


def well_sources(wells, misfit_level, layers, rows_x, cols_y, margin):
    start_x = lax.axis_index("gx") * rows_x - margin
    start_y = lax.axis_index("gy") * cols_y - margin
    coord_z = jnp.arange(layers, dtype=jnp.int32)[:, None, None]
    coord_x = (start_x + jnp.arange(rows_x + 2 * margin, dtype=jnp.int32))[None, :, None]
    coord_y = (start_y + jnp.arange(cols_y + 2 * margin, dtype=jnp.int32))[None, None, :]
    well_z = wells[:, :, 0][:, :, None, None, None]
    well_x = wells[:, :, 1][:, :, None, None, None]
    well_y = wells[:, :, 2][:, :, None, None, None]
    matches = (coord_z == well_z) & (coord_x == well_x) & (coord_y == well_y)
    return jnp.sum(jnp.where(matches, misfit_level[:, :, None, None, None], 0.0), axis=1)


def conductance(centre, other):
    return 2.0 * centre * other / jnp.where(centre + other > 0.0, centre + other, 1.0)


def heat_kernel(
    wells_ref, misfit_ref, tile_ref, after_ref, before_ref, side_ref, temp_ref,
    heat_ref, fx_ref, fy_ref, adj_ref, w_ref, box_ref,
):
    channels, layers, tile_x, tile_y = tile_ref.shape
    width = after_ref.shape[2]
    rows = box_ref.shape[2]
    box_ref[:, :, 0:tile_x, 0:tile_y] = tile_ref[...]
    box_ref[:, :, tile_x:tile_x + width, 0:tile_y] = after_ref[...]
    box_ref[:, :, tile_x + width:rows - width, 0:tile_y] = jnp.zeros(
        (channels, layers, rows - tile_x - 2 * width, tile_y), jnp.float32
    )
    box_ref[:, :, rows - width:rows, 0:tile_y] = before_ref[...]
    box_ref[:, :, :, tile_y:] = side_ref[...]
    tests, layers, rows, cols = adj_ref.shape
    tile_x, tile_y = heat_ref.shape[1], heat_ref.shape[2]
    zero = jnp.zeros((rows, cols), jnp.float32)

    def plane(ref, lead, z):
        above = jnp.where(z + 1 < layers, ref[lead, jnp.minimum(z + 1, layers - 1)], zero)
        below = jnp.where(z > 0, ref[lead, jnp.maximum(z - 1, 0)], zero)
        return ref[lead, z], above, below

    def faces(value, above, below):
        return [
            above,
            below,
            pltpu.roll(value, rows - 1, 0),
            pltpu.roll(value, 1, 0),
            pltpu.roll(value, cols - 1, 1),
            pltpu.roll(value, 1, 1),
        ]

    def weigh(z, carry):
        centre, above, below = plane(box_ref, 2, z)
        for face, other in enumerate(faces(centre, above, below)):
            w_ref[face, z] = conductance(centre, other)
        return carry

    lax.fori_loop(0, layers, weigh, 0)

    def advance(source_ref, level, store):
        def body(z, carry):
            speed_x = box_ref[3, z]
            speed_y = box_ref[4, z]
            keep = box_ref[5, z]
            heat = fx = fy = None
            for test in range(tests):
                centre, above, below = plane(source_ref, test, z)
                beside = faces(centre, above, below)
                diffusion = w_ref[0, z] * (beside[0] - centre)
                for face in range(1, 6):
                    diffusion = diffusion + w_ref[face, z] * (beside[face] - centre)
                slope_x = 0.5 * (beside[2] - beside[3])
                slope_y = 0.5 * (beside[4] - beside[5])
                updated = keep * (centre + diffusion + speed_x * slope_x + speed_y * slope_y)
                if store:
                    adj_ref[test, z] = updated
                temper = temp_ref[level, test, z].astype(jnp.float32)
                first = lax.axis_index("sec") == 0
                mine = jnp.where(first, slope_x, slope_y)
                other = jnp.where(first, slope_y, slope_x)
                terms = [temper * v[:tile_x, :tile_y] for v in (diffusion, mine, other)]
                if heat is None:
                    heat, fx, fy = terms
                else:
                    heat, fx, fy = heat + terms[0], fx + terms[1], fy + terms[2]
            if store:
                heat_ref[z], fx_ref[z], fy_ref[z] = heat, fx, fy
            else:
                heat_ref[z] = heat_ref[z] + heat
                fx_ref[z] = fx_ref[z] + fx
                fy_ref[z] = fy_ref[z] + fy
            return carry

        lax.fori_loop(0, layers, body, 0)

    advance(box_ref, 1, True)
    row_ids = lax.broadcasted_iota(jnp.int32, (rows, cols), 0)
    col_ids = lax.broadcasted_iota(jnp.int32, (rows, cols), 1)
    for test in range(tests):
        for well in range(wells_ref.shape[1]):
            depth = wells_ref[test, well, 0]
            at_x = wells_ref[test, well, 1] - lax.axis_index("gx") * tile_x
            at_y = wells_ref[test, well, 2] - lax.axis_index("gy") * tile_y
            inside = (at_x >= -2) & (at_x < tile_x + 2) & (at_y >= -2) & (at_y < tile_y + 2)
            amount = jnp.where(inside, misfit_ref[1, test, well], 0.0)
            hit = (row_ids == jnp.where(at_x < 0, at_x + rows, at_x)) & (
                col_ids == jnp.where(at_y < 0, at_y + cols, at_y)
            )
            adj_ref[test, depth] = adj_ref[test, depth] + jnp.where(hit, box_ref[5, depth] * amount, 0.0)
    advance(adj_ref, 0, False)


def heat_phase(wells, misfit, tile, after, before, side, temp, rows):
    channels, layers = tile.shape[:2]
    cols = tile.shape[3] + side.shape[3]
    tests = temp.shape[1]
    plane_shape = temp.shape[3:]
    smem = pl.BlockSpec(memory_space=pltpu.SMEM)
    vmem = pl.BlockSpec(memory_space=pltpu.VMEM)
    out = jax.ShapeDtypeStruct((layers,) + plane_shape, jnp.float32)
    return pl.pallas_call(
        heat_kernel,
        out_shape=(out, out, out),
        in_specs=[smem, smem, vmem, vmem, vmem, vmem, vmem],
        out_specs=(vmem, vmem, vmem),
        scratch_shapes=[
            pltpu.VMEM((tests, layers, rows, cols), jnp.float32),
            pltpu.VMEM((6, layers, rows, cols), jnp.float32),
            pltpu.VMEM((channels, layers, rows, cols), jnp.float32),
        ],
    )(wells, misfit, tile, after, before, side, temp)


def circular(cells, sides, width, sizes):
    for (axis, dim), size in zip(sides, sizes):
        ends = lax.axis_size(axis) - 1
        length = cells.shape[dim]
        head = lax.slice_in_dim(cells, 0, width, axis=dim)
        tail = lax.slice_in_dim(cells, length - width, length, axis=dim)
        gap = list(cells.shape)
        gap[dim] = size - length - 2 * width
        cells = jnp.concatenate(
            [
                cells,
                lax.ppermute(head, axis, [(i + 1, i) for i in range(ends)]),
                jnp.zeros(gap, cells.dtype),
                lax.ppermute(tail, axis, [(i, i + 1) for i in range(ends)]),
            ],
            axis=dim,
        )
    return cells


def head_kernel(cols_ref, gathered_ref, blocks_ref, heat_ref, grad_ref, head_ref, part_ref):
    row_blocks, per_row, size, _ = blocks_ref.shape
    halves = gathered_ref.shape[2] // size
    for row in range(row_blocks):
        total = jnp.zeros((gathered_ref.shape[1], size), jnp.float32)
        for k in range(per_row):
            col = cols_ref[row, k]
            start = pl.multiple_of((col % halves) * size, size)
            slab = gathered_ref[col // halves, :, pl.ds(start, size)]
            total = total + lax.dot_general(
                slab, blocks_ref[row, k], (((1,), (1,)), ((), ())), preferred_element_type=jnp.float32
            )
        out = slice(row * size, (row + 1) * size)
        head_ref[:, out] = total
        part_ref[:, out] = heat_ref[:, out] + total * grad_ref[:, out].astype(jnp.float32)


def apply_head(block_cols, gathered, blocks, heat, grad):
    cells, width = heat.shape
    vmem = pltpu.VMEM
    return pl.pallas_call(
        head_kernel,
        out_shape=(
            jax.ShapeDtypeStruct((cells, width), jnp.float32),
            jax.ShapeDtypeStruct((cells, width), jnp.float32),
        ),
        in_specs=[pl.BlockSpec(memory_space=pltpu.SMEM)] + [pl.BlockSpec(memory_space=vmem)] * 4,
        out_specs=(pl.BlockSpec(memory_space=vmem), pl.BlockSpec(memory_space=vmem)),
        cost_estimate=pl.CostEstimate(
            flops=2 * cells * width * blocks.shape[1] * blocks.shape[2],
            bytes_accessed=gathered.size * 2 + blocks.size * 2 + cells * width * 14,
            transcendentals=0,
        ),
    )(block_cols, gathered, blocks, heat, grad)


def shards(
    terminal,
    forward_temp,
    conductivity,
    velocity,
    fixed_mask,
    wells,
    misfit,
    head_gradient,
    blocks,
    block_cols,
):
    layers, rows_x, cols_y = conductivity.shape
    keep = 1.0 - fixed_mask.astype(jnp.float32)
    packed = jnp.concatenate([terminal, conductivity[None], velocity, keep[None]], axis=0)
    width = 2
    sizes = (-(-(rows_x + 2 * width) // 8) * 8, -(-(cols_y + 2 * width) // 128) * 128)
    ends_x = lax.axis_size("gx") - 1
    ends_y = lax.axis_size("gy") - 1
    after = lax.ppermute(packed[:, :, :width], "gx", [(i + 1, i) for i in range(ends_x)])
    before = lax.ppermute(packed[:, :, rows_x - width:], "gx", [(i, i + 1) for i in range(ends_x)])

    def column(cut):
        gap = jnp.zeros(packed.shape[:2] + (sizes[0] - rows_x - 2 * width, width), packed.dtype)
        return jnp.concatenate([packed[..., cut], after[..., cut], gap, before[..., cut]], axis=2)

    side = jnp.concatenate(
        [
            lax.ppermute(column(slice(0, width)), "gy", [(i + 1, i) for i in range(ends_y)]),
            jnp.zeros(packed.shape[:2] + (sizes[0], sizes[1] - cols_y - 2 * width), packed.dtype),
            lax.ppermute(column(slice(cols_y - width, cols_y)), "gy", [(i, i + 1) for i in range(ends_y)]),
        ],
        axis=3,
    )
    heat_sens, mine, other = heat_phase(
        wells, misfit, packed, after, before, side, forward_temp, sizes[0]
    )
    partner = [(0, 1), (1, 0)]
    rounded = (mine + lax.ppermute(other, "sec", partner)).astype(jnp.bfloat16)
    row_blocks, per_row, block_size, _ = blocks.shape
    count = lax.axis_size("gy")
    copies = jnp.broadcast_to(rounded[None], (count,) + rounded.shape)
    gathered = lax.all_to_all(copies, "gy", 0, 0, tiled=False)
    cells = layers * rows_x
    head, partial_sens = apply_head(
        block_cols,
        gathered.reshape(count, cells, cols_y),
        blocks,
        heat_sens.reshape(cells, cols_y),
        head_gradient[0].reshape(cells, cols_y),
    )
    head = head.reshape(layers, rows_x, cols_y)
    partial_sens = partial_sens.reshape(layers, rows_x, cols_y)
    sensitivity = partial_sens + lax.ppermute(partial_sens, "sec", partner)
    return (head[None], sensitivity)


def solution(mesh):
    placed = (
        P("sec", None, "gx", "gy"),
        P(None, "sec", None, "gx", "gy"),
        P(None, "gx", "gy"),
        P(None, None, "gx", "gy"),
        P(None, "gx", "gy"),
        P("sec", None, None),
        P(None, "sec", None),
        P("sec", None, "gx", "gy"),
        P("gy", None, None, None),
        P("gy", None),
    )
    return jax.shard_map(
        shards,
        mesh=mesh,
        in_specs=placed,
        out_specs=(P("sec", None, "gx", "gy"), P(None, "gx", "gy")),
        check_vma=False,
    )
```

```python
import jax
import jax.numpy as jnp
from jax import lax
from jax.sharding import PartitionSpec as P
from jax.experimental import pallas as pl
from jax.experimental.pallas import tpu as pltpu


def extended(cells, sides, width):
    for axis, dim in sides:
        count = lax.axis_size(axis)
        ends = count - 1
        head = lax.slice_in_dim(cells, 0, width, axis=dim)
        tail = lax.slice_in_dim(cells, cells.shape[dim] - width, cells.shape[dim], axis=dim)
        cells = jnp.concatenate(
            [
                lax.ppermute(tail, axis, [(i, (i + 1) % count) for i in range(ends)]),
                cells,
                lax.ppermute(head, axis, [((i + 1) % count, i) for i in range(ends)]),
            ],
            axis=dim,
        )
    return cells


def shifted(padded):
    lead = [(0, 0)] * (padded.ndim - 3)
    deeper = jnp.pad(padded, lead + [(1, 1), (0, 0), (0, 0)])
    centre = deeper[..., 1:-1, 1:-1, 1:-1]
    beside_all = [
        deeper[..., 2:, 1:-1, 1:-1],
        deeper[..., :-2, 1:-1, 1:-1],
        deeper[..., 1:-1, 2:, 1:-1],
        deeper[..., 1:-1, :-2, 1:-1],
        deeper[..., 1:-1, 1:-1, 2:],
        deeper[..., 1:-1, 1:-1, :-2],
    ]
    return (centre, beside_all)


def face_weights(kappa_pad):
    centre, beside_all = shifted(kappa_pad)
    return [
        2.0 * centre * other / jnp.where(centre + other > 0.0, centre + other, 1.0)
        for other in beside_all
    ]


def advance(adjoint_pad, weights, keep, speed_x, speed_y, source):
    centre, beside_all = shifted(adjoint_pad)
    diffusion = weights[0] * (beside_all[0] - centre)
    for face in range(1, 6):
        diffusion = diffusion + weights[face] * (beside_all[face] - centre)
    slope_x = 0.5 * (beside_all[2] - beside_all[3])
    slope_y = 0.5 * (beside_all[4] - beside_all[5])
    updated = keep * (centre + diffusion + speed_x * slope_x + speed_y * slope_y + source)
    return (updated, diffusion, slope_x, slope_y)


def well_sources(wells, misfit_level, layers, rows_x, cols_y, margin):
    start_x = lax.axis_index("gx") * rows_x - margin
    start_y = lax.axis_index("gy") * cols_y - margin
    coord_z = jnp.arange(layers, dtype=jnp.int32)[:, None, None]
    coord_x = (start_x + jnp.arange(rows_x + 2 * margin, dtype=jnp.int32))[None, :, None]
    coord_y = (start_y + jnp.arange(cols_y + 2 * margin, dtype=jnp.int32))[None, None, :]
    well_z = wells[:, :, 0][:, :, None, None, None]
    well_x = wells[:, :, 1][:, :, None, None, None]
    well_y = wells[:, :, 2][:, :, None, None, None]
    matches = (coord_z == well_z) & (coord_x == well_x) & (coord_y == well_y)
    return jnp.sum(jnp.where(matches, misfit_level[:, :, None, None, None], 0.0), axis=1)


def conductance(centre, other):
    return 2.0 * centre * other / jnp.where(centre + other > 0.0, centre + other, 1.0)


def heat_kernel(
    wells_ref, misfit_ref, tile_ref, after_ref, before_ref, side_ref, temp_ref,
    heat_ref, fx_ref, fy_ref, adj_ref, w_ref, box_ref,
):
    channels, layers, tile_x, tile_y = tile_ref.shape
    width = after_ref.shape[2]
    rows = box_ref.shape[2]
    box_ref[:, :, 0:tile_x, 0:tile_y] = tile_ref[...]
    box_ref[:, :, tile_x:tile_x + width, 0:tile_y] = after_ref[...]
    box_ref[:, :, tile_x + width:rows - width, 0:tile_y] = jnp.zeros(
        (channels, layers, rows - tile_x - 2 * width, tile_y), jnp.float32
    )
    box_ref[:, :, rows - width:rows, 0:tile_y] = before_ref[...]
    box_ref[:, :, :, tile_y:] = side_ref[...]
    tests, layers, rows, cols = adj_ref.shape
    tile_x, tile_y = heat_ref.shape[1], heat_ref.shape[2]
    zero = jnp.zeros((rows, cols), jnp.float32)

    def plane(ref, lead, z):
        above = jnp.where(z + 1 < layers, ref[lead, jnp.minimum(z + 1, layers - 1)], zero)
        below = jnp.where(z > 0, ref[lead, jnp.maximum(z - 1, 0)], zero)
        return ref[lead, z], above, below

    def faces(value, above, below):
        return [
            above,
            below,
            pltpu.roll(value, rows - 1, 0),
            pltpu.roll(value, 1, 0),
            pltpu.roll(value, cols - 1, 1),
            pltpu.roll(value, 1, 1),
        ]

    def weigh(z, carry):
        centre, above, below = plane(box_ref, 2, z)
        for face, other in enumerate(faces(centre, above, below)):
            w_ref[face, z] = conductance(centre, other)
        return carry

    lax.fori_loop(0, layers, weigh, 0)

    def advance(source_ref, level, store):
        def body(z, carry):
            speed_x = box_ref[3, z]
            speed_y = box_ref[4, z]
            keep = box_ref[5, z]
            heat = fx = fy = None
            for test in range(tests):
                centre, above, below = plane(source_ref, test, z)
                beside = faces(centre, above, below)
                diffusion = w_ref[0, z] * (beside[0] - centre)
                for face in range(1, 6):
                    diffusion = diffusion + w_ref[face, z] * (beside[face] - centre)
                slope_x = 0.5 * (beside[2] - beside[3])
                slope_y = 0.5 * (beside[4] - beside[5])
                updated = keep * (centre + diffusion + speed_x * slope_x + speed_y * slope_y)
                if store:
                    adj_ref[test, z] = updated
                temper = temp_ref[level, test, z].astype(jnp.float32)
                first = lax.axis_index("sec") == 0
                mine = jnp.where(first, slope_x, slope_y)
                other = jnp.where(first, slope_y, slope_x)
                terms = [temper * v[:tile_x, :tile_y] for v in (diffusion, mine, other)]
                if heat is None:
                    heat, fx, fy = terms
                else:
                    heat, fx, fy = heat + terms[0], fx + terms[1], fy + terms[2]
            if store:
                heat_ref[z], fx_ref[z], fy_ref[z] = heat, fx, fy
            else:
                heat_ref[z] = heat_ref[z] + heat
                fx_ref[z] = fx_ref[z] + fx
                fy_ref[z] = fy_ref[z] + fy
            return carry

        lax.fori_loop(0, layers, body, 0)

    advance(box_ref, 1, True)
    row_ids = lax.broadcasted_iota(jnp.int32, (rows, cols), 0)
    col_ids = lax.broadcasted_iota(jnp.int32, (rows, cols), 1)
    for test in range(tests):
        for well in range(wells_ref.shape[1]):
            depth = wells_ref[test, well, 0]
            at_x = wells_ref[test, well, 1] - lax.axis_index("gx") * tile_x
            at_y = wells_ref[test, well, 2] - lax.axis_index("gy") * tile_y
            inside = (at_x >= -2) & (at_x < tile_x + 2) & (at_y >= -2) & (at_y < tile_y + 2)
            amount = jnp.where(inside, misfit_ref[1, test, well], 0.0)
            hit = (row_ids == jnp.where(at_x < 0, at_x + rows, at_x)) & (
                col_ids == jnp.where(at_y < 0, at_y + cols, at_y)
            )
            adj_ref[test, depth] = adj_ref[test, depth] + jnp.where(hit, box_ref[5, depth] * amount, 0.0)
    advance(adj_ref, 0, False)


def heat_phase(wells, misfit, tile, after, before, side, temp, rows):
    channels, layers = tile.shape[:2]
    cols = tile.shape[3] + side.shape[3]
    tests = temp.shape[1]
    plane_shape = temp.shape[3:]
    smem = pl.BlockSpec(memory_space=pltpu.SMEM)
    vmem = pl.BlockSpec(memory_space=pltpu.VMEM)
    out = jax.ShapeDtypeStruct((layers,) + plane_shape, jnp.float32)
    return pl.pallas_call(
        heat_kernel,
        out_shape=(out, out, out),
        in_specs=[smem, smem, vmem, vmem, vmem, vmem, vmem],
        out_specs=(vmem, vmem, vmem),
        scratch_shapes=[
            pltpu.VMEM((tests, layers, rows, cols), jnp.float32),
            pltpu.VMEM((6, layers, rows, cols), jnp.float32),
            pltpu.VMEM((channels, layers, rows, cols), jnp.float32),
        ],
    )(wells, misfit, tile, after, before, side, temp)


def circular(cells, sides, width, sizes):
    for (axis, dim), size in zip(sides, sizes):
        ends = lax.axis_size(axis) - 1
        length = cells.shape[dim]
        head = lax.slice_in_dim(cells, 0, width, axis=dim)
        tail = lax.slice_in_dim(cells, length - width, length, axis=dim)
        gap = list(cells.shape)
        gap[dim] = size - length - 2 * width
        cells = jnp.concatenate(
            [
                cells,
                lax.ppermute(head, axis, [(i + 1, i) for i in range(ends)]),
                jnp.zeros(gap, cells.dtype),
                lax.ppermute(tail, axis, [(i, i + 1) for i in range(ends)]),
            ],
            axis=dim,
        )
    return cells


def head_kernel(cols_ref, gathered_ref, blocks_ref, heat_ref, grad_ref, head_ref, part_ref):
    row_blocks, per_row, size, _ = blocks_ref.shape
    halves = gathered_ref.shape[2] // size
    for row in range(row_blocks):
        total = jnp.zeros((gathered_ref.shape[1], size), jnp.float32)
        for k in range(per_row):
            col = cols_ref[row, k]
            start = pl.multiple_of((col % halves) * size, size)
            slab = gathered_ref[col // halves, :, pl.ds(start, size)]
            total = total + lax.dot_general(
                slab, blocks_ref[row, k], (((1,), (1,)), ((), ())), preferred_element_type=jnp.float32
            )
        out = slice(row * size, (row + 1) * size)
        head_ref[:, out] = total
        part_ref[:, out] = heat_ref[:, out] + total * grad_ref[:, out].astype(jnp.float32)


def apply_head(block_cols, gathered, blocks, heat, grad):
    cells, width = heat.shape
    vmem = pltpu.VMEM
    return pl.pallas_call(
        head_kernel,
        out_shape=(
            jax.ShapeDtypeStruct((cells, width), jnp.float32),
            jax.ShapeDtypeStruct((cells, width), jnp.float32),
        ),
        in_specs=[pl.BlockSpec(memory_space=pltpu.SMEM)] + [pl.BlockSpec(memory_space=vmem)] * 4,
        out_specs=(pl.BlockSpec(memory_space=vmem), pl.BlockSpec(memory_space=vmem)),
        cost_estimate=pl.CostEstimate(
            flops=2 * cells * width * blocks.shape[1] * blocks.shape[2],
            bytes_accessed=gathered.size * 2 + blocks.size * 2 + cells * width * 14,
            transcendentals=0,
        ),
    )(block_cols, gathered, blocks, heat, grad)


def shards(
    terminal,
    forward_temp,
    conductivity,
    velocity,
    fixed_mask,
    wells,
    misfit,
    head_gradient,
    blocks,
    block_cols,
):
    layers, rows_x, cols_y = conductivity.shape
    keep = 1.0 - fixed_mask.astype(jnp.float32)
    packed = jnp.concatenate([terminal, conductivity[None], velocity, keep[None]], axis=0)
    width = 2
    sizes = (-(-(rows_x + 2 * width) // 8) * 8, -(-(cols_y + 2 * width) // 128) * 128)
    ends_x = lax.axis_size("gx") - 1
    ends_y = lax.axis_size("gy") - 1
    def edge(lo, hi):
        cut = (Ellipsis, slice(lo, hi), slice(None))
        edge_keep = 1.0 - fixed_mask[cut].astype(jnp.float32)
        return jnp.concatenate(
            [terminal[cut], conductivity[None][cut], velocity[cut], edge_keep[None]], axis=0
        )

    after = lax.ppermute(edge(0, width), "gx", [(i + 1, i) for i in range(ends_x)])
    before = lax.ppermute(edge(rows_x - width, rows_x), "gx", [(i, i + 1) for i in range(ends_x)])

    def column(cut):
        gap = jnp.zeros(packed.shape[:2] + (sizes[0] - rows_x - 2 * width, width), packed.dtype)
        return jnp.concatenate([packed[..., cut], after[..., cut], gap, before[..., cut]], axis=2)

    side = jnp.concatenate(
        [
            lax.ppermute(column(slice(0, width)), "gy", [(i + 1, i) for i in range(ends_y)]),
            jnp.zeros(packed.shape[:2] + (sizes[0], sizes[1] - cols_y - 2 * width), packed.dtype),
            lax.ppermute(column(slice(cols_y - width, cols_y)), "gy", [(i, i + 1) for i in range(ends_y)]),
        ],
        axis=3,
    )
    heat_sens, mine, other = heat_phase(
        wells, misfit, packed, after, before, side, forward_temp, sizes[0]
    )
    partner = [(0, 1), (1, 0)]
    rounded = (mine + lax.ppermute(other, "sec", partner)).astype(jnp.bfloat16)
    row_blocks, per_row, block_size, _ = blocks.shape
    count = lax.axis_size("gy")
    copies = jnp.broadcast_to(rounded[None], (count,) + rounded.shape)
    gathered = lax.all_to_all(copies, "gy", 0, 0, tiled=False)
    cells = layers * rows_x
    head, partial_sens = apply_head(
        block_cols,
        gathered.reshape(count, cells, cols_y),
        blocks,
        heat_sens.reshape(cells, cols_y),
        head_gradient[0].reshape(cells, cols_y),
    )
    head = head.reshape(layers, rows_x, cols_y)
    partial_sens = partial_sens.reshape(layers, rows_x, cols_y)
    sensitivity = partial_sens + lax.ppermute(partial_sens, "sec", partner)
    return (head[None], sensitivity)


def solution(mesh):
    placed = (
        P("sec", None, "gx", "gy"),
        P(None, "sec", None, "gx", "gy"),
        P(None, "gx", "gy"),
        P(None, None, "gx", "gy"),
        P(None, "gx", "gy"),
        P("sec", None, None),
        P(None, "sec", None),
        P("sec", None, "gx", "gy"),
        P("gy", None, None, None),
        P("gy", None),
    )
    return jax.shard_map(
        shards,
        mesh=mesh,
        in_specs=placed,
        out_specs=(P("sec", None, "gx", "gy"), P(None, "gx", "gy")),
        check_vma=False,
    )
```

```python
import jax
import jax.numpy as jnp
from jax import lax
from jax.sharding import PartitionSpec as P
from jax.experimental import pallas as pl
from jax.experimental.pallas import tpu as pltpu


def extended(cells, sides, width):
    for axis, dim in sides:
        count = lax.axis_size(axis)
        ends = count - 1
        head = lax.slice_in_dim(cells, 0, width, axis=dim)
        tail = lax.slice_in_dim(cells, cells.shape[dim] - width, cells.shape[dim], axis=dim)
        cells = jnp.concatenate(
            [
                lax.ppermute(tail, axis, [(i, (i + 1) % count) for i in range(ends)]),
                cells,
                lax.ppermute(head, axis, [((i + 1) % count, i) for i in range(ends)]),
            ],
            axis=dim,
        )
    return cells


def shifted(padded):
    lead = [(0, 0)] * (padded.ndim - 3)
    deeper = jnp.pad(padded, lead + [(1, 1), (0, 0), (0, 0)])
    centre = deeper[..., 1:-1, 1:-1, 1:-1]
    beside_all = [
        deeper[..., 2:, 1:-1, 1:-1],
        deeper[..., :-2, 1:-1, 1:-1],
        deeper[..., 1:-1, 2:, 1:-1],
        deeper[..., 1:-1, :-2, 1:-1],
        deeper[..., 1:-1, 1:-1, 2:],
        deeper[..., 1:-1, 1:-1, :-2],
    ]
    return (centre, beside_all)


def face_weights(kappa_pad):
    centre, beside_all = shifted(kappa_pad)
    return [
        2.0 * centre * other / jnp.where(centre + other > 0.0, centre + other, 1.0)
        for other in beside_all
    ]


def advance(adjoint_pad, weights, keep, speed_x, speed_y, source):
    centre, beside_all = shifted(adjoint_pad)
    diffusion = weights[0] * (beside_all[0] - centre)
    for face in range(1, 6):
        diffusion = diffusion + weights[face] * (beside_all[face] - centre)
    slope_x = 0.5 * (beside_all[2] - beside_all[3])
    slope_y = 0.5 * (beside_all[4] - beside_all[5])
    updated = keep * (centre + diffusion + speed_x * slope_x + speed_y * slope_y + source)
    return (updated, diffusion, slope_x, slope_y)


def well_sources(wells, misfit_level, layers, rows_x, cols_y, margin):
    start_x = lax.axis_index("gx") * rows_x - margin
    start_y = lax.axis_index("gy") * cols_y - margin
    coord_z = jnp.arange(layers, dtype=jnp.int32)[:, None, None]
    coord_x = (start_x + jnp.arange(rows_x + 2 * margin, dtype=jnp.int32))[None, :, None]
    coord_y = (start_y + jnp.arange(cols_y + 2 * margin, dtype=jnp.int32))[None, None, :]
    well_z = wells[:, :, 0][:, :, None, None, None]
    well_x = wells[:, :, 1][:, :, None, None, None]
    well_y = wells[:, :, 2][:, :, None, None, None]
    matches = (coord_z == well_z) & (coord_x == well_x) & (coord_y == well_y)
    return jnp.sum(jnp.where(matches, misfit_level[:, :, None, None, None], 0.0), axis=1)


def conductance(centre, other):
    return 2.0 * centre * other / jnp.where(centre + other > 0.0, centre + other, 1.0)


def heat_kernel(
    wells_ref, misfit_ref, tile_ref, after_ref, before_ref, right_ref, left_ref, temp_ref,
    heat_ref, fx_ref, fy_ref, adj_ref, w_ref, box_ref,
):
    channels, layers, tile_x, tile_y = tile_ref.shape
    width = after_ref.shape[2]
    rows = box_ref.shape[2]
    box_ref[:, :, 0:tile_x, 0:tile_y] = tile_ref[...]
    box_ref[:, :, tile_x:tile_x + width, 0:tile_y] = after_ref[...]
    box_ref[:, :, tile_x + width:rows - width, 0:tile_y] = jnp.zeros(
        (channels, layers, rows - tile_x - 2 * width, tile_y), jnp.float32
    )
    box_ref[:, :, rows - width:rows, 0:tile_y] = before_ref[...]
    cols = box_ref.shape[3]
    box_ref[:, :, :, tile_y:tile_y + width] = right_ref[...]
    box_ref[:, :, :, tile_y + width:cols - width] = jnp.zeros(
        (channels, layers, rows, cols - tile_y - 2 * width), jnp.float32
    )
    box_ref[:, :, :, cols - width:] = left_ref[...]
    tests, layers, rows, cols = adj_ref.shape
    tile_x, tile_y = heat_ref.shape[1], heat_ref.shape[2]
    zero = jnp.zeros((rows, cols), jnp.float32)

    def plane(ref, lead, z):
        above = jnp.where(z + 1 < layers, ref[lead, jnp.minimum(z + 1, layers - 1)], zero)
        below = jnp.where(z > 0, ref[lead, jnp.maximum(z - 1, 0)], zero)
        return ref[lead, z], above, below

    def faces(value, above, below):
        return [
            above,
            below,
            pltpu.roll(value, rows - 1, 0),
            pltpu.roll(value, 1, 0),
            pltpu.roll(value, cols - 1, 1),
            pltpu.roll(value, 1, 1),
        ]

    def weigh(z, carry):
        centre, above, below = plane(box_ref, 2, z)
        for face, other in enumerate(faces(centre, above, below)):
            w_ref[face, z] = conductance(centre, other)
        return carry

    lax.fori_loop(0, layers, weigh, 0)

    def advance(source_ref, level, store):
        def body(z, carry):
            speed_x = box_ref[3, z]
            speed_y = box_ref[4, z]
            keep = box_ref[5, z]
            heat = fx = fy = None
            for test in range(tests):
                centre, above, below = plane(source_ref, test, z)
                beside = faces(centre, above, below)
                diffusion = w_ref[0, z] * (beside[0] - centre)
                for face in range(1, 6):
                    diffusion = diffusion + w_ref[face, z] * (beside[face] - centre)
                slope_x = 0.5 * (beside[2] - beside[3])
                slope_y = 0.5 * (beside[4] - beside[5])
                updated = keep * (centre + diffusion + speed_x * slope_x + speed_y * slope_y)
                if store:
                    adj_ref[test, z] = updated
                temper = temp_ref[level, test, z].astype(jnp.float32)
                first = lax.axis_index("sec") == 0
                mine = jnp.where(first, slope_x, slope_y)
                other = jnp.where(first, slope_y, slope_x)
                terms = [temper * v[:tile_x, :tile_y] for v in (diffusion, mine, other)]
                if heat is None:
                    heat, fx, fy = terms
                else:
                    heat, fx, fy = heat + terms[0], fx + terms[1], fy + terms[2]
            if store:
                heat_ref[z], fx_ref[z], fy_ref[z] = heat, fx, fy
            else:
                heat_ref[z] = heat_ref[z] + heat
                fx_ref[z] = fx_ref[z] + fx
                fy_ref[z] = fy_ref[z] + fy
            return carry

        lax.fori_loop(0, layers, body, 0)

    advance(box_ref, 1, True)
    row_ids = lax.broadcasted_iota(jnp.int32, (rows, cols), 0)
    col_ids = lax.broadcasted_iota(jnp.int32, (rows, cols), 1)
    for test in range(tests):
        for well in range(wells_ref.shape[1]):
            depth = wells_ref[test, well, 0]
            at_x = wells_ref[test, well, 1] - lax.axis_index("gx") * tile_x
            at_y = wells_ref[test, well, 2] - lax.axis_index("gy") * tile_y
            inside = (at_x >= -2) & (at_x < tile_x + 2) & (at_y >= -2) & (at_y < tile_y + 2)
            amount = jnp.where(inside, misfit_ref[1, test, well], 0.0)
            hit = (row_ids == jnp.where(at_x < 0, at_x + rows, at_x)) & (
                col_ids == jnp.where(at_y < 0, at_y + cols, at_y)
            )
            adj_ref[test, depth] = adj_ref[test, depth] + jnp.where(hit, box_ref[5, depth] * amount, 0.0)
    advance(adj_ref, 0, False)


def heat_phase(wells, misfit, tile, after, before, right, left, temp, rows, cols):
    channels, layers = tile.shape[:2]
    tests = temp.shape[1]
    plane_shape = temp.shape[3:]
    smem = pl.BlockSpec(memory_space=pltpu.SMEM)
    vmem = pl.BlockSpec(memory_space=pltpu.VMEM)
    out = jax.ShapeDtypeStruct((layers,) + plane_shape, jnp.float32)
    return pl.pallas_call(
        heat_kernel,
        out_shape=(out, out, out),
        in_specs=[smem, smem, vmem, vmem, vmem, vmem, vmem, vmem],
        out_specs=(vmem, vmem, vmem),
        scratch_shapes=[
            pltpu.VMEM((tests, layers, rows, cols), jnp.float32),
            pltpu.VMEM((6, layers, rows, cols), jnp.float32),
            pltpu.VMEM((channels, layers, rows, cols), jnp.float32),
        ],
    )(wells, misfit, tile, after, before, right, left, temp)


def circular(cells, sides, width, sizes):
    for (axis, dim), size in zip(sides, sizes):
        ends = lax.axis_size(axis) - 1
        length = cells.shape[dim]
        head = lax.slice_in_dim(cells, 0, width, axis=dim)
        tail = lax.slice_in_dim(cells, length - width, length, axis=dim)
        gap = list(cells.shape)
        gap[dim] = size - length - 2 * width
        cells = jnp.concatenate(
            [
                cells,
                lax.ppermute(head, axis, [(i + 1, i) for i in range(ends)]),
                jnp.zeros(gap, cells.dtype),
                lax.ppermute(tail, axis, [(i, i + 1) for i in range(ends)]),
            ],
            axis=dim,
        )
    return cells


def head_kernel(cols_ref, gathered_ref, blocks_ref, heat_ref, grad_ref, head_ref, part_ref):
    row_blocks, per_row, size, _ = blocks_ref.shape
    halves = gathered_ref.shape[2] // size
    for row in range(row_blocks):
        total = jnp.zeros((gathered_ref.shape[1], size), jnp.float32)
        for k in range(per_row):
            col = cols_ref[row, k]
            start = pl.multiple_of((col % halves) * size, size)
            slab = gathered_ref[col // halves, :, pl.ds(start, size)]
            total = total + lax.dot_general(
                slab, blocks_ref[row, k], (((1,), (1,)), ((), ())), preferred_element_type=jnp.float32
            )
        out = slice(row * size, (row + 1) * size)
        head_ref[:, out] = total
        part_ref[:, out] = heat_ref[:, out] + total * grad_ref[:, out].astype(jnp.float32)


def apply_head(block_cols, gathered, blocks, heat, grad):
    cells, width = heat.shape
    vmem = pltpu.VMEM
    return pl.pallas_call(
        head_kernel,
        out_shape=(
            jax.ShapeDtypeStruct((cells, width), jnp.float32),
            jax.ShapeDtypeStruct((cells, width), jnp.float32),
        ),
        in_specs=[pl.BlockSpec(memory_space=pltpu.SMEM)] + [pl.BlockSpec(memory_space=vmem)] * 4,
        out_specs=(pl.BlockSpec(memory_space=vmem), pl.BlockSpec(memory_space=vmem)),
        cost_estimate=pl.CostEstimate(
            flops=2 * cells * width * blocks.shape[1] * blocks.shape[2],
            bytes_accessed=gathered.size * 2 + blocks.size * 2 + cells * width * 14,
            transcendentals=0,
        ),
    )(block_cols, gathered, blocks, heat, grad)


def shards(
    terminal,
    forward_temp,
    conductivity,
    velocity,
    fixed_mask,
    wells,
    misfit,
    head_gradient,
    blocks,
    block_cols,
):
    layers, rows_x, cols_y = conductivity.shape
    keep = 1.0 - fixed_mask.astype(jnp.float32)
    packed = jnp.concatenate([terminal, conductivity[None], velocity, keep[None]], axis=0)
    width = 2
    sizes = (-(-(rows_x + 2 * width) // 8) * 8, -(-(cols_y + 2 * width) // 128) * 128)
    ends_x = lax.axis_size("gx") - 1
    ends_y = lax.axis_size("gy") - 1
    after = lax.ppermute(packed[:, :, :width], "gx", [(i + 1, i) for i in range(ends_x)])
    before = lax.ppermute(packed[:, :, rows_x - width:], "gx", [(i, i + 1) for i in range(ends_x)])

    def column(cut):
        gap = jnp.zeros(packed.shape[:2] + (sizes[0] - rows_x - 2 * width, width), packed.dtype)
        return jnp.concatenate([packed[..., cut], after[..., cut], gap, before[..., cut]], axis=2)

    right = lax.ppermute(column(slice(0, width)), "gy", [(i + 1, i) for i in range(ends_y)])
    left = lax.ppermute(column(slice(cols_y - width, cols_y)), "gy", [(i, i + 1) for i in range(ends_y)])
    heat_sens, mine, other = heat_phase(
        wells, misfit, packed, after, before, right, left, forward_temp, sizes[0], sizes[1]
    )
    partner = [(0, 1), (1, 0)]
    rounded = (mine + lax.ppermute(other, "sec", partner)).astype(jnp.bfloat16)
    row_blocks, per_row, block_size, _ = blocks.shape
    count = lax.axis_size("gy")
    copies = jnp.broadcast_to(rounded[None], (count,) + rounded.shape)
    gathered = lax.all_to_all(copies, "gy", 0, 0, tiled=False)
    cells = layers * rows_x
    head, partial_sens = apply_head(
        block_cols,
        gathered.reshape(count, cells, cols_y),
        blocks,
        heat_sens.reshape(cells, cols_y),
        head_gradient[0].reshape(cells, cols_y),
    )
    head = head.reshape(layers, rows_x, cols_y)
    partial_sens = partial_sens.reshape(layers, rows_x, cols_y)
    sensitivity = partial_sens + lax.ppermute(partial_sens, "sec", partner)
    return (head[None], sensitivity)


def solution(mesh):
    placed = (
        P("sec", None, "gx", "gy"),
        P(None, "sec", None, "gx", "gy"),
        P(None, "gx", "gy"),
        P(None, None, "gx", "gy"),
        P(None, "gx", "gy"),
        P("sec", None, None),
        P(None, "sec", None),
        P("sec", None, "gx", "gy"),
        P("gy", None, None, None),
        P("gy", None),
    )
    return jax.shard_map(
        shards,
        mesh=mesh,
        in_specs=placed,
        out_specs=(P("sec", None, "gx", "gy"), P(None, "gx", "gy")),
        check_vma=False,
    )
```

```python
import jax
import jax.numpy as jnp
from jax import lax
from jax.sharding import PartitionSpec as P
from jax.experimental import pallas as pl
from jax.experimental.pallas import tpu as pltpu


def extended(cells, sides, width):
    for axis, dim in sides:
        count = lax.axis_size(axis)
        ends = count - 1
        head = lax.slice_in_dim(cells, 0, width, axis=dim)
        tail = lax.slice_in_dim(cells, cells.shape[dim] - width, cells.shape[dim], axis=dim)
        cells = jnp.concatenate(
            [
                lax.ppermute(tail, axis, [(i, (i + 1) % count) for i in range(ends)]),
                cells,
                lax.ppermute(head, axis, [((i + 1) % count, i) for i in range(ends)]),
            ],
            axis=dim,
        )
    return cells


def shifted(padded):
    lead = [(0, 0)] * (padded.ndim - 3)
    deeper = jnp.pad(padded, lead + [(1, 1), (0, 0), (0, 0)])
    centre = deeper[..., 1:-1, 1:-1, 1:-1]
    beside_all = [
        deeper[..., 2:, 1:-1, 1:-1],
        deeper[..., :-2, 1:-1, 1:-1],
        deeper[..., 1:-1, 2:, 1:-1],
        deeper[..., 1:-1, :-2, 1:-1],
        deeper[..., 1:-1, 1:-1, 2:],
        deeper[..., 1:-1, 1:-1, :-2],
    ]
    return (centre, beside_all)


def face_weights(kappa_pad):
    centre, beside_all = shifted(kappa_pad)
    return [
        2.0 * centre * other / jnp.where(centre + other > 0.0, centre + other, 1.0)
        for other in beside_all
    ]


def advance(adjoint_pad, weights, keep, speed_x, speed_y, source):
    centre, beside_all = shifted(adjoint_pad)
    diffusion = weights[0] * (beside_all[0] - centre)
    for face in range(1, 6):
        diffusion = diffusion + weights[face] * (beside_all[face] - centre)
    slope_x = 0.5 * (beside_all[2] - beside_all[3])
    slope_y = 0.5 * (beside_all[4] - beside_all[5])
    updated = keep * (centre + diffusion + speed_x * slope_x + speed_y * slope_y + source)
    return (updated, diffusion, slope_x, slope_y)


def well_sources(wells, misfit_level, layers, rows_x, cols_y, margin):
    start_x = lax.axis_index("gx") * rows_x - margin
    start_y = lax.axis_index("gy") * cols_y - margin
    coord_z = jnp.arange(layers, dtype=jnp.int32)[:, None, None]
    coord_x = (start_x + jnp.arange(rows_x + 2 * margin, dtype=jnp.int32))[None, :, None]
    coord_y = (start_y + jnp.arange(cols_y + 2 * margin, dtype=jnp.int32))[None, None, :]
    well_z = wells[:, :, 0][:, :, None, None, None]
    well_x = wells[:, :, 1][:, :, None, None, None]
    well_y = wells[:, :, 2][:, :, None, None, None]
    matches = (coord_z == well_z) & (coord_x == well_x) & (coord_y == well_y)
    return jnp.sum(jnp.where(matches, misfit_level[:, :, None, None, None], 0.0), axis=1)


def conductance(centre, other):
    return 2.0 * centre * other / jnp.where(centre + other > 0.0, centre + other, 1.0)


def heat_kernel(
    wells_ref, misfit_ref, tile_ref, after_ref, before_ref, side_ref, temp_ref,
    heat_ref, fx_ref, fy_ref, adj_ref, w_ref, box_ref,
):
    channels, layers, tile_x, tile_y = tile_ref.shape
    width = after_ref.shape[2]
    rows = box_ref.shape[2]
    box_ref[:, :, 0:tile_x, 0:tile_y] = tile_ref[...]
    box_ref[:, :, tile_x:tile_x + width, 0:tile_y] = after_ref[...]
    box_ref[:, :, tile_x + width:rows - width, 0:tile_y] = jnp.zeros(
        (channels, layers, rows - tile_x - 2 * width, tile_y), jnp.float32
    )
    box_ref[:, :, rows - width:rows, 0:tile_y] = before_ref[...]
    box_ref[:, :, :, tile_y:] = side_ref[...]
    tests, layers, rows, cols = adj_ref.shape
    tile_x, tile_y = heat_ref.shape[1], heat_ref.shape[2]
    zero = jnp.zeros((rows, cols), jnp.float32)

    def plane(ref, lead, z):
        above = jnp.where(z + 1 < layers, ref[lead, jnp.minimum(z + 1, layers - 1)], zero)
        below = jnp.where(z > 0, ref[lead, jnp.maximum(z - 1, 0)], zero)
        return ref[lead, z], above, below

    def faces(value, above, below):
        return [
            above,
            below,
            pltpu.roll(value, rows - 1, 0),
            pltpu.roll(value, 1, 0),
            pltpu.roll(value, cols - 1, 1),
            pltpu.roll(value, 1, 1),
        ]

    def weigh(z, carry):
        centre, above, below = plane(box_ref, 2, z)
        for face, other in enumerate(faces(centre, above, below)):
            w_ref[face, z] = conductance(centre, other)
        return carry

    lax.fori_loop(0, layers, weigh, 0)

    def advance(source_ref, level, store):
        def body(z, carry):
            speed_x = box_ref[3, z]
            speed_y = box_ref[4, z]
            keep = box_ref[5, z]
            heat = fx = fy = None
            for test in range(tests):
                centre, above, below = plane(source_ref, test, z)
                beside = faces(centre, above, below)
                diffusion = w_ref[0, z] * (beside[0] - centre)
                for face in range(1, 6):
                    diffusion = diffusion + w_ref[face, z] * (beside[face] - centre)
                slope_x = 0.5 * (beside[2] - beside[3])
                slope_y = 0.5 * (beside[4] - beside[5])
                updated = keep * (centre + diffusion + speed_x * slope_x + speed_y * slope_y)
                if store:
                    adj_ref[test, z] = updated
                temper = temp_ref[level, test, z].astype(jnp.float32)
                first = lax.axis_index("sec") == 0
                mine = jnp.where(first, slope_x, slope_y)
                other = jnp.where(first, slope_y, slope_x)
                terms = [temper * v[:tile_x, :tile_y] for v in (diffusion, mine, other)]
                if heat is None:
                    heat, fx, fy = terms
                else:
                    heat, fx, fy = heat + terms[0], fx + terms[1], fy + terms[2]
            if store:
                heat_ref[z], fx_ref[z], fy_ref[z] = heat, fx, fy
            else:
                heat_ref[z] = heat_ref[z] + heat
                fx_ref[z] = fx_ref[z] + fx
                fy_ref[z] = fy_ref[z] + fy
            return carry

        lax.fori_loop(0, layers, body, 0)

    advance(box_ref, 1, True)
    row_ids = lax.broadcasted_iota(jnp.int32, (rows, cols), 0)
    col_ids = lax.broadcasted_iota(jnp.int32, (rows, cols), 1)
    for test in range(tests):
        for well in range(wells_ref.shape[1]):
            depth = wells_ref[test, well, 0]
            at_x = wells_ref[test, well, 1] - lax.axis_index("gx") * tile_x
            at_y = wells_ref[test, well, 2] - lax.axis_index("gy") * tile_y
            inside = (at_x >= -2) & (at_x < tile_x + 2) & (at_y >= -2) & (at_y < tile_y + 2)
            amount = jnp.where(inside, misfit_ref[1, test, well], 0.0)
            hit = (row_ids == jnp.where(at_x < 0, at_x + rows, at_x)) & (
                col_ids == jnp.where(at_y < 0, at_y + cols, at_y)
            )
            adj_ref[test, depth] = adj_ref[test, depth] + jnp.where(hit, box_ref[5, depth] * amount, 0.0)
    advance(adj_ref, 0, False)


def heat_phase(wells, misfit, tile, after, before, side, temp, rows):
    channels, layers = tile.shape[:2]
    cols = tile.shape[3] + side.shape[3]
    tests = temp.shape[1]
    plane_shape = temp.shape[3:]
    smem = pl.BlockSpec(memory_space=pltpu.SMEM)
    vmem = pl.BlockSpec(memory_space=pltpu.VMEM)
    out = jax.ShapeDtypeStruct((layers,) + plane_shape, jnp.float32)
    return pl.pallas_call(
        heat_kernel,
        out_shape=(out, out, out),
        in_specs=[smem, smem, vmem, vmem, vmem, vmem, vmem],
        out_specs=(vmem, vmem, vmem),
        scratch_shapes=[
            pltpu.VMEM((tests, layers, rows, cols), jnp.float32),
            pltpu.VMEM((6, layers, rows, cols), jnp.float32),
            pltpu.VMEM((channels, layers, rows, cols), jnp.float32),
        ],
    )(wells, misfit, tile, after, before, side, temp)


def circular(cells, sides, width, sizes):
    for (axis, dim), size in zip(sides, sizes):
        ends = lax.axis_size(axis) - 1
        length = cells.shape[dim]
        head = lax.slice_in_dim(cells, 0, width, axis=dim)
        tail = lax.slice_in_dim(cells, length - width, length, axis=dim)
        gap = list(cells.shape)
        gap[dim] = size - length - 2 * width
        cells = jnp.concatenate(
            [
                cells,
                lax.ppermute(head, axis, [(i + 1, i) for i in range(ends)]),
                jnp.zeros(gap, cells.dtype),
                lax.ppermute(tail, axis, [(i, i + 1) for i in range(ends)]),
            ],
            axis=dim,
        )
    return cells


def head_kernel(cols_ref, gathered_ref, blocks_ref, heat_ref, grad_ref, head_ref, part_ref, slabs, sems):
    row_blocks, per_row, size, _ = blocks_ref.shape
    halves = gathered_ref.shape[2] // size
    copies = []
    for row in range(row_blocks):
        for k in range(per_row):
            col = cols_ref[row, k]
            start = pl.multiple_of((col % halves) * size, size)
            copy = pltpu.make_async_copy(
                gathered_ref.at[col // halves, :, pl.ds(start, size)],
                slabs.at[row * per_row + k],
                sems.at[row * per_row + k],
            )
            copy.start()
            copies.append(copy)
    for row in range(row_blocks):
        total = jnp.zeros((gathered_ref.shape[1], size), jnp.float32)
        for k in range(per_row):
            copies[row * per_row + k].wait()
            total = total + lax.dot_general(
                slabs[row * per_row + k], blocks_ref[row, k], (((1,), (1,)), ((), ())),
                preferred_element_type=jnp.float32,
            )
        out = slice(row * size, (row + 1) * size)
        head_ref[:, out] = total
        part_ref[:, out] = heat_ref[:, out] + total * grad_ref[:, out].astype(jnp.float32)


def apply_head(block_cols, gathered, blocks, heat, grad):
    cells, width = heat.shape
    vmem = pltpu.VMEM
    return pl.pallas_call(
        head_kernel,
        out_shape=(
            jax.ShapeDtypeStruct((cells, width), jnp.float32),
            jax.ShapeDtypeStruct((cells, width), jnp.float32),
        ),
        in_specs=[pl.BlockSpec(memory_space=pltpu.SMEM), pl.BlockSpec(memory_space=pl.ANY)]
        + [pl.BlockSpec(memory_space=vmem)] * 3,
        out_specs=(pl.BlockSpec(memory_space=vmem), pl.BlockSpec(memory_space=vmem)),
        scratch_shapes=[
            pltpu.VMEM((blocks.shape[0] * blocks.shape[1], cells, blocks.shape[2]), gathered.dtype),
            pltpu.SemaphoreType.DMA((blocks.shape[0] * blocks.shape[1],)),
        ],
        cost_estimate=pl.CostEstimate(
            flops=2 * cells * width * blocks.shape[1] * blocks.shape[2],
            bytes_accessed=gathered.size * 2 + blocks.size * 2 + cells * width * 14,
            transcendentals=0,
        ),
    )(block_cols, gathered, blocks, heat, grad)


def shards(
    terminal,
    forward_temp,
    conductivity,
    velocity,
    fixed_mask,
    wells,
    misfit,
    head_gradient,
    blocks,
    block_cols,
):
    layers, rows_x, cols_y = conductivity.shape
    keep = 1.0 - fixed_mask.astype(jnp.float32)
    packed = jnp.concatenate([terminal, conductivity[None], velocity, keep[None]], axis=0)
    width = 2
    sizes = (-(-(rows_x + 2 * width) // 8) * 8, -(-(cols_y + 2 * width) // 128) * 128)
    ends_x = lax.axis_size("gx") - 1
    ends_y = lax.axis_size("gy") - 1
    after = lax.ppermute(packed[:, :, :width], "gx", [(i + 1, i) for i in range(ends_x)])
    before = lax.ppermute(packed[:, :, rows_x - width:], "gx", [(i, i + 1) for i in range(ends_x)])

    def column(cut):
        gap = jnp.zeros(packed.shape[:2] + (sizes[0] - rows_x - 2 * width, width), packed.dtype)
        return jnp.concatenate([packed[..., cut], after[..., cut], gap, before[..., cut]], axis=2)

    side = jnp.concatenate(
        [
            lax.ppermute(column(slice(0, width)), "gy", [(i + 1, i) for i in range(ends_y)]),
            jnp.zeros(packed.shape[:2] + (sizes[0], sizes[1] - cols_y - 2 * width), packed.dtype),
            lax.ppermute(column(slice(cols_y - width, cols_y)), "gy", [(i, i + 1) for i in range(ends_y)]),
        ],
        axis=3,
    )
    heat_sens, mine, other = heat_phase(
        wells, misfit, packed, after, before, side, forward_temp, sizes[0]
    )
    partner = [(0, 1), (1, 0)]
    rounded = (mine + lax.ppermute(other, "sec", partner)).astype(jnp.bfloat16)
    row_blocks, per_row, block_size, _ = blocks.shape
    count = lax.axis_size("gy")
    copies = jnp.broadcast_to(rounded[None], (count,) + rounded.shape)
    gathered = lax.all_to_all(copies, "gy", 0, 0, tiled=False)
    cells = layers * rows_x
    head, partial_sens = apply_head(
        block_cols,
        gathered.reshape(count, cells, cols_y),
        blocks,
        heat_sens.reshape(cells, cols_y),
        head_gradient[0].reshape(cells, cols_y),
    )
    head = head.reshape(layers, rows_x, cols_y)
    partial_sens = partial_sens.reshape(layers, rows_x, cols_y)
    sensitivity = partial_sens + lax.ppermute(partial_sens, "sec", partner)
    return (head[None], sensitivity)


def solution(mesh):
    placed = (
        P("sec", None, "gx", "gy"),
        P(None, "sec", None, "gx", "gy"),
        P(None, "gx", "gy"),
        P(None, None, "gx", "gy"),
        P(None, "gx", "gy"),
        P("sec", None, None),
        P(None, "sec", None),
        P("sec", None, "gx", "gy"),
        P("gy", None, None, None),
        P("gy", None),
    )
    return jax.shard_map(
        shards,
        mesh=mesh,
        in_specs=placed,
        out_specs=(P("sec", None, "gx", "gy"), P(None, "gx", "gy")),
        check_vma=False,
    )
```

```python
import jax
import jax.numpy as jnp
from jax import lax
from jax.sharding import PartitionSpec as P
from jax.experimental import pallas as pl
from jax.experimental.pallas import tpu as pltpu


def extended(cells, sides, width):
    for axis, dim in sides:
        count = lax.axis_size(axis)
        ends = count - 1
        head = lax.slice_in_dim(cells, 0, width, axis=dim)
        tail = lax.slice_in_dim(cells, cells.shape[dim] - width, cells.shape[dim], axis=dim)
        cells = jnp.concatenate(
            [
                lax.ppermute(tail, axis, [(i, (i + 1) % count) for i in range(ends)]),
                cells,
                lax.ppermute(head, axis, [((i + 1) % count, i) for i in range(ends)]),
            ],
            axis=dim,
        )
    return cells


def shifted(padded):
    lead = [(0, 0)] * (padded.ndim - 3)
    deeper = jnp.pad(padded, lead + [(1, 1), (0, 0), (0, 0)])
    centre = deeper[..., 1:-1, 1:-1, 1:-1]
    beside_all = [
        deeper[..., 2:, 1:-1, 1:-1],
        deeper[..., :-2, 1:-1, 1:-1],
        deeper[..., 1:-1, 2:, 1:-1],
        deeper[..., 1:-1, :-2, 1:-1],
        deeper[..., 1:-1, 1:-1, 2:],
        deeper[..., 1:-1, 1:-1, :-2],
    ]
    return (centre, beside_all)


def face_weights(kappa_pad):
    centre, beside_all = shifted(kappa_pad)
    return [
        2.0 * centre * other / jnp.where(centre + other > 0.0, centre + other, 1.0)
        for other in beside_all
    ]


def advance(adjoint_pad, weights, keep, speed_x, speed_y, source):
    centre, beside_all = shifted(adjoint_pad)
    diffusion = weights[0] * (beside_all[0] - centre)
    for face in range(1, 6):
        diffusion = diffusion + weights[face] * (beside_all[face] - centre)
    slope_x = 0.5 * (beside_all[2] - beside_all[3])
    slope_y = 0.5 * (beside_all[4] - beside_all[5])
    updated = keep * (centre + diffusion + speed_x * slope_x + speed_y * slope_y + source)
    return (updated, diffusion, slope_x, slope_y)


def well_sources(wells, misfit_level, layers, rows_x, cols_y, margin):
    start_x = lax.axis_index("gx") * rows_x - margin
    start_y = lax.axis_index("gy") * cols_y - margin
    coord_z = jnp.arange(layers, dtype=jnp.int32)[:, None, None]
    coord_x = (start_x + jnp.arange(rows_x + 2 * margin, dtype=jnp.int32))[None, :, None]
    coord_y = (start_y + jnp.arange(cols_y + 2 * margin, dtype=jnp.int32))[None, None, :]
    well_z = wells[:, :, 0][:, :, None, None, None]
    well_x = wells[:, :, 1][:, :, None, None, None]
    well_y = wells[:, :, 2][:, :, None, None, None]
    matches = (coord_z == well_z) & (coord_x == well_x) & (coord_y == well_y)
    return jnp.sum(jnp.where(matches, misfit_level[:, :, None, None, None], 0.0), axis=1)


def conductance(centre, other):
    return 2.0 * centre * other / jnp.where(centre + other > 0.0, centre + other, 1.0)


def heat_kernel(
    wells_ref, misfit_ref, tile_ref, after_ref, before_ref, side_ref, temp_ref,
    heat_ref, fx_ref, fy_ref, adj_ref, w_ref, box_ref,
):
    channels, layers, tile_x, tile_y = tile_ref.shape
    width = after_ref.shape[2]
    rows = box_ref.shape[2]
    box_ref[:, :, 0:tile_x, 0:tile_y] = tile_ref[...]
    box_ref[:, :, tile_x:tile_x + width, 0:tile_y] = after_ref[...]
    box_ref[:, :, tile_x + width:rows - width, 0:tile_y] = jnp.zeros(
        (channels, layers, rows - tile_x - 2 * width, tile_y), jnp.float32
    )
    box_ref[:, :, rows - width:rows, 0:tile_y] = before_ref[...]
    box_ref[:, :, :, tile_y:] = side_ref[...]
    tests, layers, rows, cols = adj_ref.shape
    tile_x, tile_y = heat_ref.shape[1], heat_ref.shape[2]
    zero = jnp.zeros((rows, cols), jnp.float32)

    def plane(ref, lead, z):
        above = jnp.where(z + 1 < layers, ref[lead, jnp.minimum(z + 1, layers - 1)], zero)
        below = jnp.where(z > 0, ref[lead, jnp.maximum(z - 1, 0)], zero)
        return ref[lead, z], above, below

    def faces(value, above, below):
        return [
            above,
            below,
            pltpu.roll(value, rows - 1, 0),
            pltpu.roll(value, 1, 0),
            pltpu.roll(value, cols - 1, 1),
            pltpu.roll(value, 1, 1),
        ]

    def weigh(z, carry):
        centre, above, below = plane(box_ref, 2, z)
        for face, other in enumerate(faces(centre, above, below)):
            w_ref[face, z] = conductance(centre, other)
        return carry

    lax.fori_loop(0, layers, weigh, 0)

    def advance(source_ref, level, store):
        def body(z, carry):
            speed_x = box_ref[3, z]
            speed_y = box_ref[4, z]
            keep = box_ref[5, z]
            heat = fx = fy = None
            for test in range(tests):
                centre, above, below = plane(source_ref, test, z)
                beside = faces(centre, above, below)
                diffusion = w_ref[0, z] * (beside[0] - centre)
                for face in range(1, 6):
                    diffusion = diffusion + w_ref[face, z] * (beside[face] - centre)
                slope_x = 0.5 * (beside[2] - beside[3])
                slope_y = 0.5 * (beside[4] - beside[5])
                updated = keep * (centre + diffusion + speed_x * slope_x + speed_y * slope_y)
                if store:
                    adj_ref[test, z] = updated
                temper = temp_ref[level, test, z].astype(jnp.float32)
                first = lax.axis_index("sec") == 0
                mine = jnp.where(first, slope_x, slope_y)
                other = jnp.where(first, slope_y, slope_x)
                terms = [temper * v[:tile_x, :tile_y] for v in (diffusion, mine, other)]
                if heat is None:
                    heat, fx, fy = terms
                else:
                    heat, fx, fy = heat + terms[0], fx + terms[1], fy + terms[2]
            if store:
                heat_ref[z], fx_ref[z], fy_ref[z] = heat, fx, fy
            else:
                heat_ref[z] = heat_ref[z] + heat
                fx_ref[z] = fx_ref[z] + fx
                fy_ref[z] = fy_ref[z] + fy
            return carry

        lax.fori_loop(0, layers, body, 0)

    advance(box_ref, 1, True)
    row_ids = lax.broadcasted_iota(jnp.int32, (rows, cols), 0)
    col_ids = lax.broadcasted_iota(jnp.int32, (rows, cols), 1)
    for test in range(tests):
        for well in range(wells_ref.shape[1]):
            depth = wells_ref[test, well, 0]
            at_x = wells_ref[test, well, 1] - lax.axis_index("gx") * tile_x
            at_y = wells_ref[test, well, 2] - lax.axis_index("gy") * tile_y
            inside = (at_x >= -2) & (at_x < tile_x + 2) & (at_y >= -2) & (at_y < tile_y + 2)
            amount = jnp.where(inside, misfit_ref[1, test, well], 0.0)
            hit = (row_ids == jnp.where(at_x < 0, at_x + rows, at_x)) & (
                col_ids == jnp.where(at_y < 0, at_y + cols, at_y)
            )
            adj_ref[test, depth] = adj_ref[test, depth] + jnp.where(hit, box_ref[5, depth] * amount, 0.0)
    advance(adj_ref, 0, False)


def heat_phase(wells, misfit, tile, after, before, side, temp, rows):
    channels, layers = tile.shape[:2]
    cols = tile.shape[3] + side.shape[3]
    tests = temp.shape[1]
    plane_shape = temp.shape[3:]
    smem = pl.BlockSpec(memory_space=pltpu.SMEM)
    vmem = pl.BlockSpec(memory_space=pltpu.VMEM)
    out = jax.ShapeDtypeStruct((layers,) + plane_shape, jnp.float32)
    return pl.pallas_call(
        heat_kernel,
        out_shape=(out, out, out),
        in_specs=[smem, smem, vmem, vmem, vmem, vmem, vmem],
        out_specs=(vmem, vmem, vmem),
        scratch_shapes=[
            pltpu.VMEM((tests, layers, rows, cols), jnp.float32),
            pltpu.VMEM((6, layers, rows, cols), jnp.float32),
            pltpu.VMEM((channels, layers, rows, cols), jnp.float32),
        ],
    )(wells, misfit, tile, after, before, side, temp)


def circular(cells, sides, width, sizes):
    for (axis, dim), size in zip(sides, sizes):
        ends = lax.axis_size(axis) - 1
        length = cells.shape[dim]
        head = lax.slice_in_dim(cells, 0, width, axis=dim)
        tail = lax.slice_in_dim(cells, length - width, length, axis=dim)
        gap = list(cells.shape)
        gap[dim] = size - length - 2 * width
        cells = jnp.concatenate(
            [
                cells,
                lax.ppermute(head, axis, [(i + 1, i) for i in range(ends)]),
                jnp.zeros(gap, cells.dtype),
                lax.ppermute(tail, axis, [(i, i + 1) for i in range(ends)]),
            ],
            axis=dim,
        )
    return cells


def head_kernel(cols_ref, gathered_ref, blocks_ref, heat_ref, grad_ref, head_ref, part_ref):
    row_blocks, per_row, size, _ = blocks_ref.shape
    halves = gathered_ref.shape[2] // size
    for row in range(row_blocks):
        total = jnp.zeros((gathered_ref.shape[1], size), jnp.float32)
        for k in range(per_row):
            col = cols_ref[row, k]
            start = pl.multiple_of((col % halves) * size, size)
            slab = gathered_ref[col // halves, :, pl.ds(start, size)]
            total = total + lax.dot_general(
                slab, blocks_ref[row, k], (((1,), (1,)), ((), ())), preferred_element_type=jnp.float32
            )
        out = slice(row * size, (row + 1) * size)
        head_ref[:, out] = total
        part_ref[:, out] = heat_ref[:, out] + total * grad_ref[:, out].astype(jnp.float32)


def apply_head(block_cols, gathered, blocks, heat, grad):
    cells, width = heat.shape
    vmem = pltpu.VMEM
    return pl.pallas_call(
        head_kernel,
        out_shape=(
            jax.ShapeDtypeStruct((cells, width), jnp.float32),
            jax.ShapeDtypeStruct((cells, width), jnp.float32),
        ),
        in_specs=[pl.BlockSpec(memory_space=pltpu.SMEM)] + [pl.BlockSpec(memory_space=vmem)] * 4,
        out_specs=(pl.BlockSpec(memory_space=vmem), pl.BlockSpec(memory_space=vmem)),
        cost_estimate=pl.CostEstimate(
            flops=2 * cells * width * blocks.shape[1] * blocks.shape[2],
            bytes_accessed=gathered.size * 2 + blocks.size * 2 + cells * width * 14,
            transcendentals=0,
        ),
    )(block_cols, gathered, blocks, heat, grad)


def shards(
    terminal,
    forward_temp,
    conductivity,
    velocity,
    fixed_mask,
    wells,
    misfit,
    head_gradient,
    blocks,
    block_cols,
):
    layers, rows_x, cols_y = conductivity.shape
    keep = 1.0 - fixed_mask.astype(jnp.float32)
    packed = jnp.concatenate([terminal, conductivity[None], velocity, keep[None]], axis=0)
    width = 2
    sizes = (-(-(rows_x + 2 * width) // 8) * 8, -(-(cols_y + 2 * width) // 128) * 128)
    ends_x = lax.axis_size("gx") - 1
    ends_y = lax.axis_size("gy") - 1
    after = lax.ppermute(packed[:, :, :width], "gx", [(i + 1, i) for i in range(ends_x)])
    before = lax.ppermute(packed[:, :, rows_x - width:], "gx", [(i, i + 1) for i in range(ends_x)])

    picks = jnp.concatenate(
        [jnp.arange(width), jnp.arange(cols_y - width, cols_y)]
    )[None, :] == jnp.arange(cols_y)[:, None]
    picks = picks.astype(jnp.float32)

    def edges(part):
        return jnp.einsum("czxy,ye->czxe", part, picks, precision=lax.Precision.HIGHEST)

    gap = jnp.zeros(packed.shape[:2] + (sizes[0] - rows_x - 2 * width, 2 * width), packed.dtype)
    strips = jnp.concatenate([edges(packed), edges(after), gap, edges(before)], axis=2)

    def column(cut):
        return strips[..., cut]

    side = jnp.concatenate(
        [
            lax.ppermute(column(slice(0, width)), "gy", [(i + 1, i) for i in range(ends_y)]),
            jnp.zeros(packed.shape[:2] + (sizes[0], sizes[1] - cols_y - 2 * width), packed.dtype),
            lax.ppermute(column(slice(width, 2 * width)), "gy", [(i, i + 1) for i in range(ends_y)]),
        ],
        axis=3,
    )
    heat_sens, mine, other = heat_phase(
        wells, misfit, packed, after, before, side, forward_temp, sizes[0]
    )
    partner = [(0, 1), (1, 0)]
    rounded = (mine + lax.ppermute(other, "sec", partner)).astype(jnp.bfloat16)
    row_blocks, per_row, block_size, _ = blocks.shape
    count = lax.axis_size("gy")
    copies = jnp.broadcast_to(rounded[None], (count,) + rounded.shape)
    gathered = lax.all_to_all(copies, "gy", 0, 0, tiled=False)
    cells = layers * rows_x
    head, partial_sens = apply_head(
        block_cols,
        gathered.reshape(count, cells, cols_y),
        blocks,
        heat_sens.reshape(cells, cols_y),
        head_gradient[0].reshape(cells, cols_y),
    )
    head = head.reshape(layers, rows_x, cols_y)
    partial_sens = partial_sens.reshape(layers, rows_x, cols_y)
    sensitivity = partial_sens + lax.ppermute(partial_sens, "sec", partner)
    return (head[None], sensitivity)


def solution(mesh):
    placed = (
        P("sec", None, "gx", "gy"),
        P(None, "sec", None, "gx", "gy"),
        P(None, "gx", "gy"),
        P(None, None, "gx", "gy"),
        P(None, "gx", "gy"),
        P("sec", None, None),
        P(None, "sec", None),
        P("sec", None, "gx", "gy"),
        P("gy", None, None, None),
        P("gy", None),
    )
    return jax.shard_map(
        shards,
        mesh=mesh,
        in_specs=placed,
        out_specs=(P("sec", None, "gx", "gy"), P(None, "gx", "gy")),
        check_vma=False,
    )
```

```python
import jax
import jax.numpy as jnp
from jax import lax
from jax.sharding import PartitionSpec as P
from jax.experimental import pallas as pl
from jax.experimental.pallas import tpu as pltpu


def extended(cells, sides, width):
    for axis, dim in sides:
        count = lax.axis_size(axis)
        ends = count - 1
        head = lax.slice_in_dim(cells, 0, width, axis=dim)
        tail = lax.slice_in_dim(cells, cells.shape[dim] - width, cells.shape[dim], axis=dim)
        cells = jnp.concatenate(
            [
                lax.ppermute(tail, axis, [(i, (i + 1) % count) for i in range(ends)]),
                cells,
                lax.ppermute(head, axis, [((i + 1) % count, i) for i in range(ends)]),
            ],
            axis=dim,
        )
    return cells


def shifted(padded):
    lead = [(0, 0)] * (padded.ndim - 3)
    deeper = jnp.pad(padded, lead + [(1, 1), (0, 0), (0, 0)])
    centre = deeper[..., 1:-1, 1:-1, 1:-1]
    beside_all = [
        deeper[..., 2:, 1:-1, 1:-1],
        deeper[..., :-2, 1:-1, 1:-1],
        deeper[..., 1:-1, 2:, 1:-1],
        deeper[..., 1:-1, :-2, 1:-1],
        deeper[..., 1:-1, 1:-1, 2:],
        deeper[..., 1:-1, 1:-1, :-2],
    ]
    return (centre, beside_all)


def face_weights(kappa_pad):
    centre, beside_all = shifted(kappa_pad)
    return [
        2.0 * centre * other / jnp.where(centre + other > 0.0, centre + other, 1.0)
        for other in beside_all
    ]


def advance(adjoint_pad, weights, keep, speed_x, speed_y, source):
    centre, beside_all = shifted(adjoint_pad)
    diffusion = weights[0] * (beside_all[0] - centre)
    for face in range(1, 6):
        diffusion = diffusion + weights[face] * (beside_all[face] - centre)
    slope_x = 0.5 * (beside_all[2] - beside_all[3])
    slope_y = 0.5 * (beside_all[4] - beside_all[5])
    updated = keep * (centre + diffusion + speed_x * slope_x + speed_y * slope_y + source)
    return (updated, diffusion, slope_x, slope_y)


def well_sources(wells, misfit_level, layers, rows_x, cols_y, margin):
    start_x = lax.axis_index("gx") * rows_x - margin
    start_y = lax.axis_index("gy") * cols_y - margin
    coord_z = jnp.arange(layers, dtype=jnp.int32)[:, None, None]
    coord_x = (start_x + jnp.arange(rows_x + 2 * margin, dtype=jnp.int32))[None, :, None]
    coord_y = (start_y + jnp.arange(cols_y + 2 * margin, dtype=jnp.int32))[None, None, :]
    well_z = wells[:, :, 0][:, :, None, None, None]
    well_x = wells[:, :, 1][:, :, None, None, None]
    well_y = wells[:, :, 2][:, :, None, None, None]
    matches = (coord_z == well_z) & (coord_x == well_x) & (coord_y == well_y)
    return jnp.sum(jnp.where(matches, misfit_level[:, :, None, None, None], 0.0), axis=1)


def conductance(centre, other):
    return 2.0 * centre * other / jnp.where(centre + other > 0.0, centre + other, 1.0)


def heat_kernel(
    wells_ref, misfit_ref, tile_ref, after_ref, before_ref, side_ref, temp_ref,
    heat_ref, fx_ref, fy_ref, adj_ref, w_ref, box_ref,
):
    channels, layers, tile_x, tile_y = tile_ref.shape
    width = after_ref.shape[2]
    rows = box_ref.shape[2]
    box_ref[:, :, 0:tile_x, 0:tile_y] = tile_ref[...]
    box_ref[:, :, tile_x:tile_x + width, 0:tile_y] = after_ref[...]
    box_ref[:, :, tile_x + width:rows - width, 0:tile_y] = jnp.zeros(
        (channels, layers, rows - tile_x - 2 * width, tile_y), jnp.float32
    )
    box_ref[:, :, rows - width:rows, 0:tile_y] = before_ref[...]
    box_ref[:, :, :, tile_y:] = side_ref[...]
    tests, layers, rows, cols = adj_ref.shape
    tile_x, tile_y = heat_ref.shape[1], heat_ref.shape[2]
    zero = jnp.zeros((rows, cols), jnp.float32)

    def plane(ref, lead, z):
        above = jnp.where(z + 1 < layers, ref[lead, jnp.minimum(z + 1, layers - 1)], zero)
        below = jnp.where(z > 0, ref[lead, jnp.maximum(z - 1, 0)], zero)
        return ref[lead, z], above, below

    def faces(value, above, below):
        return [
            above,
            below,
            pltpu.roll(value, rows - 1, 0),
            pltpu.roll(value, 1, 0),
            pltpu.roll(value, cols - 1, 1),
            pltpu.roll(value, 1, 1),
        ]

    def weigh(z, carry):
        centre, above, below = plane(box_ref, 2, z)
        for face, other in enumerate(faces(centre, above, below)):
            w_ref[face, z] = conductance(centre, other)
        return carry

    lax.fori_loop(0, layers, weigh, 0)

    def advance(source_ref, level, store):
        def body(z, carry):
            speed_x = box_ref[3, z]
            speed_y = box_ref[4, z]
            keep = box_ref[5, z]
            heat = fx = fy = None
            for test in range(tests):
                centre, above, below = plane(source_ref, test, z)
                beside = faces(centre, above, below)
                diffusion = w_ref[0, z] * (beside[0] - centre)
                for face in range(1, 6):
                    diffusion = diffusion + w_ref[face, z] * (beside[face] - centre)
                slope_x = 0.5 * (beside[2] - beside[3])
                slope_y = 0.5 * (beside[4] - beside[5])
                updated = keep * (centre + diffusion + speed_x * slope_x + speed_y * slope_y)
                if store:
                    adj_ref[test, z] = updated
                temper = temp_ref[level, test, z].astype(jnp.float32)
                first = lax.axis_index("sec") == 0
                mine = jnp.where(first, slope_x, slope_y)
                other = jnp.where(first, slope_y, slope_x)
                terms = [temper * v[:tile_x, :tile_y] for v in (diffusion, mine, other)]
                if heat is None:
                    heat, fx, fy = terms
                else:
                    heat, fx, fy = heat + terms[0], fx + terms[1], fy + terms[2]
            if store:
                heat_ref[z], fx_ref[z], fy_ref[z] = heat, fx, fy
            else:
                heat_ref[z] = heat_ref[z] + heat
                fx_ref[z] = fx_ref[z] + fx
                fy_ref[z] = fy_ref[z] + fy
            return carry

        lax.fori_loop(0, layers, body, 0)

    advance(box_ref, 1, True)
    row_ids = lax.broadcasted_iota(jnp.int32, (rows, cols), 0)
    col_ids = lax.broadcasted_iota(jnp.int32, (rows, cols), 1)
    for test in range(tests):
        for well in range(wells_ref.shape[1]):
            depth = wells_ref[test, well, 0]
            at_x = wells_ref[test, well, 1] - lax.axis_index("gx") * tile_x
            at_y = wells_ref[test, well, 2] - lax.axis_index("gy") * tile_y
            inside = (at_x >= -2) & (at_x < tile_x + 2) & (at_y >= -2) & (at_y < tile_y + 2)
            amount = jnp.where(inside, misfit_ref[1, test, well], 0.0)
            hit = (row_ids == jnp.where(at_x < 0, at_x + rows, at_x)) & (
                col_ids == jnp.where(at_y < 0, at_y + cols, at_y)
            )
            adj_ref[test, depth] = adj_ref[test, depth] + jnp.where(hit, box_ref[5, depth] * amount, 0.0)
    advance(adj_ref, 0, False)


def heat_phase(wells, misfit, tile, after, before, side, temp, rows):
    channels, layers = tile.shape[:2]
    cols = tile.shape[3] + side.shape[3]
    tests = temp.shape[1]
    plane_shape = temp.shape[3:]
    smem = pl.BlockSpec(memory_space=pltpu.SMEM)
    vmem = pl.BlockSpec(memory_space=pltpu.VMEM)
    out = jax.ShapeDtypeStruct((layers,) + plane_shape, jnp.float32)
    return pl.pallas_call(
        heat_kernel,
        out_shape=(out, out, out),
        in_specs=[smem, smem, vmem, vmem, vmem, vmem, vmem],
        out_specs=(vmem, vmem, vmem),
        scratch_shapes=[
            pltpu.VMEM((tests, layers, rows, cols), jnp.float32),
            pltpu.VMEM((6, layers, rows, cols), jnp.float32),
            pltpu.VMEM((channels, layers, rows, cols), jnp.float32),
        ],
    )(wells, misfit, tile, after, before, side, temp)


def circular(cells, sides, width, sizes):
    for (axis, dim), size in zip(sides, sizes):
        ends = lax.axis_size(axis) - 1
        length = cells.shape[dim]
        head = lax.slice_in_dim(cells, 0, width, axis=dim)
        tail = lax.slice_in_dim(cells, length - width, length, axis=dim)
        gap = list(cells.shape)
        gap[dim] = size - length - 2 * width
        cells = jnp.concatenate(
            [
                cells,
                lax.ppermute(head, axis, [(i + 1, i) for i in range(ends)]),
                jnp.zeros(gap, cells.dtype),
                lax.ppermute(tail, axis, [(i, i + 1) for i in range(ends)]),
            ],
            axis=dim,
        )
    return cells


def head_kernel(cols_ref, gathered_ref, blocks_ref, heat_ref, grad_ref, head_ref, part_ref):
    row_blocks, per_row, size, _ = blocks_ref.shape
    halves = gathered_ref.shape[2] // size
    for row in range(row_blocks):
        total = jnp.zeros((gathered_ref.shape[1], size), jnp.float32)
        for k in range(per_row):
            col = cols_ref[row, k]
            start = pl.multiple_of((col % halves) * size, size)
            slab = gathered_ref[col // halves, :, pl.ds(start, size)]
            total = total + lax.dot_general(
                slab, blocks_ref[row, k], (((1,), (1,)), ((), ())), preferred_element_type=jnp.float32
            )
        out = slice(row * size, (row + 1) * size)
        head_ref[:, out] = total
        part_ref[:, out] = heat_ref[:, out] + total * grad_ref[:, out].astype(jnp.float32)


def apply_head(block_cols, gathered, blocks, heat, grad):
    cells, width = heat.shape
    vmem = pltpu.VMEM
    return pl.pallas_call(
        head_kernel,
        out_shape=(
            jax.ShapeDtypeStruct((cells, width), jnp.float32),
            jax.ShapeDtypeStruct((cells, width), jnp.float32),
        ),
        in_specs=[pl.BlockSpec(memory_space=pltpu.SMEM)] + [pl.BlockSpec(memory_space=vmem)] * 4,
        out_specs=(pl.BlockSpec(memory_space=vmem), pl.BlockSpec(memory_space=vmem)),
        cost_estimate=pl.CostEstimate(
            flops=2 * cells * width * blocks.shape[1] * blocks.shape[2],
            bytes_accessed=gathered.size * 2 + blocks.size * 2 + cells * width * 14,
            transcendentals=0,
        ),
    )(block_cols, gathered, blocks, heat, grad)


def shards(
    terminal,
    forward_temp,
    conductivity,
    velocity,
    fixed_mask,
    wells,
    misfit,
    head_gradient,
    blocks,
    block_cols,
):
    layers, rows_x, cols_y = conductivity.shape
    keep = 1.0 - fixed_mask.astype(jnp.float32)
    packed = jnp.concatenate([terminal, conductivity[None], velocity, keep[None]], axis=0)
    width = 2
    sizes = (-(-(rows_x + 2 * width) // 8) * 8, -(-(cols_y + 2 * width) // 128) * 128)
    ends_x = lax.axis_size("gx") - 1
    ends_y = lax.axis_size("gy") - 1
    rows_pick = (
        jnp.concatenate([jnp.arange(width), jnp.arange(rows_x - width, rows_x)])[None, :]
        == jnp.arange(rows_x)[:, None]
    ).astype(jnp.float32)
    rims = jnp.einsum("czxy,xe->czey", packed, rows_pick, precision=lax.Precision.HIGHEST)
    after = lax.ppermute(rims[:, :, :width], "gx", [(i + 1, i) for i in range(ends_x)])
    before = lax.ppermute(rims[:, :, width:], "gx", [(i, i + 1) for i in range(ends_x)])

    picks = jnp.concatenate(
        [jnp.arange(width), jnp.arange(cols_y - width, cols_y)]
    )[None, :] == jnp.arange(cols_y)[:, None]
    picks = picks.astype(jnp.float32)

    def edges(part):
        return jnp.einsum("czxy,ye->czxe", part, picks, precision=lax.Precision.HIGHEST)

    gap = jnp.zeros(packed.shape[:2] + (sizes[0] - rows_x - 2 * width, 2 * width), packed.dtype)
    strips = jnp.concatenate([edges(packed), edges(after), gap, edges(before)], axis=2)

    def column(cut):
        return strips[..., cut]

    side = jnp.concatenate(
        [
            lax.ppermute(column(slice(0, width)), "gy", [(i + 1, i) for i in range(ends_y)]),
            jnp.zeros(packed.shape[:2] + (sizes[0], sizes[1] - cols_y - 2 * width), packed.dtype),
            lax.ppermute(column(slice(width, 2 * width)), "gy", [(i, i + 1) for i in range(ends_y)]),
        ],
        axis=3,
    )
    heat_sens, mine, other = heat_phase(
        wells, misfit, packed, after, before, side, forward_temp, sizes[0]
    )
    partner = [(0, 1), (1, 0)]
    rounded = (mine + lax.ppermute(other, "sec", partner)).astype(jnp.bfloat16)
    row_blocks, per_row, block_size, _ = blocks.shape
    count = lax.axis_size("gy")
    copies = jnp.broadcast_to(rounded[None], (count,) + rounded.shape)
    gathered = lax.all_to_all(copies, "gy", 0, 0, tiled=False)
    cells = layers * rows_x
    head, partial_sens = apply_head(
        block_cols,
        gathered.reshape(count, cells, cols_y),
        blocks,
        heat_sens.reshape(cells, cols_y),
        head_gradient[0].reshape(cells, cols_y),
    )
    head = head.reshape(layers, rows_x, cols_y)
    partial_sens = partial_sens.reshape(layers, rows_x, cols_y)
    sensitivity = partial_sens + lax.ppermute(partial_sens, "sec", partner)
    return (head[None], sensitivity)


def solution(mesh):
    placed = (
        P("sec", None, "gx", "gy"),
        P(None, "sec", None, "gx", "gy"),
        P(None, "gx", "gy"),
        P(None, None, "gx", "gy"),
        P(None, "gx", "gy"),
        P("sec", None, None),
        P(None, "sec", None),
        P("sec", None, "gx", "gy"),
        P("gy", None, None, None),
        P("gy", None),
    )
    return jax.shard_map(
        shards,
        mesh=mesh,
        in_specs=placed,
        out_specs=(P("sec", None, "gx", "gy"), P(None, "gx", "gy")),
        check_vma=False,
    )
```
